256 devices in a mesh: tm: 32 (over x_hi, z, core), tile: 8 (over y, x_lo).
Axes of the slice: x: 4 (x_hi: 2, x_lo: 2; x = x_hi * 2 + x_lo), y: 4, z: 8, core: 2. Of those that a mesh axis runs over, the one named last changes fastest.
Arguments:
- latent: bfloat16 [32, 16, 160, 384], P('tm', 'tile'), may hold values from -6 to 6
- gain: float32 [384], replicated, may hold values from 0.1 to 1.9
- conv_weight: bfloat16 [3, 3, 3, 384, 384], replicated, may hold values from -0.0625 to 0.0625
- conv_bias: float32 [384], replicated, may hold values from -3 to 3
- time_weight: bfloat16 [3, 384, 768], replicated, may hold values from -0.1875 to 0.1875
- time_bias: float32 [768], replicated, may hold values from -3 to 3
- up_weight: bfloat16 [3, 3, 384, 192], replicated, may hold values from -0.109375 to 0.109375
- up_bias: float32 [192], replicated, may hold values from -3 to 3
Outputs:
- decoded: bfloat16 [64, 32, 320, 192], P('tm', 'tile')
The draws below stay inside these ranges and needn't reach their ends.
All inputs are finite; a program needn't handle non-finite values.
Results may differ from the reference program's by a relative error of at most 0.0057.
Values may be sent and summed in bfloat16 or wider, within the bound.
A program may use at most 64 MiB of HBM per device.

```python
import jax
import jax.numpy as jnp
from jax import lax

C = 384
CO = 192
COLS = 160
FRAMES = 32
ROWS = 16


def block_scale(key, extent, shards, least, top_value):
    level = 1.0
    for position, parts in shards:
        draws = jax.random.uniform(jax.random.fold_in(jax.random.fold_in(key, 6), position), (parts,), jnp.float32, least / len(shards), top_value / len(shards))
        level = level * jnp.repeat(jnp.exp(draws), extent[position] // parts).reshape((-1,) + (1,) * (len(extent) - 1 - position))
    return level


def gaussian(own_key, shape, scale, bound, pieces=(), held_as=jnp.bfloat16):
    drawn = jax.random.normal(own_key, shape, jnp.float32) * scale
    if len(pieces) > 0:
        drawn = block_scale(own_key, shape, pieces, -0.22, 0.18) * drawn
    return jnp.clip(drawn, min=-bound, max=bound).astype(held_as)


def setup_inputs(seed: int = 0) -> dict:
    arg_keys = jax.random.split(jax.random.key(seed), 9)
    latent = gaussian(arg_keys[0], (FRAMES, ROWS, COLS, C), 1.0, 6.0, ((0, 32), (1, 8)))
    gain = jnp.clip(1.0 + 0.18 * jax.random.normal(arg_keys[1], (C,), jnp.float32), 0.1, 1.9)
    conv_weight = gaussian(arg_keys[2], (3, 3, 3, C, C), (27 * C) ** -0.5, 0.0625)
    conv_bias = gaussian(arg_keys[3], (C,), 0.5, 3.0, (), jnp.float32)
    time_weight = gaussian(arg_keys[4], (3, C, 2 * C), (3 * C) ** -0.5, 0.1875)
    time_bias = gaussian(arg_keys[5], (2 * C,), 0.5, 3.0, (), jnp.float32)
    up_weight = gaussian(arg_keys[6], (3, 3, C, CO), (9 * C) ** -0.5, 0.109375)
    up_bias = gaussian(arg_keys[7], (CO,), 0.5, 3.0, (), jnp.float32)
    return dict(latent=latent, gain=gain, conv_weight=conv_weight, conv_bias=conv_bias, time_weight=time_weight, time_bias=time_bias, up_weight=up_weight, up_bias=up_bias)


def activate(field, gain):
    values = field.astype(jnp.float32)
    meansq = lax.optimization_barrier(jnp.mean(values * values, axis=-1, keepdims=True))
    scaled = values * lax.rsqrt(meansq + 1e-06) * gain
    return (scaled * jax.nn.sigmoid(scaled)).astype(jnp.bfloat16)

def reference(latent, gain, conv_weight, conv_bias, time_weight, time_bias, up_weight, up_bias):
    activated = activate(latent, gain)
    summed = lax.conv_general_dilated(activated.astype(jnp.float32)[None], conv_weight.astype(jnp.float32), (1, 1, 1), ((2, 0), (1, 1), (1, 1)), dimension_numbers=('NDHWC', 'DHWIO', 'NDHWC'), precision=lax.Precision.HIGHEST)[0]
    block = (summed + conv_bias + latent.astype(jnp.float32)).astype(jnp.bfloat16)
    mixed = lax.conv_general_dilated(block.astype(jnp.float32)[None], time_weight.astype(jnp.float32)[:, None, None], (1, 1, 1), ((2, 0), (0, 0), (0, 0)), dimension_numbers=('NDHWC', 'DHWIO', 'NDHWC'), precision=lax.Precision.HIGHEST)[0]
    doubled = (mixed + time_bias).astype(jnp.bfloat16)
    frames_n, rows_n, cols_n, chans = block.shape
    frames = doubled.reshape(frames_n, rows_n, cols_n, 2, chans).transpose(0, 3, 1, 2, 4).reshape(2 * frames_n, rows_n, cols_n, chans)
    kernel = up_weight.astype(jnp.float32)

    def one_frame(frame):
        upsampled = jnp.repeat(jnp.repeat(frame, 2, axis=0), 2, axis=1).astype(jnp.float32)
        result = lax.conv_general_dilated(upsampled[None], kernel, (1, 1), ((1, 1), (1, 1)), dimension_numbers=('NHWC', 'HWIO', 'NHWC'), precision=lax.Precision.HIGHEST)[0]
        return (result + up_bias).astype(jnp.bfloat16)
    return lax.map(one_frame, frames)
```

```python
import functools

import jax
import jax.numpy as jnp
from jax import lax
from jax.experimental import pallas as pl
from jax.experimental.pallas import tpu as pltpu
from jax.sharding import PartitionSpec as P

F32 = jnp.float32
BF16 = jnp.bfloat16
MESH = pl.DeviceIdType.MESH


def column_shift(flat, cols, step):
    total = flat.shape[0]
    rolled = pltpu.roll(flat, step % total, 0)
    place = lax.broadcasted_iota(jnp.int32, flat.shape, 0) % cols
    edge = 0 if step > 0 else cols - 1
    return jnp.where(place == edge, 0.0, rolled)


def kernel(
    frames, tiles,
    lat_hbm, gain_ref, cb_ref, tb_ref, ub_ref, cw_hbm, tw_hbm, uw_hbm,
    out_ref,
    lat, act, act_hist, parts, part_in, blk, blk_hist, dbl,
    cw, tw, uw, umat, acc, wide_lo, wide_hi,
    lat_sem, cw_sem, tw_sem, uw_sem,
    a_send, a_recv, a_fsend, b_send, b_recv, b_fsend,
    p_send, p_recv, d_send, d_recv,
):
    rows, cols, chans = lat.shape
    outs_n = uw.shape[2]
    low = 128
    high = outs_n - low
    cells = rows * cols
    t = lax.axis_index("tm")
    s = lax.axis_index("tile")
    odd = lax.rem(t, 2) == 1
    has_next = t + 2 < frames
    has_prev = t >= 2
    has_up = s > 0
    has_down = s < tiles - 1

    lat_copy = pltpu.make_async_copy(lat_hbm.at[0], lat, lat_sem)
    lat_copy.start()
    cw_copies = {}
    for dt in (2, 0, 1):
        for dh in range(3):
            copy = pltpu.make_async_copy(
                cw_hbm.at[dt, dh],
                cw.at[dt, :, :, pl.ds(dh * chans, chans)],
                cw_sem.at[dt, dh],
            )
            copy.start()
            cw_copies[dt, dh] = copy
    tw_copy = pltpu.make_async_copy(tw_hbm, tw, tw_sem)
    tw_copy.start()
    uw_copy = pltpu.make_async_copy(uw_hbm, uw, uw_sem)
    uw_copy.start()

    sibling = t + 1 - 2 * lax.rem(t, 2)
    barrier = pltpu.get_barrier_semaphore()

    def greet(condition, where):
        @pl.when(condition)
        def _():
            pl.semaphore_signal(barrier, inc=1, device_id=where, device_id_type=MESH)

    pl.semaphore_signal(barrier, inc=1, device_id={"tm": sibling}, device_id_type=MESH)
    greet(has_next, {"tm": t + 2})
    greet(has_prev, {"tm": t - 2})
    greet(has_up, {"tile": s - 1})
    greet(has_down, {"tile": s + 1})

    lat_copy.wait()
    for r in range(rows):
        values = lat[r].astype(F32)
        meansq = jnp.mean(values * values, axis=-1, keepdims=True)
        scaled = values * lax.rsqrt(meansq + 1e-06) * gain_ref[...]
        act[r] = (scaled * jax.nn.sigmoid(scaled)).astype(BF16)

    peers = 1
    for condition in (has_next, has_prev, has_up, has_down):
        peers = peers + condition.astype(jnp.int32)
    pl.semaphore_wait(barrier, peers)

    def history_copies(own, hist, send, recv, fsend):
        def nearer(r):
            return pltpu.make_async_remote_copy(
                own.at[r], hist.at[1, r], send.at[0, r], recv.at[1, r],
                device_id={"tm": sibling}, device_id_type=MESH,
            )

        def farther(r):
            return pltpu.make_async_remote_copy(
                own.at[r], hist.at[0, r], send.at[1, r], recv.at[0, r],
                device_id={"tm": t + 2}, device_id_type=MESH,
            )

        def forward(r):
            return pltpu.make_async_remote_copy(
                hist.at[0, r], hist.at[1, r], fsend.at[r], recv.at[1, r],
                device_id={"tm": sibling}, device_id_type=MESH,
            )

        return nearer, farther, forward

    def history_start(copies):
        nearer, farther, _ = copies
        for r in range(rows):
            @pl.when(has_next)
            def _():
                farther(r).start()

            @pl.when(jnp.logical_not(odd))
            def _():
                nearer(r).start()

    def history_far(copies, hist):
        _, farther, forward = copies

        @pl.when(has_prev)
        def _():
            for r in range(rows):
                farther(r).wait_recv()

                @pl.when(odd)
                def _():
                    forward(r).start()

        @pl.when(jnp.logical_not(has_prev))
        def _():
            hist[0] = jnp.zeros(hist.shape[1:], BF16)

    def history_near(copies, hist):
        nearer, _, _ = copies

        @pl.when(t >= 1)
        def _():
            for r in range(rows):
                nearer(r).wait_recv()

        @pl.when(t == 0)
        def _():
            hist[1] = jnp.zeros(hist.shape[1:], BF16)

    def history_end(copies):
        nearer, farther, forward = copies
        for r in range(rows):
            @pl.when(has_next)
            def _():
                farther(r).wait_send()

            @pl.when(jnp.logical_not(odd))
            def _():
                nearer(r).wait_send()

            @pl.when(jnp.logical_and(odd, has_prev))
            def _():
                forward(r).wait_send()

    def exchange(up_src, up_dst, down_src, down_dst, send, recv):
        up = pltpu.make_async_remote_copy(
            up_src, up_dst, send.at[0], recv.at[0], device_id={"tile": s - 1}, device_id_type=MESH
        )
        down = pltpu.make_async_remote_copy(
            down_src, down_dst, send.at[1], recv.at[1], device_id={"tile": s + 1}, device_id_type=MESH
        )

        @pl.when(has_up)
        def _():
            up.start()

        @pl.when(has_down)
        def _():
            down.start()

        return up, down

    act_copies = history_copies(act, act_hist, a_send, a_recv, a_fsend)
    history_start(act_copies)

    def conv_step(frame, dt):
        flat = frame.reshape(cells, chans)
        wide = flat.astype(F32)
        before = column_shift(wide, cols, 1).astype(BF16)
        after = column_shift(wide, cols, -1).astype(BF16)
        stacked = jnp.concatenate([before, flat, after], axis=1)
        for dh in range(3):
            cw_copies[dt, dh].wait()
        return jnp.dot(
            stacked, cw[dt].reshape(3 * chans, 3 * chans), preferred_element_type=F32
        )

    acc[...] = conv_step(act[...], 2)
    history_far(act_copies, act_hist)
    acc[...] += conv_step(act_hist[0], 0)
    history_near(act_copies, act_hist)
    acc[...] += conv_step(act_hist[1], 1)

    parts[0] = acc[pl.ds(0, cols), pl.ds(2 * chans, chans)].astype(BF16)
    parts[1] = acc[pl.ds(cells - cols, cols), pl.ds(0, chans)].astype(BF16)
    p_up, p_down = exchange(
        parts.at[0], part_in.at[1], parts.at[1], part_in.at[0], p_send, p_recv
    )

    def own_rows(r):
        total = acc[pl.ds(r * cols, cols), pl.ds(chans, chans)]
        if r > 0:
            total = total + acc[pl.ds((r - 1) * cols, cols), pl.ds(0, chans)]
        if r < rows - 1:
            total = total + acc[pl.ds((r + 1) * cols, cols), pl.ds(2 * chans, chans)]
        return total + cb_ref[...] + lat[r].astype(F32)

    @pl.when(has_up)
    def _():
        p_down.wait_recv()

    @pl.when(jnp.logical_not(has_up))
    def _():
        part_in[0] = jnp.zeros((cols, chans), BF16)

    @pl.when(has_down)
    def _():
        p_up.wait_recv()

    @pl.when(jnp.logical_not(has_down))
    def _():
        part_in[1] = jnp.zeros((cols, chans), BF16)

    for r in range(rows):
        total = own_rows(r)
        if r == 0:
            total = total + part_in[0].astype(F32)
        if r == rows - 1:
            total = total + part_in[1].astype(F32)
        blk[r] = total.astype(BF16)

    blk_copies = history_copies(blk, blk_hist, b_send, b_recv, b_fsend)
    history_start(blk_copies)

    uw_copy.wait()
    row_sets = {(0, 0): (0,), (0, 1): (1, 2), (1, 0): (0, 1), (1, 1): (2,)}
    for (a, i), picks in row_sets.items():
        taps = []
        for kw in range(3):
            tap = uw[picks[0], kw].astype(F32)
            for kh in picks[1:]:
                tap = tap + uw[kh, kw].astype(F32)
            taps.append(tap)
        center = (taps[1] + taps[2], taps[0] + taps[1])
        sides = (taps[0], taps[2])
        lanes = pl.ds(i * chans, chans)
        for base, pair in ((0, center), (2 * outs_n, sides)):
            for b in range(2):
                value = pair[b].astype(BF16)
                umat[a, pl.ds(base + b * low, low), lanes] = value[:low]
                umat[a, pl.ds(base + 2 * low + b * high, high), lanes] = value[low:]

    tw_copy.wait()

    def mix(frame, k):
        return jnp.dot(frame.reshape(cells, chans), tw[k], preferred_element_type=F32)

    mixed = mix(blk[...], 2) + tb_ref[...]
    history_far(blk_copies, blk_hist)
    mixed = mixed + mix(blk_hist[0], 0)
    history_near(blk_copies, blk_hist)
    mixed = (mixed + mix(blk_hist[1], 1)).astype(BF16)
    for r in range(rows):
        for f in range(2):
            dbl[1 + r, f] = mixed[r * cols : (r + 1) * cols, f * chans : (f + 1) * chans]

    d_up, d_down = exchange(
        dbl.at[1], dbl.at[rows + 1], dbl.at[rows], dbl.at[0], d_send, d_recv
    )

    def upsample_row(a, r):
        near = dbl[r + a].reshape(2 * cols, chans)
        far = dbl[r + a + 1].reshape(2 * cols, chans)
        both = jnp.concatenate([near, far], axis=1)
        result = lax.dot_general(
            both, umat[a], (((1,), (1,)), ((), ())), preferred_element_type=F32
        )
        center = result[:, : 2 * outs_n] + ub_ref[...]
        sides = result[:, 2 * outs_n :]
        even = center[:, :low] + column_shift(sides[:, :low], cols, 1)
        uneven = center[:, low : 2 * low] + column_shift(sides[:, low : 2 * low], cols, -1)
        tail = sides[:, 2 * low :]
        lane = lax.broadcasted_iota(jnp.int32, tail.shape, 1)
        tail = center[:, 2 * low :] + jnp.where(
            lane < high, column_shift(tail, cols, 1), column_shift(tail, cols, -1)
        )
        swapped = pltpu.roll(tail, high, 1)
        for f in range(2):
            span = slice(f * cols, (f + 1) * cols)
            wide_lo[pl.ds(0, cols, stride=2), :] = even[span]
            wide_lo[pl.ds(1, cols, stride=2), :] = uneven[span]
            wide_hi[pl.ds(0, cols, stride=2), :] = tail[span]
            wide_hi[pl.ds(1, cols, stride=2), :] = swapped[span]
            out_ref[f, 2 * r + a, :, pl.ds(0, low)] = wide_lo[...].astype(BF16)
            out_ref[f, 2 * r + a, :, pl.ds(low, high)] = wide_hi[:, :high].astype(BF16)

    for r in range(rows):
        for a in range(2):
            if 0 < r + a < rows:
                upsample_row(a, r)

    @pl.when(has_up)
    def _():
        d_down.wait_recv()

    @pl.when(jnp.logical_not(has_up))
    def _():
        dbl[0] = jnp.zeros(dbl.shape[1:], BF16)

    upsample_row(0, 0)

    @pl.when(has_down)
    def _():
        d_up.wait_recv()

    @pl.when(jnp.logical_not(has_down))
    def _():
        dbl[rows + 1] = jnp.zeros(dbl.shape[1:], BF16)

    upsample_row(1, rows - 1)

    history_end(act_copies)
    history_end(blk_copies)

    @pl.when(has_up)
    def _():
        p_up.wait_send()
        d_up.wait_send()

    @pl.when(has_down)
    def _():
        p_down.wait_send()
        d_down.wait_send()


def local(frames, tiles, latent, gain, conv_weight, conv_bias, time_weight, time_bias, up_weight, up_bias):
    _, rows, cols, chans = latent.shape
    outs_n = up_weight.shape[3]
    low, high = 128, outs_n - 128
    up_bias = jnp.concatenate([up_bias[:low], up_bias[:low], up_bias[low:], up_bias[low:]])
    vmem = pl.BlockSpec(memory_space=pltpu.VMEM)
    anywhere = pl.BlockSpec(memory_space=pl.ANY)
    dma = pltpu.SemaphoreType.DMA
    row = (cols, chans)
    return pl.pallas_call(
        functools.partial(kernel, frames, tiles),
        out_shape=jax.ShapeDtypeStruct((2, 2 * rows, 2 * cols, outs_n), BF16),
        in_specs=[anywhere, vmem, vmem, vmem, vmem, anywhere, anywhere, anywhere],
        out_specs=vmem,
        scratch_shapes=[
            pltpu.VMEM((rows,) + row, BF16),
            pltpu.VMEM((rows,) + row, BF16),
            pltpu.VMEM((2, rows) + row, BF16),
            pltpu.VMEM((2,) + row, BF16),
            pltpu.VMEM((2,) + row, BF16),
            pltpu.VMEM((rows,) + row, BF16),
            pltpu.VMEM((2, rows) + row, BF16),
            pltpu.VMEM((rows + 2, 2) + row, BF16),
            pltpu.VMEM((3, 3, chans, 3 * chans), BF16),
            pltpu.VMEM((3, chans, 2 * chans), BF16),
            pltpu.VMEM((3, 3, outs_n, chans), BF16),
            pltpu.VMEM((2, 4 * outs_n, 2 * chans), BF16),
            pltpu.VMEM((rows * cols, 3 * chans), F32),
            pltpu.VMEM((2 * cols, low), F32),
            pltpu.VMEM((2 * cols, low), F32),
            dma(()), dma((3, 3)), dma(()), dma(()),
            dma((2, rows)), dma((2, rows)), dma((rows,)),
            dma((2, rows)), dma((2, rows)), dma((rows,)),
            dma((2,)), dma((2,)), dma((2,)), dma((2,)),
        ],
        compiler_params=pltpu.CompilerParams(
            collective_id=0, has_side_effects=True, vmem_limit_bytes=60 * 1024 * 1024
        ),
    )(
        latent, gain[None], conv_bias[None], time_bias[None], up_bias[None],
        conv_weight, time_weight, jnp.swapaxes(up_weight, 2, 3),
    )


def solution(mesh):
    placed = (P("tm", "tile", None, None), P(), P(), P(), P(), P(), P(), P())
    return jax.shard_map(
        functools.partial(local, mesh.shape["tm"], mesh.shape["tile"]),
        mesh=mesh, in_specs=placed, out_specs=P("tm", "tile", None, None), check_vma=False,
    )
```

```python
import functools

import jax
import jax.numpy as jnp
from jax import lax
from jax.experimental import pallas as pl
from jax.experimental.pallas import tpu as pltpu
from jax.sharding import PartitionSpec as P

F32 = jnp.float32
BF16 = jnp.bfloat16
MESH = pl.DeviceIdType.MESH


def column_shift(flat, cols, step):
    total = flat.shape[0]
    rolled = pltpu.roll(flat, step % total, 0)
    place = lax.broadcasted_iota(jnp.int32, flat.shape, 0) % cols
    edge = 0 if step > 0 else cols - 1
    return jnp.where(place == edge, 0.0, rolled)


def kernel(
    frames, tiles,
    lat_hbm, gain_ref, cb_ref, tb_ref, ub_ref, cw_hbm, tw_hbm, uw_hbm,
    out_ref,
    lat, act, act_hist, parts, part_in, blk, blk_hist, dbl,
    cw, tw, uw, umat, acc, wide_lo, wide_hi,
    lat_sem, cw_sem, tw_sem, uw_sem,
    a_send, a_recv, a_fsend, b_send, b_recv, b_fsend,
    p_down_sem, p_up_sem, b_down_sem, d_up_sem,
):
    rows, cols, chans = lat.shape
    outs_n = uw.shape[2]
    low = 128
    high = outs_n - low
    cells = rows * cols
    t = lax.axis_index("tm")
    s = lax.axis_index("tile")
    odd = lax.rem(t, 2) == 1
    even = jnp.logical_not(odd)
    has_next = t + 2 < frames
    has_prev = t >= 2
    has_up = s > 0
    has_down = s < tiles - 1

    lat_copy = pltpu.make_async_copy(lat_hbm.at[0], lat, lat_sem)
    lat_copy.start()
    cw_copies = {}
    for dt in (2, 0, 1):
        for dh in range(3):
            copy = pltpu.make_async_copy(
                cw_hbm.at[dt, dh],
                cw.at[dt, :, :, pl.ds(dh * chans, chans)],
                cw_sem.at[dt, dh],
            )
            copy.start()
            cw_copies[dt, dh] = copy
    tw_copy = pltpu.make_async_copy(tw_hbm, tw, tw_sem)
    tw_copy.start()
    uw_copy = pltpu.make_async_copy(uw_hbm, uw, uw_sem)
    uw_copy.start()

    sibling = t + 1 - 2 * lax.rem(t, 2)
    barrier = pltpu.get_barrier_semaphore()

    def greet(condition, where):
        @pl.when(condition)
        def _():
            pl.semaphore_signal(barrier, inc=1, device_id=where, device_id_type=MESH)

    pl.semaphore_signal(barrier, inc=1, device_id={"tm": sibling}, device_id_type=MESH)
    greet(has_next, {"tm": t + 2})
    greet(has_prev, {"tm": t - 2})
    greet(has_up, {"tile": s - 1})
    greet(has_down, {"tile": s + 1})

    lat_copy.wait()
    for r in range(rows)[::-1]:
        values = lat[r].astype(F32)
        meansq = jnp.mean(values * values, axis=-1, keepdims=True)
        scaled = values * lax.rsqrt(meansq + 1e-06) * gain_ref[...].reshape(1, chans)
        act[r] = (scaled * jax.nn.sigmoid(scaled)).astype(BF16)

    peers = 1
    for condition in (has_next, has_prev, has_up, has_down):
        peers = peers + condition.astype(jnp.int32)
    pl.semaphore_wait(barrier, peers)

    def history_copies(own, hist, send, recv, fsend):
        def nearer(r):
            return pltpu.make_async_remote_copy(
                own.at[r], hist.at[1, r], send.at[0, r], recv.at[1, r],
                device_id={"tm": sibling}, device_id_type=MESH,
            )

        def farther(r):
            return pltpu.make_async_remote_copy(
                own.at[r], hist.at[0, r], send.at[1, r], recv.at[0, r],
                device_id={"tm": t + 2}, device_id_type=MESH,
            )

        def forward(r):
            return pltpu.make_async_remote_copy(
                hist.at[0, r], hist.at[1, r], fsend.at[r], recv.at[1, r],
                device_id={"tm": sibling}, device_id_type=MESH,
            )

        return nearer, farther, forward

    def history_start(copies, r):
        nearer, farther, _ = copies

        @pl.when(has_next)
        def _():
            farther(r).start()

        @pl.when(even)
        def _():
            nearer(r).start()

    def history_far(copies, hist, r):
        _, farther, forward = copies

        @pl.when(has_prev)
        def _():
            farther(r).wait_recv()

            @pl.when(odd)
            def _():
                forward(r).start()

        @pl.when(jnp.logical_not(has_prev))
        def _():
            hist[0, r] = jnp.zeros(hist.shape[2:], BF16)

    def history_near(copies, hist, r):
        nearer, _, _ = copies

        @pl.when(t >= 1)
        def _():
            nearer(r).wait_recv()

        @pl.when(t == 0)
        def _():
            hist[1, r] = jnp.zeros(hist.shape[2:], BF16)

    def history_end(copies, r):
        nearer, farther, forward = copies

        @pl.when(has_next)
        def _():
            farther(r).wait_send()

        @pl.when(even)
        def _():
            nearer(r).wait_send()

        @pl.when(jnp.logical_and(odd, has_prev))
        def _():
            forward(r).wait_send()

    def to_tile(src, dst, sems, where):
        return pltpu.make_async_remote_copy(
            src, dst, sems.at[0], sems.at[1], device_id={"tile": where}, device_id_type=MESH
        )

    first, last = 0, rows - 1
    act_copies = history_copies(act, act_hist, a_send, a_recv, a_fsend)
    blk_copies = history_copies(blk, blk_hist, b_send, b_recv, b_fsend)
    part_down = to_tile(parts.at[1], part_in.at[0], p_down_sem, s + 1)
    part_up = to_tile(parts.at[0], part_in.at[1], p_up_sem, s - 1)
    blk_down = to_tile(blk.at[rows], blk.at[0], b_down_sem, s + 1)
    dbl_up = to_tile(dbl.at[1], dbl.at[rows + 1], d_up_sem, s - 1)

    order = tuple(range(rows))[::-1]
    for r in order:
        history_start(act_copies, r)

    def conv_step(frame, dt):
        flat = frame.reshape(-1, chans)
        wide = flat.astype(F32)
        before = column_shift(wide, cols, 1).astype(BF16)
        after = column_shift(wide, cols, -1).astype(BF16)
        stacked = jnp.concatenate([before, flat, after], axis=1)
        return jnp.dot(
            stacked, cw[dt].reshape(3 * chans, 3 * chans), preferred_element_type=F32
        )

    def weights_ready(dt):
        for dh in range(3):
            cw_copies[dt, dh].wait()

    weights_ready(2)
    acc[...] = conv_step(act[...], 2)
    weights_ready(0)
    weights_ready(1)
    for r in order:
        span = pl.ds(r * cols, cols)
        history_far(act_copies, act_hist, r)
        acc[span, :] += conv_step(act_hist[0, r], 0)
        history_near(act_copies, act_hist, r)
        acc[span, :] += conv_step(act_hist[1, r], 1)
        if r == last:
            parts[1] = acc[span, pl.ds(0, chans)].astype(BF16)

            @pl.when(has_down)
            def _():
                part_down.start()
        if r == first:
            parts[0] = acc[span, pl.ds(2 * chans, chans)].astype(BF16)

            @pl.when(has_up)
            def _():
                part_up.start()

    def finish_row(r):
        total = acc[pl.ds(r * cols, cols), pl.ds(chans, chans)]
        if r > 0:
            total = total + acc[pl.ds((r - 1) * cols, cols), pl.ds(0, chans)]
        if r < rows - 1:
            total = total + acc[pl.ds((r + 1) * cols, cols), pl.ds(2 * chans, chans)]
        total = total + cb_ref[...].reshape(1, chans) + lat[r].astype(F32)
        if r == first:
            total = total + part_in[0].astype(F32)
        if r == last:
            total = total + part_in[1].astype(F32)
        blk[1 + r] = total.astype(BF16)

    @pl.when(has_up)
    def _():
        part_down.wait_recv()

    @pl.when(jnp.logical_not(has_up))
    def _():
        part_in[0] = jnp.zeros((cols, chans), BF16)

    for r in range(rows - 1):
        finish_row(r)
        history_start(blk_copies, 1 + r)

    @pl.when(has_down)
    def _():
        part_up.wait_recv()

    @pl.when(jnp.logical_not(has_down))
    def _():
        part_in[1] = jnp.zeros((cols, chans), BF16)

    finish_row(last)

    @pl.when(has_down)
    def _():
        blk_down.start()

    history_start(blk_copies, rows)

    uw_copy.wait()
    row_sets = {(0, 0): (0,), (0, 1): (1, 2), (1, 0): (0, 1), (1, 1): (2,)}
    for (a, i), picks in row_sets.items():
        taps = []
        for kw in range(3):
            tap = uw[picks[0], kw].astype(F32)
            for kh in picks[1:]:
                tap = tap + uw[kh, kw].astype(F32)
            taps.append(tap)
        center = (taps[1] + taps[2], taps[0] + taps[1])
        sides = (taps[0], taps[2])
        lanes = pl.ds(i * chans, chans)
        for base, pair in ((0, center), (2 * outs_n, sides)):
            for b in range(2):
                value = pair[b].astype(BF16)
                umat[a, pl.ds(base + b * low, low), lanes] = value[:low]
                umat[a, pl.ds(base + 2 * low + b * high, high), lanes] = value[low:]

    tw_copy.wait()

    def mix(row, k):
        return jnp.dot(row.reshape(-1, chans), tw[k], preferred_element_type=F32)

    def mix_row(j, mixed):
        mixed = mixed + mix(blk_hist[0, j], 0)
        history_near(blk_copies, blk_hist, j)
        mixed = (mixed + mix(blk_hist[1, j], 1)).astype(BF16)
        for f in range(2):
            dbl[j, f] = mixed[:, f * chans : (f + 1) * chans]

    def newest(j):
        return mix(blk[j], 2) + tb_ref[...].reshape(1, 2 * chans)

    for r in range(rows):
        start = newest(1 + r)
        if r == last:
            @pl.when(has_up)
            def _():
                blk_down.wait_recv()
                history_start(blk_copies, 0)

        history_far(blk_copies, blk_hist, 1 + r)
        mix_row(1 + r, start)
        if r == first:
            @pl.when(has_up)
            def _():
                dbl_up.start()

    bias_row = ub_ref[...].reshape(1, outs_n)
    up_bias = jnp.concatenate(
        [bias_row[:, :low], bias_row[:, :low], bias_row[:, low:], bias_row[:, low:]], axis=1
    )

    def upsample_row(a, r):
        near = dbl[r + a].reshape(2 * cols, chans)
        far = dbl[r + a + 1].reshape(2 * cols, chans)
        both = jnp.concatenate([near, far], axis=1)
        result = lax.dot_general(
            both, umat[a], (((1,), (1,)), ((), ())), preferred_element_type=F32
        )
        center = result[:, : 2 * outs_n] + up_bias
        sides = result[:, 2 * outs_n :]
        even = center[:, :low] + column_shift(sides[:, :low], cols, 1)
        uneven = center[:, low : 2 * low] + column_shift(sides[:, low : 2 * low], cols, -1)
        tail = sides[:, 2 * low :]
        lane = lax.broadcasted_iota(jnp.int32, tail.shape, 1)
        tail = center[:, 2 * low :] + jnp.where(
            lane < high, column_shift(tail, cols, 1), column_shift(tail, cols, -1)
        )
        swapped = pltpu.roll(tail, high, 1)
        for f in range(2):
            span = slice(f * cols, (f + 1) * cols)
            wide_lo[pl.ds(0, cols, stride=2), :] = even[span]
            wide_lo[pl.ds(1, cols, stride=2), :] = uneven[span]
            wide_hi[pl.ds(0, cols, stride=2), :] = tail[span]
            wide_hi[pl.ds(1, cols, stride=2), :] = swapped[span]
            out_ref[f, 2 * r + a, :, pl.ds(0, low)] = wide_lo[...].astype(BF16)
            out_ref[f, 2 * r + a, :, pl.ds(low, high)] = wide_hi[:, :high].astype(BF16)

    for r in range(rows):
        for a in range(2):
            if 0 < r + a < rows:
                upsample_row(a, r)

    @pl.when(has_up)
    def _():
        history_far(blk_copies, blk_hist, 0)
        mix_row(0, newest(0))

    @pl.when(jnp.logical_not(has_up))
    def _():
        dbl[0] = jnp.zeros(dbl.shape[1:], BF16)

    upsample_row(0, 0)

    @pl.when(has_down)
    def _():
        dbl_up.wait_recv()

    @pl.when(jnp.logical_not(has_down))
    def _():
        dbl[rows + 1] = jnp.zeros(dbl.shape[1:], BF16)

    upsample_row(1, last)

    for r in range(rows):
        history_end(act_copies, r)
        history_end(blk_copies, 1 + r)

    @pl.when(has_up)
    def _():
        history_end(blk_copies, 0)
        part_up.wait_send()
        dbl_up.wait_send()

    @pl.when(has_down)
    def _():
        part_down.wait_send()
        blk_down.wait_send()


def local(frames, tiles, latent, gain, conv_weight, conv_bias, time_weight, time_bias, up_weight, up_bias):
    _, rows, cols, chans = latent.shape
    outs_n = up_weight.shape[3]
    low = 128
    vmem = pl.BlockSpec(memory_space=pltpu.VMEM)
    anywhere = pl.BlockSpec(memory_space=pltpu.HBM)
    dma = pltpu.SemaphoreType.DMA
    row = (cols, chans)
    return pl.pallas_call(
        functools.partial(kernel, frames, tiles),
        out_shape=jax.ShapeDtypeStruct((2, 2 * rows, 2 * cols, outs_n), BF16),
        in_specs=[anywhere, vmem, vmem, vmem, vmem, anywhere, anywhere, anywhere],
        out_specs=vmem,
        scratch_shapes=[
            pltpu.VMEM((rows,) + row, BF16),
            pltpu.VMEM((rows,) + row, BF16),
            pltpu.VMEM((2, rows) + row, BF16),
            pltpu.VMEM((2,) + row, BF16),
            pltpu.VMEM((2,) + row, BF16),
            pltpu.VMEM((rows + 1,) + row, BF16),
            pltpu.VMEM((2, rows + 1) + row, BF16),
            pltpu.VMEM((rows + 2, 2) + row, BF16),
            pltpu.VMEM((3, 3, chans, 3 * chans), BF16),
            pltpu.VMEM((3, chans, 2 * chans), BF16),
            pltpu.VMEM((3, 3, outs_n, chans), BF16),
            pltpu.VMEM((2, 4 * outs_n, 2 * chans), BF16),
            pltpu.VMEM((rows * cols, 3 * chans), F32),
            pltpu.VMEM((2 * cols, low), F32),
            pltpu.VMEM((2 * cols, low), F32),
            dma(()), dma((3, 3)), dma(()), dma(()),
            dma((2, rows)), dma((2, rows)), dma((rows,)),
            dma((2, rows + 1)), dma((2, rows + 1)), dma((rows + 1,)),
            dma((2,)), dma((2,)), dma((2,)), dma((2,)),
        ],
        compiler_params=pltpu.CompilerParams(
            collective_id=0, has_side_effects=True, vmem_limit_bytes=60 * 1024 * 1024
        ),
    )(
        latent, gain, conv_bias, time_bias, up_bias,
        conv_weight, time_weight, jnp.swapaxes(up_weight, 2, 3),
    )


def solution(mesh):
    placed = (P("tm", "tile", None, None), P(), P(), P(), P(), P(), P(), P())
    return jax.shard_map(
        functools.partial(local, mesh.shape["tm"], mesh.shape["tile"]),
        mesh=mesh, in_specs=placed, out_specs=P("tm", "tile", None, None), check_vma=False,
    )
```

```python
import functools

import jax
import jax.numpy as jnp
from jax import lax
from jax.experimental import pallas as pl
from jax.experimental.pallas import tpu as pltpu
from jax.sharding import PartitionSpec as P

F32 = jnp.float32
BF16 = jnp.bfloat16
MESH = pl.DeviceIdType.MESH


def column_shift(flat, cols, step):
    total = flat.shape[0]
    rolled = pltpu.roll(flat, step % total, 0)
    place = lax.broadcasted_iota(jnp.int32, flat.shape, 0) % cols
    edge = 0 if step > 0 else cols - 1
    return jnp.where(place == edge, 0.0, rolled)


def kernel(
    frames, tiles,
    lat_hbm, gain_ref, cb_ref, tb_ref, ub_ref, cw_hbm, tw_hbm, uw_hbm,
    out_ref,
    lat, act, act_hist, parts, part_in, blk, blk_hist, dbl,
    cw, tw, uw, umat, acc, mixed, edge, wide_lo, wide_hi,
    lat_sem, cw_sem, tw_sem, uw_sem,
    a_send, a_recv, a_fsend, b_send, b_recv, b_fsend,
    p_down_sem, p_up_sem, b_down_sem, d_up_sem,
):
    rows, cols, chans = lat.shape
    outs_n = uw.shape[2]
    low = 128
    high = outs_n - low
    cells = rows * cols
    t = lax.axis_index("tm")
    s = lax.axis_index("tile")
    odd = lax.rem(t, 2) == 1
    even = jnp.logical_not(odd)
    has_next = t + 2 < frames
    has_prev = t >= 2
    has_near = t >= 1
    has_up = s > 0
    has_down = s < tiles - 1

    lat_copy = pltpu.make_async_copy(lat_hbm.at[0], lat, lat_sem)
    lat_copy.start()
    cw_copies = {}
    for dt in (2, 0, 1):
        for dh in range(3):
            copy = pltpu.make_async_copy(
                cw_hbm.at[dt, dh],
                cw.at[dt, :, :, pl.ds(dh * chans, chans)],
                cw_sem.at[dt, dh],
            )
            copy.start()
            cw_copies[dt, dh] = copy
    tw_copy = pltpu.make_async_copy(tw_hbm, tw, tw_sem)
    tw_copy.start()
    uw_copy = pltpu.make_async_copy(uw_hbm, uw, uw_sem)
    uw_copy.start()

    sibling = t + 1 - 2 * lax.rem(t, 2)
    barrier = pltpu.get_barrier_semaphore()

    def greet(condition, where):
        @pl.when(condition)
        def _():
            pl.semaphore_signal(barrier, inc=1, device_id=where, device_id_type=MESH)

    pl.semaphore_signal(barrier, inc=1, device_id={"tm": sibling}, device_id_type=MESH)
    greet(has_next, {"tm": t + 2})
    greet(has_prev, {"tm": t - 2})
    greet(has_up, {"tile": s - 1})
    greet(has_down, {"tile": s + 1})

    def history_copies(own, hist, send, recv, fsend):
        def nearer(r):
            return pltpu.make_async_remote_copy(
                own.at[r], hist.at[1, r], send.at[0, r], recv.at[1, r],
                device_id={"tm": sibling}, device_id_type=MESH,
            )

        def farther(r):
            return pltpu.make_async_remote_copy(
                own.at[r], hist.at[0, r], send.at[1, r], recv.at[0, r],
                device_id={"tm": t + 2}, device_id_type=MESH,
            )

        def forward(r):
            return pltpu.make_async_remote_copy(
                hist.at[0, r], hist.at[1, r], fsend.at[r], recv.at[1, r],
                device_id={"tm": sibling}, device_id_type=MESH,
            )

        return nearer, farther, forward

    def history_start(copies, r):
        nearer, farther, _ = copies

        @pl.when(has_next)
        def _():
            farther(r).start()

        @pl.when(even)
        def _():
            nearer(r).start()

    def history_far(copies, r):
        _, farther, forward = copies
        farther(r).wait_recv()

        @pl.when(odd)
        def _():
            forward(r).start()

    def history_near(copies, r):
        copies[0](r).wait_recv()

    def history_end(copies, r):
        nearer, farther, forward = copies

        @pl.when(has_next)
        def _():
            farther(r).wait_send()

        @pl.when(even)
        def _():
            nearer(r).wait_send()

        @pl.when(jnp.logical_and(odd, has_prev))
        def _():
            forward(r).wait_send()

    def to_tile(src, dst, sems, where):
        return pltpu.make_async_remote_copy(
            src, dst, sems.at[0], sems.at[1], device_id={"tile": where}, device_id_type=MESH
        )

    first, last = 0, rows - 1
    act_copies = history_copies(act, act_hist, a_send, a_recv, a_fsend)
    blk_copies = history_copies(blk, blk_hist, b_send, b_recv, b_fsend)
    part_down = to_tile(parts.at[1], part_in.at[0], p_down_sem, s + 1)
    part_up = to_tile(parts.at[0], part_in.at[1], p_up_sem, s - 1)
    blk_down = to_tile(blk.at[rows], blk.at[0], b_down_sem, s + 1)
    dbl_up = to_tile(dbl.at[1], dbl.at[rows + 1], d_up_sem, s - 1)

    def activate(r):
        values = lat[r].astype(F32)
        meansq = jnp.mean(values * values, axis=-1, keepdims=True)
        scaled = values * lax.rsqrt(meansq + 1e-06) * gain_ref[...].reshape(1, chans)
        act[r] = (scaled * jax.nn.sigmoid(scaled)).astype(BF16)

    peers = 1
    for condition in (has_next, has_prev, has_up, has_down):
        peers = peers + condition.astype(jnp.int32)

    order = tuple(range(rows))[::-1]
    lat_copy.wait()
    for r in order:
        activate(r)
        if r == order[0]:
            pl.semaphore_wait(barrier, peers)
        history_start(act_copies, r)

    def widen(frame):
        flat = frame.reshape(-1, chans)
        wide = flat.astype(F32)
        before = column_shift(wide, cols, 1).astype(BF16)
        after = column_shift(wide, cols, -1).astype(BF16)
        return jnp.concatenate([before, flat, after], axis=1)

    def conv(stacked, dt, start, size):
        taps = cw.at[dt, :, :, pl.ds(start, size)][...].reshape(3 * chans, size)
        return jnp.dot(stacked, taps, preferred_element_type=F32)

    def weights_ready(dt):
        for dh in range(3):
            cw_copies[dt, dh].wait()

    weights_ready(2)
    acc[...] = conv(widen(act[...]), 2, 0, 3 * chans)
    weights_ready(0)
    weights_ready(1)
    for r in order:
        span = pl.ds(r * cols, cols)
        goes, stays = (0, chans) if r == last else (2 * chans, 0)
        out_part = 1 if r == last else 0

        @pl.when(has_prev)
        def _():
            history_far(act_copies, r)
            acc[span, :] += conv(widen(act_hist[0, r]), 0, 0, 3 * chans)

        @pl.when(has_near)
        def _():
            history_near(act_copies, r)
            acc[span, pl.ds(goes, chans)] += conv(widen(act_hist[1, r]), 1, goes, chans)

        parts[out_part] = acc[span, pl.ds(goes, chans)].astype(BF16)
        if r == last:
            @pl.when(has_down)
            def _():
                part_down.start()
        else:
            @pl.when(has_up)
            def _():
                part_up.start()

        @pl.when(has_near)
        def _():
            acc[span, pl.ds(stays, 2 * chans)] += conv(widen(act_hist[1, r]), 1, stays, 2 * chans)

    def finish_row(r):
        total = acc[pl.ds(r * cols, cols), pl.ds(chans, chans)]
        if r > 0:
            total = total + acc[pl.ds((r - 1) * cols, cols), pl.ds(0, chans)]
        if r < rows - 1:
            total = total + acc[pl.ds((r + 1) * cols, cols), pl.ds(2 * chans, chans)]
        total = total + cb_ref[...].reshape(1, chans) + lat[r].astype(F32)
        if r == first:
            total = total + part_in[0].astype(F32)
        if r == last:
            total = total + part_in[1].astype(F32)
        blk[1 + r] = total.astype(BF16)

    @pl.when(has_up)
    def _():
        part_down.wait_recv()

    @pl.when(jnp.logical_not(has_up))
    def _():
        part_in[0] = jnp.zeros((cols, chans), BF16)

    for r in range(rows - 1):
        finish_row(r)
        history_start(blk_copies, 1 + r)

    @pl.when(has_down)
    def _():
        part_up.wait_recv()

    @pl.when(jnp.logical_not(has_down))
    def _():
        part_in[1] = jnp.zeros((cols, chans), BF16)

    finish_row(last)

    @pl.when(has_down)
    def _():
        blk_down.start()

    history_start(blk_copies, rows)

    uw_copy.wait()
    row_sets = {(0, 0): (0,), (0, 1): (1, 2), (1, 0): (0, 1), (1, 1): (2,)}
    for (a, i), picks in row_sets.items():
        taps = []
        for kw in range(3):
            tap = uw[picks[0], kw].astype(F32)
            for kh in picks[1:]:
                tap = tap + uw[kh, kw].astype(F32)
            taps.append(tap)
        center = (taps[1] + taps[2], taps[0] + taps[1])
        sides = (taps[0], taps[2])
        lanes = pl.ds(i * chans, chans)
        for base, pair in ((0, center), (2 * outs_n, sides)):
            for b in range(2):
                value = pair[b].astype(BF16)
                umat[a, pl.ds(base + b * low, low), lanes] = value[:low]
                umat[a, pl.ds(base + 2 * low + b * high, high), lanes] = value[low:]

    tw_copy.wait()

    def mix(row, k):
        return jnp.dot(row, tw[k], preferred_element_type=F32)

    def newest(j):
        mixed[j] = mix(blk[j], 2) + tb_ref[...].reshape(1, 2 * chans)

    def mix_row(j):
        @pl.when(has_prev)
        def _():
            history_far(blk_copies, j)
            mixed[j] += mix(blk_hist[0, j], 0)

        @pl.when(has_near)
        def _():
            history_near(blk_copies, j)
            mixed[j] += mix(blk_hist[1, j], 1)

        for f in range(2):
            dbl[j, f] = mixed[j, :, pl.ds(f * chans, chans)].astype(BF16)

    for r in range(rows):
        newest(1 + r)
    for r in range(rows):
        if r == last:
            @pl.when(has_up)
            def _():
                blk_down.wait_recv()
                history_start(blk_copies, 0)

        mix_row(1 + r)
        if r == first:
            @pl.when(has_up)
            def _():
                dbl_up.start()

    bias_row = ub_ref[...].reshape(1, outs_n)
    up_bias = jnp.concatenate(
        [bias_row[:, :low], bias_row[:, :low], bias_row[:, low:], bias_row[:, low:]], axis=1
    )

    def taps_dot(row, a, start, size):
        return lax.dot_general(
            row, umat[a, :, pl.ds(start, size)], (((1,), (1,)), ((), ())), preferred_element_type=F32
        )

    def stored_row(j):
        return dbl[j].reshape(2 * cols, chans)

    def upsample_row(a, r, result):
        center = result[:, : 2 * outs_n] + up_bias
        sides = result[:, 2 * outs_n :]
        even = center[:, :low] + column_shift(sides[:, :low], cols, 1)
        uneven = center[:, low : 2 * low] + column_shift(sides[:, low : 2 * low], cols, -1)
        tail = sides[:, 2 * low :]
        lane = lax.broadcasted_iota(jnp.int32, tail.shape, 1)
        tail = center[:, 2 * low :] + jnp.where(
            lane < high, column_shift(tail, cols, 1), column_shift(tail, cols, -1)
        )
        swapped = pltpu.roll(tail, high, 1)
        for f in range(2):
            span = slice(f * cols, (f + 1) * cols)
            wide_lo[pl.ds(0, cols, stride=2), :] = even[span]
            wide_lo[pl.ds(1, cols, stride=2), :] = uneven[span]
            wide_hi[pl.ds(0, cols, stride=2), :] = tail[span]
            wide_hi[pl.ds(1, cols, stride=2), :] = swapped[span]
            out_ref[f, 2 * r + a, :, pl.ds(0, low)] = wide_lo[...].astype(BF16)
            out_ref[f, 2 * r + a, :, pl.ds(low, high)] = wide_hi[:, :high].astype(BF16)

    for r in range(rows):
        for a in range(2):
            if 0 < r + a < rows:
                both = jnp.concatenate([stored_row(r + a), stored_row(r + a + 1)], axis=1)
                upsample_row(a, r, taps_dot(both, a, 0, 2 * chans))

    edge[0] = taps_dot(stored_row(1), 0, chans, chans)
    edge[1] = taps_dot(stored_row(rows), 1, 0, chans)

    @pl.when(has_up)
    def _():
        newest(0)
        mix_row(0)
        edge[0] += taps_dot(stored_row(0), 0, 0, chans)

    upsample_row(0, 0, edge[0])

    @pl.when(has_down)
    def _():
        dbl_up.wait_recv()
        edge[1] += taps_dot(stored_row(rows + 1), 1, chans, chans)

    upsample_row(1, last, edge[1])

    for r in range(rows):
        history_end(act_copies, r)
        history_end(blk_copies, 1 + r)

    @pl.when(has_up)
    def _():
        history_end(blk_copies, 0)
        part_up.wait_send()
        dbl_up.wait_send()

    @pl.when(has_down)
    def _():
        part_down.wait_send()
        blk_down.wait_send()


def local(frames, tiles, latent, gain, conv_weight, conv_bias, time_weight, time_bias, up_weight, up_bias):
    _, rows, cols, chans = latent.shape
    outs_n = up_weight.shape[3]
    low = 128
    vmem = pl.BlockSpec(memory_space=pltpu.VMEM)
    anywhere = pl.BlockSpec(memory_space=pltpu.HBM)
    dma = pltpu.SemaphoreType.DMA
    row = (cols, chans)
    return pl.pallas_call(
        functools.partial(kernel, frames, tiles),
        out_shape=jax.ShapeDtypeStruct((2, 2 * rows, 2 * cols, outs_n), BF16),
        in_specs=[anywhere, vmem, vmem, vmem, vmem, anywhere, anywhere, anywhere],
        out_specs=vmem,
        scratch_shapes=[
            pltpu.VMEM((rows,) + row, BF16),
            pltpu.VMEM((rows,) + row, BF16),
            pltpu.VMEM((2, rows) + row, BF16),
            pltpu.VMEM((2,) + row, BF16),
            pltpu.VMEM((2,) + row, BF16),
            pltpu.VMEM((rows + 1,) + row, BF16),
            pltpu.VMEM((2, rows + 1) + row, BF16),
            pltpu.VMEM((rows + 2, 2) + row, BF16),
            pltpu.VMEM((3, 3, chans, 3 * chans), BF16),
            pltpu.VMEM((3, chans, 2 * chans), BF16),
            pltpu.VMEM((3, 3, outs_n, chans), BF16),
            pltpu.VMEM((2, 4 * outs_n, 2 * chans), BF16),
            pltpu.VMEM((rows * cols, 3 * chans), F32),
            pltpu.VMEM((rows + 1, cols, 2 * chans), F32),
            pltpu.VMEM((2, 2 * cols, 4 * outs_n), F32),
            pltpu.VMEM((2 * cols, low), F32),
            pltpu.VMEM((2 * cols, low), F32),
            dma(()), dma((3, 3)), dma(()), dma(()),
            dma((2, rows)), dma((2, rows)), dma((rows,)),
            dma((2, rows + 1)), dma((2, rows + 1)), dma((rows + 1,)),
            dma((2,)), dma((2,)), dma((2,)), dma((2,)),
        ],
        compiler_params=pltpu.CompilerParams(
            collective_id=0, has_side_effects=True, vmem_limit_bytes=60 * 1024 * 1024
        ),
    )(
        latent, gain, conv_bias, time_bias, up_bias,
        conv_weight, time_weight, jnp.swapaxes(up_weight, 2, 3),
    )


def solution(mesh):
    placed = (P("tm", "tile", None, None), P(), P(), P(), P(), P(), P(), P())
    return jax.shard_map(
        functools.partial(local, mesh.shape["tm"], mesh.shape["tile"]),
        mesh=mesh, in_specs=placed, out_specs=P("tm", "tile", None, None), check_vma=False,
    )
```

```python
import functools

import jax
import jax.numpy as jnp
from jax import lax
from jax.experimental import pallas as pl
from jax.experimental.pallas import tpu as pltpu
from jax.sharding import PartitionSpec as P

F32 = jnp.float32
BF16 = jnp.bfloat16
MESH = pl.DeviceIdType.MESH


def column_shift(flat, cols, step):
    total = flat.shape[0]
    rolled = pltpu.roll(flat, step % total, 0)
    place = lax.broadcasted_iota(jnp.int32, flat.shape, 0) % cols
    edge = 0 if step > 0 else cols - 1
    return jnp.where(place == edge, 0.0, rolled)


def kernel(
    frames, tiles,
    lat_hbm, gain_hbm, cb_hbm, tb_hbm, ub_hbm, cw_hbm, tw_hbm, uw_hbm,
    out_ref,
    lat, act, act_hist, parts, part_in, blk, blk_hist, dbl,
    gain_ref, cb_ref, tb_ref, ub_ref, cw, tw, uw, umat, acc, mixed, edge, wide_lo, wide_hi,
    lat_sem, bias_sem, cw_sem, tw_sem, uw_sem,
    a_send, a_recv, a_fsend, b_send, b_recv, b_fsend,
    p_down_sem, p_up_sem, b_down_sem, d_up_sem,
):
    rows, cols, chans = lat.shape
    outs_n = uw.shape[2]
    low = 128
    high = outs_n - low
    cells = rows * cols
    t = lax.axis_index("tm")
    s = lax.axis_index("tile")
    odd = lax.rem(t, 2) == 1
    even = jnp.logical_not(odd)
    has_next = t + 2 < frames
    has_prev = t >= 2
    has_near = t >= 1
    has_up = s > 0
    has_down = s < tiles - 1

    lat_copy = pltpu.make_async_copy(lat_hbm.at[0], lat, lat_sem)
    lat_copy.start()
    bias_copies = []
    for k, (src, dst) in enumerate(
        ((gain_hbm, gain_ref), (cb_hbm, cb_ref), (tb_hbm, tb_ref), (ub_hbm, ub_ref))
    ):
        copy = pltpu.make_async_copy(src, dst, bias_sem.at[k])
        copy.start()
        bias_copies.append(copy)
    cw_copies = {}
    for dt in (2, 0, 1):
        for dh in range(3):
            copy = pltpu.make_async_copy(
                cw_hbm.at[dt, dh],
                cw.at[dt, :, :, pl.ds(dh * chans, chans)],
                cw_sem.at[dt, dh],
            )
            copy.start()
            cw_copies[dt, dh] = copy
    tw_copy = pltpu.make_async_copy(tw_hbm, tw, tw_sem)
    tw_copy.start()
    uw_copy = pltpu.make_async_copy(uw_hbm, uw, uw_sem)
    uw_copy.start()

    sibling = t + 1 - 2 * lax.rem(t, 2)
    barrier = pltpu.get_barrier_semaphore()

    def greet(condition, where):
        @pl.when(condition)
        def _():
            pl.semaphore_signal(barrier, inc=1, device_id=where, device_id_type=MESH)

    pl.semaphore_signal(barrier, inc=1, device_id={"tm": sibling}, device_id_type=MESH)
    greet(has_next, {"tm": t + 2})
    greet(has_prev, {"tm": t - 2})
    greet(has_up, {"tile": s - 1})
    greet(has_down, {"tile": s + 1})

    def history_copies(own, hist, send, recv, fsend):
        def nearer(r):
            return pltpu.make_async_remote_copy(
                own.at[r], hist.at[1, r], send.at[0, r], recv.at[1, r],
                device_id={"tm": sibling}, device_id_type=MESH,
            )

        def farther(r):
            return pltpu.make_async_remote_copy(
                own.at[r], hist.at[0, r], send.at[1, r], recv.at[0, r],
                device_id={"tm": t + 2}, device_id_type=MESH,
            )

        def forward(r):
            return pltpu.make_async_remote_copy(
                hist.at[0, r], hist.at[1, r], fsend.at[r], recv.at[1, r],
                device_id={"tm": sibling}, device_id_type=MESH,
            )

        return nearer, farther, forward

    def history_start(copies, r):
        nearer, farther, _ = copies

        @pl.when(has_next)
        def _():
            farther(r).start()

        @pl.when(even)
        def _():
            nearer(r).start()

    def history_far(copies, r):
        _, farther, forward = copies
        farther(r).wait_recv()

        @pl.when(odd)
        def _():
            forward(r).start()

    def history_near(copies, r):
        copies[0](r).wait_recv()

    def history_end(copies, r):
        nearer, farther, forward = copies

        @pl.when(has_next)
        def _():
            farther(r).wait_send()

        @pl.when(even)
        def _():
            nearer(r).wait_send()

        @pl.when(jnp.logical_and(odd, has_prev))
        def _():
            forward(r).wait_send()

    def to_tile(src, dst, sems, where):
        return pltpu.make_async_remote_copy(
            src, dst, sems.at[0], sems.at[1], device_id={"tile": where}, device_id_type=MESH
        )

    first, last = 0, rows - 1
    act_copies = history_copies(act, act_hist, a_send, a_recv, a_fsend)
    blk_copies = history_copies(blk, blk_hist, b_send, b_recv, b_fsend)
    part_down = to_tile(parts.at[1], part_in.at[0], p_down_sem, s + 1)
    part_up = to_tile(parts.at[0], part_in.at[1], p_up_sem, s - 1)
    blk_down = to_tile(blk.at[rows], blk.at[0], b_down_sem, s + 1)
    dbl_up = to_tile(dbl.at[1], dbl.at[rows + 1], d_up_sem, s - 1)

    def activate(r):
        values = lat[r].astype(F32)
        meansq = jnp.mean(values * values, axis=-1, keepdims=True)
        scaled = values * lax.rsqrt(meansq + 1e-06) * gain_ref[...].reshape(1, chans)
        act[r] = (scaled * jax.nn.sigmoid(scaled)).astype(BF16)

    peers = 1
    for condition in (has_next, has_prev, has_up, has_down):
        peers = peers + condition.astype(jnp.int32)

    order = tuple(range(rows))[::-1]
    lat_copy.wait()
    for copy in bias_copies:
        copy.wait()
    for r in order:
        activate(r)
        if r == order[0]:
            pl.semaphore_wait(barrier, peers)
        history_start(act_copies, r)

    def widen(frame):
        flat = frame.reshape(-1, chans)
        wide = flat.astype(F32)
        before = column_shift(wide, cols, 1).astype(BF16)
        after = column_shift(wide, cols, -1).astype(BF16)
        return jnp.concatenate([before, flat, after], axis=1)

    def conv(stacked, dt, start, size):
        taps = cw.at[dt, :, :, pl.ds(start, size)][...].reshape(3 * chans, size)
        return jnp.dot(stacked, taps, preferred_element_type=F32)

    def weights_ready(dt):
        for dh in range(3):
            cw_copies[dt, dh].wait()

    weights_ready(2)
    acc[...] = conv(widen(act[...]), 2, 0, 3 * chans)
    weights_ready(0)
    weights_ready(1)
    for r in order:
        span = pl.ds(r * cols, cols)
        goes, stays = (0, chans) if r == last else (2 * chans, 0)
        out_part = 1 if r == last else 0

        @pl.when(has_prev)
        def _():
            history_far(act_copies, r)
            acc[span, :] += conv(widen(act_hist[0, r]), 0, 0, 3 * chans)

        @pl.when(has_near)
        def _():
            history_near(act_copies, r)
            acc[span, pl.ds(goes, chans)] += conv(widen(act_hist[1, r]), 1, goes, chans)

        parts[out_part] = acc[span, pl.ds(goes, chans)].astype(BF16)
        if r == last:
            @pl.when(has_down)
            def _():
                part_down.start()
        else:
            @pl.when(has_up)
            def _():
                part_up.start()

        @pl.when(has_near)
        def _():
            acc[span, pl.ds(stays, 2 * chans)] += conv(widen(act_hist[1, r]), 1, stays, 2 * chans)

    def finish_row(r):
        total = acc[pl.ds(r * cols, cols), pl.ds(chans, chans)]
        if r > 0:
            total = total + acc[pl.ds((r - 1) * cols, cols), pl.ds(0, chans)]
        if r < rows - 1:
            total = total + acc[pl.ds((r + 1) * cols, cols), pl.ds(2 * chans, chans)]
        total = total + cb_ref[...].reshape(1, chans) + lat[r].astype(F32)
        if r == first:
            total = total + part_in[0].astype(F32)
        if r == last:
            total = total + part_in[1].astype(F32)
        blk[1 + r] = total.astype(BF16)

    @pl.when(has_up)
    def _():
        part_down.wait_recv()

    @pl.when(jnp.logical_not(has_up))
    def _():
        part_in[0] = jnp.zeros((cols, chans), BF16)

    for r in range(rows - 1):
        finish_row(r)
        history_start(blk_copies, 1 + r)

    @pl.when(has_down)
    def _():
        part_up.wait_recv()

    @pl.when(jnp.logical_not(has_down))
    def _():
        part_in[1] = jnp.zeros((cols, chans), BF16)

    finish_row(last)

    @pl.when(has_down)
    def _():
        blk_down.start()

    history_start(blk_copies, rows)

    uw_copy.wait()
    row_sets = {(0, 0): (0,), (0, 1): (1, 2), (1, 0): (0, 1), (1, 1): (2,)}
    for (a, i), picks in row_sets.items():
        taps = []
        for kw in range(3):
            tap = uw[picks[0], kw].astype(F32)
            for kh in picks[1:]:
                tap = tap + uw[kh, kw].astype(F32)
            taps.append(tap)
        center = (taps[1] + taps[2], taps[0] + taps[1])
        sides = (taps[0], taps[2])
        lanes = pl.ds(i * chans, chans)
        for base, pair in ((0, center), (2 * outs_n, sides)):
            for b in range(2):
                value = pair[b].astype(BF16)
                umat[a, pl.ds(base + b * low, low), lanes] = value[:low]
                umat[a, pl.ds(base + 2 * low + b * high, high), lanes] = value[low:]

    tw_copy.wait()

    def mix(row, k):
        return jnp.dot(row, tw[k], preferred_element_type=F32)

    def newest(j):
        mixed[j] = mix(blk[j], 2) + tb_ref[...].reshape(1, 2 * chans)

    def mix_row(j):
        @pl.when(has_prev)
        def _():
            history_far(blk_copies, j)
            mixed[j] += mix(blk_hist[0, j], 0)

        @pl.when(has_near)
        def _():
            history_near(blk_copies, j)
            mixed[j] += mix(blk_hist[1, j], 1)

        for f in range(2):
            dbl[j, f] = mixed[j, :, pl.ds(f * chans, chans)].astype(BF16)

    for r in range(rows):
        newest(1 + r)
    for r in range(rows):
        if r == last:
            @pl.when(has_up)
            def _():
                blk_down.wait_recv()
                history_start(blk_copies, 0)

        mix_row(1 + r)
        if r == first:
            @pl.when(has_up)
            def _():
                dbl_up.start()

    bias_row = ub_ref[...].reshape(1, outs_n)
    up_bias = jnp.concatenate(
        [bias_row[:, :low], bias_row[:, :low], bias_row[:, low:], bias_row[:, low:]], axis=1
    )

    def taps_dot(row, a, start, size):
        return lax.dot_general(
            row, umat[a, :, pl.ds(start, size)], (((1,), (1,)), ((), ())), preferred_element_type=F32
        )

    def stored_row(j):
        return dbl[j].reshape(2 * cols, chans)

    def upsample_row(a, r, result):
        center = result[:, : 2 * outs_n] + up_bias
        sides = result[:, 2 * outs_n :]
        even = center[:, :low] + column_shift(sides[:, :low], cols, 1)
        uneven = center[:, low : 2 * low] + column_shift(sides[:, low : 2 * low], cols, -1)
        tail = sides[:, 2 * low :]
        lane = lax.broadcasted_iota(jnp.int32, tail.shape, 1)
        tail = center[:, 2 * low :] + jnp.where(
            lane < high, column_shift(tail, cols, 1), column_shift(tail, cols, -1)
        )
        swapped = pltpu.roll(tail, high, 1)
        for f in range(2):
            span = slice(f * cols, (f + 1) * cols)
            wide_lo[pl.ds(0, cols, stride=2), :] = even[span]
            wide_lo[pl.ds(1, cols, stride=2), :] = uneven[span]
            wide_hi[pl.ds(0, cols, stride=2), :] = tail[span]
            wide_hi[pl.ds(1, cols, stride=2), :] = swapped[span]
            out_ref[f, 2 * r + a, :, pl.ds(0, low)] = wide_lo[...].astype(BF16)
            out_ref[f, 2 * r + a, :, pl.ds(low, high)] = wide_hi[:, :high].astype(BF16)

    for r in range(rows):
        for a in range(2):
            if 0 < r + a < rows:
                both = jnp.concatenate([stored_row(r + a), stored_row(r + a + 1)], axis=1)
                upsample_row(a, r, taps_dot(both, a, 0, 2 * chans))

    edge[0] = taps_dot(stored_row(1), 0, chans, chans)
    edge[1] = taps_dot(stored_row(rows), 1, 0, chans)

    @pl.when(has_up)
    def _():
        newest(0)
        mix_row(0)
        edge[0] += taps_dot(stored_row(0), 0, 0, chans)

    upsample_row(0, 0, edge[0])

    @pl.when(has_down)
    def _():
        dbl_up.wait_recv()
        edge[1] += taps_dot(stored_row(rows + 1), 1, chans, chans)

    upsample_row(1, last, edge[1])

    for r in range(rows):
        history_end(act_copies, r)
        history_end(blk_copies, 1 + r)

    @pl.when(has_up)
    def _():
        history_end(blk_copies, 0)
        part_up.wait_send()
        dbl_up.wait_send()

    @pl.when(has_down)
    def _():
        part_down.wait_send()
        blk_down.wait_send()


def local(frames, tiles, latent, gain, conv_weight, conv_bias, time_weight, time_bias, up_weight, up_bias):
    _, rows, cols, chans = latent.shape
    outs_n = up_weight.shape[3]
    low = 128
    dma = pltpu.SemaphoreType.DMA
    row = (cols, chans)
    return pl.pallas_call(
        functools.partial(kernel, frames, tiles),
        out_shape=jax.ShapeDtypeStruct((2, 2 * rows, 2 * cols, outs_n), BF16),
        in_specs=[pl.BlockSpec(memory_space=pltpu.HBM)] * 8,
        out_specs=pl.BlockSpec(memory_space=pltpu.VMEM),
        scratch_shapes=[
            pltpu.VMEM((rows,) + row, BF16),
            pltpu.VMEM((rows,) + row, BF16),
            pltpu.VMEM((2, rows) + row, BF16),
            pltpu.VMEM((2,) + row, BF16),
            pltpu.VMEM((2,) + row, BF16),
            pltpu.VMEM((rows + 1,) + row, BF16),
            pltpu.VMEM((2, rows + 1) + row, BF16),
            pltpu.VMEM((rows + 2, 2) + row, BF16),
            pltpu.VMEM((chans,), F32),
            pltpu.VMEM((chans,), F32),
            pltpu.VMEM((2 * chans,), F32),
            pltpu.VMEM((outs_n,), F32),
            pltpu.VMEM((3, 3, chans, 3 * chans), BF16),
            pltpu.VMEM((3, chans, 2 * chans), BF16),
            pltpu.VMEM((3, 3, outs_n, chans), BF16),
            pltpu.VMEM((2, 4 * outs_n, 2 * chans), BF16),
            pltpu.VMEM((rows * cols, 3 * chans), F32),
            pltpu.VMEM((rows + 1, cols, 2 * chans), F32),
            pltpu.VMEM((2, 2 * cols, 4 * outs_n), F32),
            pltpu.VMEM((2 * cols, low), F32),
            pltpu.VMEM((2 * cols, low), F32),
            dma(()), dma((4,)), dma((3, 3)), dma(()), dma(()),
            dma((2, rows)), dma((2, rows)), dma((rows,)),
            dma((2, rows + 1)), dma((2, rows + 1)), dma((rows + 1,)),
            dma((2,)), dma((2,)), dma((2,)), dma((2,)),
        ],
        compiler_params=pltpu.CompilerParams(
            collective_id=0, has_side_effects=True, vmem_limit_bytes=48 * 1024 * 1024
        ),
    )(*(
        pltpu.with_memory_space_constraint(array, pltpu.HBM)
        for array in (
            latent, gain, conv_bias, time_bias, up_bias,
            conv_weight, time_weight, jnp.swapaxes(up_weight, 2, 3),
        )
    ))


def solution(mesh):
    placed = (P("tm", "tile", None, None), P(), P(), P(), P(), P(), P(), P())
    return jax.shard_map(
        functools.partial(local, mesh.shape["tm"], mesh.shape["tile"]),
        mesh=mesh, in_specs=placed, out_specs=P("tm", "tile", None, None), check_vma=False,
    )
```

```python
import functools

import jax
import jax.numpy as jnp
from jax import lax
from jax.experimental import pallas as pl
from jax.experimental.pallas import tpu as pltpu
from jax.sharding import PartitionSpec as P

F32 = jnp.float32
BF16 = jnp.bfloat16
MESH = pl.DeviceIdType.MESH


def column_shift(flat, cols, step):
    total = flat.shape[0]
    rolled = pltpu.roll(flat, step % total, 0)
    place = lax.broadcasted_iota(jnp.int32, flat.shape, 0) % cols
    edge = 0 if step > 0 else cols - 1
    return jnp.where(place == edge, 0.0, rolled)


def kernel(
    frames, tiles,
    lat_hbm, gain_hbm, cb_hbm, tb_hbm, ub_hbm, cw_hbm, tw_hbm, uw_hbm,
    out_ref,
    lat, act, act_hist, act_relay, parts, part_in, blk, blk_hist, dbl,
    gain_ref, cb_ref, tb_ref, ub_ref, cw, tw, uw, umat, acc, mixed, edge, wide_lo, wide_hi,
    lat_sem, bias_sem, cw_sem, tw_sem, uw_sem,
    a_send, a_recv, a_fsend, r_send, r_recv, b_send, b_recv, b_fsend,
    p_down_sem, p_up_sem, b_down_sem, d_up_sem,
):
    rows, cols, chans = lat.shape
    outs_n = uw.shape[2]
    low = 128
    high = outs_n - low
    cells = rows * cols
    t = lax.axis_index("tm")
    s = lax.axis_index("tile")
    odd = lax.rem(t, 2) == 1
    even = jnp.logical_not(odd)
    has_next = t + 2 < frames
    has_prev = t >= 2
    has_near = t >= 1
    has_up = s > 0
    has_down = s < tiles - 1

    lat_copy = pltpu.make_async_copy(lat_hbm.at[0], lat, lat_sem)
    lat_copy.start()
    bias_copies = []
    for k, (src, dst) in enumerate(
        ((gain_hbm, gain_ref), (cb_hbm, cb_ref), (tb_hbm, tb_ref), (ub_hbm, ub_ref))
    ):
        copy = pltpu.make_async_copy(src, dst, bias_sem.at[k])
        copy.start()
        bias_copies.append(copy)
    cw_copies = {}
    for dt in (2, 0, 1):
        for dh in range(3):
            copy = pltpu.make_async_copy(
                cw_hbm.at[dt, dh],
                cw.at[dt, :, :, pl.ds(dh * chans, chans)],
                cw_sem.at[dt, dh],
            )
            copy.start()
            cw_copies[dt, dh] = copy
    tw_copy = pltpu.make_async_copy(tw_hbm, tw, tw_sem)
    tw_copy.start()
    uw_copy = pltpu.make_async_copy(uw_hbm, uw, uw_sem)
    uw_copy.start()

    half = frames // 2
    partner = s + 1 - 2 * lax.rem(s, 2)
    relays_out = t // 2 == half // 2 - 1
    relays_in = t // 2 == half // 2
    plain_out = jnp.logical_and(has_next, jnp.logical_not(relays_out))

    sibling = t + 1 - 2 * lax.rem(t, 2)
    barrier = pltpu.get_barrier_semaphore()

    def greet(condition, where):
        @pl.when(condition)
        def _():
            pl.semaphore_signal(barrier, inc=1, device_id=where, device_id_type=MESH)

    pl.semaphore_signal(barrier, inc=1, device_id={"tm": sibling}, device_id_type=MESH)
    greet(has_next, {"tm": t + 2})
    greet(has_prev, {"tm": t - 2})
    greet(relays_out, {"tm": t + 2, "tile": partner})
    greet(relays_in, {"tm": t - 2, "tile": partner})
    greet(has_up, {"tile": s - 1})
    greet(has_down, {"tile": s + 1})

    def history_copies(own, hist, send, recv, fsend):
        def nearer(r):
            return pltpu.make_async_remote_copy(
                own.at[r], hist.at[1, r], send.at[0, r], recv.at[1, r],
                device_id={"tm": sibling}, device_id_type=MESH,
            )

        def farther(r):
            return pltpu.make_async_remote_copy(
                own.at[r], hist.at[0, r], send.at[1, r], recv.at[0, r],
                device_id={"tm": t + 2}, device_id_type=MESH,
            )

        def forward(r):
            return pltpu.make_async_remote_copy(
                hist.at[0, r], hist.at[1, r], fsend.at[r], recv.at[1, r],
                device_id={"tm": sibling}, device_id_type=MESH,
            )

        return nearer, farther, forward

    def history_start(copies, r, sends=has_next):
        nearer, farther, _ = copies

        @pl.when(sends)
        def _():
            farther(r).start()

        @pl.when(even)
        def _():
            nearer(r).start()

    def history_far(copies, r):
        _, farther, forward = copies
        farther(r).wait_recv()

        @pl.when(odd)
        def _():
            forward(r).start()

    def history_near(copies, r):
        copies[0](r).wait_recv()

    def history_end(copies, r, sends=has_next):
        nearer, farther, forward = copies

        @pl.when(sends)
        def _():
            farther(r).wait_send()

        @pl.when(even)
        def _():
            nearer(r).wait_send()

        @pl.when(jnp.logical_and(odd, has_prev))
        def _():
            forward(r).wait_send()

    def to_tile(src, dst, sems, where):
        return pltpu.make_async_remote_copy(
            src, dst, sems.at[0], sems.at[1], device_id={"tile": where}, device_id_type=MESH
        )

    first, last = 0, rows - 1
    act_copies = history_copies(act, act_hist, a_send, a_recv, a_fsend)
    blk_copies = history_copies(blk, blk_hist, b_send, b_recv, b_fsend)
    part_down = to_tile(parts.at[1], part_in.at[0], p_down_sem, s + 1)
    part_up = to_tile(parts.at[0], part_in.at[1], p_up_sem, s - 1)
    blk_down = to_tile(blk.at[rows], blk.at[0], b_down_sem, s + 1)
    dbl_up = to_tile(dbl.at[1], dbl.at[rows + 1], d_up_sem, s - 1)

    def activate(r):
        values = lat[r].astype(F32)
        meansq = jnp.mean(values * values, axis=-1, keepdims=True)
        scaled = values * lax.rsqrt(meansq + 1e-06) * gain_ref[...].reshape(1, chans)
        act[r] = (scaled * jax.nn.sigmoid(scaled)).astype(BF16)

    peers = 1
    for condition in (has_next, has_prev, relays_out, relays_in, has_up, has_down):
        peers = peers + condition.astype(jnp.int32)

    def relay_out(r):
        return pltpu.make_async_remote_copy(
            act.at[r], act_relay.at[r], r_send.at[0, r], r_recv.at[r],
            device_id={"tm": t + 2, "tile": partner}, device_id_type=MESH,
        )

    def relay_on(r):
        return pltpu.make_async_remote_copy(
            act_relay.at[r], act_hist.at[0, r], r_send.at[1, r], a_recv.at[0, r],
            device_id={"tile": partner}, device_id_type=MESH,
        )

    order = tuple(range(rows))[::-1]
    lat_copy.wait()
    for copy in bias_copies:
        copy.wait()
    for r in order:
        activate(r)
        if r == order[0]:
            pl.semaphore_wait(barrier, peers)
        @pl.when(relays_out)
        def _():
            relay_out(r).start()

        history_start(act_copies, r, plain_out)

    def widen(frame):
        flat = frame.reshape(-1, chans)
        wide = flat.astype(F32)
        before = column_shift(wide, cols, 1).astype(BF16)
        after = column_shift(wide, cols, -1).astype(BF16)
        return jnp.concatenate([before, flat, after], axis=1)

    def conv(stacked, dt, start, size):
        taps = cw.at[dt, :, :, pl.ds(start, size)][...].reshape(3 * chans, size)
        return jnp.dot(stacked, taps, preferred_element_type=F32)

    def weights_ready(dt):
        for dh in range(3):
            cw_copies[dt, dh].wait()

    weights_ready(2)
    acc[...] = conv(widen(act[...]), 2, 0, 3 * chans)
    weights_ready(0)
    weights_ready(1)
    for r in order:
        span = pl.ds(r * cols, cols)
        goes, stays = (0, chans) if r == last else (2 * chans, 0)
        out_part = 1 if r == last else 0

        @pl.when(has_prev)
        def _():
            @pl.when(relays_in)
            def _():
                relay_out(r).wait_recv()
                relay_on(r).start()

            history_far(act_copies, r)
            acc[span, :] += conv(widen(act_hist[0, r]), 0, 0, 3 * chans)

        @pl.when(has_near)
        def _():
            history_near(act_copies, r)
            acc[span, pl.ds(goes, chans)] += conv(widen(act_hist[1, r]), 1, goes, chans)

        parts[out_part] = acc[span, pl.ds(goes, chans)].astype(BF16)
        if r == last:
            @pl.when(has_down)
            def _():
                part_down.start()
        else:
            @pl.when(has_up)
            def _():
                part_up.start()

        @pl.when(has_near)
        def _():
            acc[span, pl.ds(stays, 2 * chans)] += conv(widen(act_hist[1, r]), 1, stays, 2 * chans)

    def finish_row(r):
        total = acc[pl.ds(r * cols, cols), pl.ds(chans, chans)]
        if r > 0:
            total = total + acc[pl.ds((r - 1) * cols, cols), pl.ds(0, chans)]
        if r < rows - 1:
            total = total + acc[pl.ds((r + 1) * cols, cols), pl.ds(2 * chans, chans)]
        total = total + cb_ref[...].reshape(1, chans) + lat[r].astype(F32)
        if r == first:
            total = total + part_in[0].astype(F32)
        if r == last:
            total = total + part_in[1].astype(F32)
        blk[1 + r] = total.astype(BF16)

    @pl.when(has_up)
    def _():
        part_down.wait_recv()

    @pl.when(jnp.logical_not(has_up))
    def _():
        part_in[0] = jnp.zeros((cols, chans), BF16)

    for r in range(rows - 1):
        finish_row(r)
        history_start(blk_copies, 1 + r)

    @pl.when(has_down)
    def _():
        part_up.wait_recv()

    @pl.when(jnp.logical_not(has_down))
    def _():
        part_in[1] = jnp.zeros((cols, chans), BF16)

    finish_row(last)

    @pl.when(has_down)
    def _():
        blk_down.start()

    history_start(blk_copies, rows)

    uw_copy.wait()
    row_sets = {(0, 0): (0,), (0, 1): (1, 2), (1, 0): (0, 1), (1, 1): (2,)}
    for (a, i), picks in row_sets.items():
        taps = []
        for kw in range(3):
            tap = uw[picks[0], kw].astype(F32)
            for kh in picks[1:]:
                tap = tap + uw[kh, kw].astype(F32)
            taps.append(tap)
        center = (taps[1] + taps[2], taps[0] + taps[1])
        sides = (taps[0], taps[2])
        lanes = pl.ds(i * chans, chans)
        for base, pair in ((0, center), (2 * outs_n, sides)):
            for b in range(2):
                value = pair[b].astype(BF16)
                umat[a, pl.ds(base + b * low, low), lanes] = value[:low]
                umat[a, pl.ds(base + 2 * low + b * high, high), lanes] = value[low:]

    tw_copy.wait()

    def mix(row, k):
        return jnp.dot(row, tw[k], preferred_element_type=F32)

    def newest(j):
        mixed[j] = mix(blk[j], 2) + tb_ref[...].reshape(1, 2 * chans)

    def mix_row(j):
        @pl.when(has_prev)
        def _():
            history_far(blk_copies, j)
            mixed[j] += mix(blk_hist[0, j], 0)

        @pl.when(has_near)
        def _():
            history_near(blk_copies, j)
            mixed[j] += mix(blk_hist[1, j], 1)

        for f in range(2):
            dbl[j, f] = mixed[j, :, pl.ds(f * chans, chans)].astype(BF16)

    for r in range(rows):
        newest(1 + r)
    for r in range(rows):
        if r == last:
            @pl.when(has_up)
            def _():
                blk_down.wait_recv()
                history_start(blk_copies, 0)

        mix_row(1 + r)
        if r == first:
            @pl.when(has_up)
            def _():
                dbl_up.start()

    bias_row = ub_ref[...].reshape(1, outs_n)
    up_bias = jnp.concatenate(
        [bias_row[:, :low], bias_row[:, :low], bias_row[:, low:], bias_row[:, low:]], axis=1
    )

    def taps_dot(row, a, start, size):
        return lax.dot_general(
            row, umat[a, :, pl.ds(start, size)], (((1,), (1,)), ((), ())), preferred_element_type=F32
        )

    def stored_row(j):
        return dbl[j].reshape(2 * cols, chans)

    def upsample_row(a, r, result):
        center = result[:, : 2 * outs_n] + up_bias
        sides = result[:, 2 * outs_n :]
        even = center[:, :low] + column_shift(sides[:, :low], cols, 1)
        uneven = center[:, low : 2 * low] + column_shift(sides[:, low : 2 * low], cols, -1)
        tail = sides[:, 2 * low :]
        lane = lax.broadcasted_iota(jnp.int32, tail.shape, 1)
        tail = center[:, 2 * low :] + jnp.where(
            lane < high, column_shift(tail, cols, 1), column_shift(tail, cols, -1)
        )
        swapped = pltpu.roll(tail, high, 1)
        for f in range(2):
            span = slice(f * cols, (f + 1) * cols)
            wide_lo[pl.ds(0, cols, stride=2), :] = even[span]
            wide_lo[pl.ds(1, cols, stride=2), :] = uneven[span]
            wide_hi[pl.ds(0, cols, stride=2), :] = tail[span]
            wide_hi[pl.ds(1, cols, stride=2), :] = swapped[span]
            out_ref[f, 2 * r + a, :, pl.ds(0, low)] = wide_lo[...].astype(BF16)
            out_ref[f, 2 * r + a, :, pl.ds(low, high)] = wide_hi[:, :high].astype(BF16)

    for r in range(rows):
        for a in range(2):
            if 0 < r + a < rows:
                both = jnp.concatenate([stored_row(r + a), stored_row(r + a + 1)], axis=1)
                upsample_row(a, r, taps_dot(both, a, 0, 2 * chans))

    edge[0] = taps_dot(stored_row(1), 0, chans, chans)
    edge[1] = taps_dot(stored_row(rows), 1, 0, chans)

    @pl.when(has_up)
    def _():
        newest(0)
        mix_row(0)
        edge[0] += taps_dot(stored_row(0), 0, 0, chans)

    upsample_row(0, 0, edge[0])

    @pl.when(has_down)
    def _():
        dbl_up.wait_recv()
        edge[1] += taps_dot(stored_row(rows + 1), 1, chans, chans)

    upsample_row(1, last, edge[1])

    for r in range(rows):
        history_end(act_copies, r, plain_out)

        @pl.when(relays_out)
        def _():
            relay_out(r).wait_send()

        @pl.when(relays_in)
        def _():
            relay_on(r).wait_send()

        history_end(blk_copies, 1 + r)

    @pl.when(has_up)
    def _():
        history_end(blk_copies, 0)
        part_up.wait_send()
        dbl_up.wait_send()

    @pl.when(has_down)
    def _():
        part_down.wait_send()
        blk_down.wait_send()


def local(frames, tiles, latent, gain, conv_weight, conv_bias, time_weight, time_bias, up_weight, up_bias):
    _, rows, cols, chans = latent.shape
    outs_n = up_weight.shape[3]
    low = 128
    dma = pltpu.SemaphoreType.DMA
    row = (cols, chans)
    return pl.pallas_call(
        functools.partial(kernel, frames, tiles),
        out_shape=jax.ShapeDtypeStruct((2, 2 * rows, 2 * cols, outs_n), BF16),
        in_specs=[pl.BlockSpec(memory_space=pltpu.HBM)] * 8,
        out_specs=pl.BlockSpec(memory_space=pltpu.VMEM),
        scratch_shapes=[
            pltpu.VMEM((rows,) + row, BF16),
            pltpu.VMEM((rows,) + row, BF16),
            pltpu.VMEM((2, rows) + row, BF16),
            pltpu.VMEM((rows,) + row, BF16),
            pltpu.VMEM((2,) + row, BF16),
            pltpu.VMEM((2,) + row, BF16),
            pltpu.VMEM((rows + 1,) + row, BF16),
            pltpu.VMEM((2, rows + 1) + row, BF16),
            pltpu.VMEM((rows + 2, 2) + row, BF16),
            pltpu.VMEM((chans,), F32),
            pltpu.VMEM((chans,), F32),
            pltpu.VMEM((2 * chans,), F32),
            pltpu.VMEM((outs_n,), F32),
            pltpu.VMEM((3, 3, chans, 3 * chans), BF16),
            pltpu.VMEM((3, chans, 2 * chans), BF16),
            pltpu.VMEM((3, 3, outs_n, chans), BF16),
            pltpu.VMEM((2, 4 * outs_n, 2 * chans), BF16),
            pltpu.VMEM((rows * cols, 3 * chans), F32),
            pltpu.VMEM((rows + 1, cols, 2 * chans), F32),
            pltpu.VMEM((2, 2 * cols, 4 * outs_n), F32),
            pltpu.VMEM((2 * cols, low), F32),
            pltpu.VMEM((2 * cols, low), F32),
            dma(()), dma((4,)), dma((3, 3)), dma(()), dma(()),
            dma((2, rows)), dma((2, rows)), dma((rows,)),
            dma((2, rows)), dma((rows,)),
            dma((2, rows + 1)), dma((2, rows + 1)), dma((rows + 1,)),
            dma((2,)), dma((2,)), dma((2,)), dma((2,)),
        ],
        compiler_params=pltpu.CompilerParams(
            collective_id=0, has_side_effects=True, vmem_limit_bytes=48 * 1024 * 1024
        ),
    )(*(
        pltpu.with_memory_space_constraint(array, pltpu.HBM)
        for array in (
            latent, gain, conv_bias, time_bias, up_bias,
            conv_weight, time_weight, jnp.swapaxes(up_weight, 2, 3),
        )
    ))


def solution(mesh):
    placed = (P("tm", "tile", None, None), P(), P(), P(), P(), P(), P(), P())
    return jax.shard_map(
        functools.partial(local, mesh.shape["tm"], mesh.shape["tile"]),
        mesh=mesh, in_specs=placed, out_specs=P("tm", "tile", None, None), check_vma=False,
    )
```

```python
import functools

import jax
import jax.numpy as jnp
from jax import lax
from jax.experimental import pallas as pl
from jax.experimental.pallas import tpu as pltpu
from jax.sharding import PartitionSpec as P

F32 = jnp.float32
BF16 = jnp.bfloat16
MESH = pl.DeviceIdType.MESH


def column_shift(flat, cols, step):
    total = flat.shape[0]
    rolled = pltpu.roll(flat, step % total, 0)
    place = lax.broadcasted_iota(jnp.int32, flat.shape, 0) % cols
    edge = 0 if step > 0 else cols - 1
    return jnp.where(place == edge, 0.0, rolled)


def kernel(
    frames, tiles,
    lat_hbm, gain_hbm, cb_hbm, tb_hbm, ub_hbm, cw_hbm, tw_hbm, uw_hbm,
    out_ref,
    lat, act, act_hist, act_relay, parts, part_in, blk, blk_hist, dbl,
    gain_ref, cb_ref, tb_ref, ub_ref, cw, tw, uw, umat, acc, mixed, edge, wide_lo, wide_hi,
    lat_sem, bias_sem, cw_sem, tw_sem, uw_sem,
    a_send, a_recv, a_fsend, r_send, r_recv, b_send, b_recv, b_fsend,
    p_down_sem, p_up_sem, b_down_sem, d_up_sem,
):
    rows, cols, chans = lat.shape
    outs_n = uw.shape[2]
    low = 128
    high = outs_n - low
    cells = rows * cols
    t = lax.axis_index("tm")
    s = lax.axis_index("tile")
    odd = lax.rem(t, 2) == 1
    even = jnp.logical_not(odd)
    has_next = t + 2 < frames
    has_prev = t >= 2
    has_near = t >= 1
    has_up = s > 0
    has_down = s < tiles - 1

    lat_copy = pltpu.make_async_copy(lat_hbm.at[0], lat, lat_sem)
    lat_copy.start()
    bias_copies = []
    for k, (src, dst) in enumerate(
        ((gain_hbm, gain_ref), (cb_hbm, cb_ref), (tb_hbm, tb_ref), (ub_hbm, ub_ref))
    ):
        copy = pltpu.make_async_copy(src, dst, bias_sem.at[k])
        copy.start()
        bias_copies.append(copy)
    cw_copies = {}
    for dt in (2, 0, 1):
        for dh in range(3):
            copy = pltpu.make_async_copy(
                cw_hbm.at[dt, dh],
                cw.at[dt, :, :, pl.ds(dh * chans, chans)],
                cw_sem.at[dt, dh],
            )
            copy.start()
            cw_copies[dt, dh] = copy
    tw_copy = pltpu.make_async_copy(tw_hbm, tw, tw_sem)
    tw_copy.start()
    uw_copy = pltpu.make_async_copy(uw_hbm, uw, uw_sem)
    uw_copy.start()

    half = frames // 2
    partner = s + 1 - 2 * lax.rem(s, 2)
    relays = t // 2 == half // 2 - 1
    relayed = t // 2 == half // 2
    direct = jnp.logical_and(has_next, jnp.logical_not(relays))

    sibling = t + 1 - 2 * lax.rem(t, 2)
    barrier = pltpu.get_barrier_semaphore()

    def greet(condition, where):
        @pl.when(condition)
        def _():
            pl.semaphore_signal(barrier, inc=1, device_id=where, device_id_type=MESH)

    pl.semaphore_signal(barrier, inc=1, device_id={"tm": sibling}, device_id_type=MESH)
    greet(has_next, {"tm": t + 2})
    greet(has_prev, {"tm": t - 2})
    greet(relays, {"tm": t + 2, "tile": partner})
    greet(relayed, {"tm": t - 2, "tile": partner})
    greet(has_up, {"tile": s - 1})
    greet(has_down, {"tile": s + 1})

    def history_copies(own, hist, send, recv, fsend):
        def nearer(r):
            return pltpu.make_async_remote_copy(
                own.at[r], hist.at[1, r], send.at[0, r], recv.at[1, r],
                device_id={"tm": sibling}, device_id_type=MESH,
            )

        def farther(r):
            return pltpu.make_async_remote_copy(
                own.at[r], hist.at[0, r], send.at[1, r], recv.at[0, r],
                device_id={"tm": t + 2}, device_id_type=MESH,
            )

        def forward(r):
            return pltpu.make_async_remote_copy(
                hist.at[0, r], hist.at[1, r], fsend.at[r], recv.at[1, r],
                device_id={"tm": sibling}, device_id_type=MESH,
            )

        return nearer, farther, forward

    def history_start(copies, r, sends=has_next):
        nearer, farther, _ = copies

        @pl.when(sends)
        def _():
            farther(r).start()

        @pl.when(even)
        def _():
            nearer(r).start()

    def history_far(copies, r):
        _, farther, forward = copies
        farther(r).wait_recv()

        @pl.when(odd)
        def _():
            forward(r).start()

    def history_near(copies, r):
        copies[0](r).wait_recv()

    def history_end(copies, r, sends=has_next):
        nearer, farther, forward = copies

        @pl.when(sends)
        def _():
            farther(r).wait_send()

        @pl.when(even)
        def _():
            nearer(r).wait_send()

        @pl.when(jnp.logical_and(odd, has_prev))
        def _():
            forward(r).wait_send()

    def to_tile(src, dst, sems, where):
        return pltpu.make_async_remote_copy(
            src, dst, sems.at[0], sems.at[1], device_id={"tile": where}, device_id_type=MESH
        )

    first, last = 0, rows - 1
    act_copies = history_copies(act, act_hist, a_send, a_recv, a_fsend)
    blk_copies = history_copies(blk, blk_hist, b_send, b_recv, b_fsend)
    part_down = to_tile(parts.at[1], part_in.at[0], p_down_sem, s + 1)
    part_up = to_tile(parts.at[0], part_in.at[1], p_up_sem, s - 1)
    blk_down = to_tile(blk.at[rows], blk.at[0], b_down_sem, s + 1)
    dbl_up = to_tile(dbl.at[1], dbl.at[rows + 1], d_up_sem, s - 1)

    def activate(r):
        values = lat[r].astype(F32)
        meansq = jnp.mean(values * values, axis=-1, keepdims=True)
        scaled = values * lax.rsqrt(meansq + 1e-06) * gain_ref[...].reshape(1, chans)
        act[r] = (scaled * jax.nn.sigmoid(scaled)).astype(BF16)

    peers = 1
    for condition in (has_next, has_prev, relays, relayed, has_up, has_down):
        peers = peers + condition.astype(jnp.int32)

    def to_partner(r):
        return pltpu.make_async_remote_copy(
            act.at[r], act_relay.at[r], r_send.at[0, r], r_recv.at[r],
            device_id={"tile": partner}, device_id_type=MESH,
        )

    def from_partner(r):
        return pltpu.make_async_remote_copy(
            act_relay.at[r], act_hist.at[0, r], r_send.at[1, r], a_recv.at[0, r],
            device_id={"tm": t + 2, "tile": partner}, device_id_type=MESH,
        )

    order = tuple(range(rows))[::-1]
    lat_copy.wait()
    for copy in bias_copies:
        copy.wait()
    for r in order:
        activate(r)
        if r == order[0]:
            pl.semaphore_wait(barrier, peers)
        if r == order[0]:
            history_start(act_copies, r)
        else:
            @pl.when(relays)
            def _():
                to_partner(r).start()

            history_start(act_copies, r, direct)

    def widen(frame):
        flat = frame.reshape(-1, chans)
        wide = flat.astype(F32)
        before = column_shift(wide, cols, 1).astype(BF16)
        after = column_shift(wide, cols, -1).astype(BF16)
        return jnp.concatenate([before, flat, after], axis=1)

    def conv(stacked, dt, start, size):
        taps = cw.at[dt, :, :, pl.ds(start, size)][...].reshape(3 * chans, size)
        return jnp.dot(stacked, taps, preferred_element_type=F32)

    def weights_ready(dt):
        for dh in range(3):
            cw_copies[dt, dh].wait()

    weights_ready(2)
    acc[...] = conv(widen(act[...]), 2, 0, 3 * chans)
    weights_ready(0)
    weights_ready(1)

    @pl.when(relays)
    def _():
        for r in order[1:]:
            to_partner(r).wait_recv()
            from_partner(r).start()

    for r in order:
        span = pl.ds(r * cols, cols)
        goes, stays = (0, chans) if r == last else (2 * chans, 0)
        out_part = 1 if r == last else 0

        @pl.when(has_prev)
        def _():
            history_far(act_copies, r)
            acc[span, :] += conv(widen(act_hist[0, r]), 0, 0, 3 * chans)

        @pl.when(has_near)
        def _():
            history_near(act_copies, r)
            acc[span, pl.ds(goes, chans)] += conv(widen(act_hist[1, r]), 1, goes, chans)

        parts[out_part] = acc[span, pl.ds(goes, chans)].astype(BF16)
        if r == last:
            @pl.when(has_down)
            def _():
                part_down.start()
        else:
            @pl.when(has_up)
            def _():
                part_up.start()

        @pl.when(has_near)
        def _():
            acc[span, pl.ds(stays, 2 * chans)] += conv(widen(act_hist[1, r]), 1, stays, 2 * chans)

    def finish_row(r):
        total = acc[pl.ds(r * cols, cols), pl.ds(chans, chans)]
        if r > 0:
            total = total + acc[pl.ds((r - 1) * cols, cols), pl.ds(0, chans)]
        if r < rows - 1:
            total = total + acc[pl.ds((r + 1) * cols, cols), pl.ds(2 * chans, chans)]
        total = total + cb_ref[...].reshape(1, chans) + lat[r].astype(F32)
        if r == first:
            total = total + part_in[0].astype(F32)
        if r == last:
            total = total + part_in[1].astype(F32)
        blk[1 + r] = total.astype(BF16)

    @pl.when(has_up)
    def _():
        part_down.wait_recv()

    @pl.when(jnp.logical_not(has_up))
    def _():
        part_in[0] = jnp.zeros((cols, chans), BF16)

    for r in range(rows - 1):
        finish_row(r)
        history_start(blk_copies, 1 + r)

    @pl.when(has_down)
    def _():
        part_up.wait_recv()

    @pl.when(jnp.logical_not(has_down))
    def _():
        part_in[1] = jnp.zeros((cols, chans), BF16)

    finish_row(last)

    @pl.when(has_down)
    def _():
        blk_down.start()

    history_start(blk_copies, rows)

    uw_copy.wait()
    row_sets = {(0, 0): (0,), (0, 1): (1, 2), (1, 0): (0, 1), (1, 1): (2,)}
    for (a, i), picks in row_sets.items():
        taps = []
        for kw in range(3):
            tap = uw[picks[0], kw].astype(F32)
            for kh in picks[1:]:
                tap = tap + uw[kh, kw].astype(F32)
            taps.append(tap)
        center = (taps[1] + taps[2], taps[0] + taps[1])
        sides = (taps[0], taps[2])
        lanes = pl.ds(i * chans, chans)
        for base, pair in ((0, center), (2 * outs_n, sides)):
            for b in range(2):
                value = pair[b].astype(BF16)
                umat[a, pl.ds(base + b * low, low), lanes] = value[:low]
                umat[a, pl.ds(base + 2 * low + b * high, high), lanes] = value[low:]

    tw_copy.wait()

    def mix(row, k):
        return jnp.dot(row, tw[k], preferred_element_type=F32)

    def newest(j):
        mixed[j] = mix(blk[j], 2) + tb_ref[...].reshape(1, 2 * chans)

    def mix_row(j):
        @pl.when(has_prev)
        def _():
            history_far(blk_copies, j)
            mixed[j] += mix(blk_hist[0, j], 0)

        @pl.when(has_near)
        def _():
            history_near(blk_copies, j)
            mixed[j] += mix(blk_hist[1, j], 1)

        for f in range(2):
            dbl[j, f] = mixed[j, :, pl.ds(f * chans, chans)].astype(BF16)

    for r in range(rows):
        newest(1 + r)
    for r in range(rows):
        if r == last:
            @pl.when(has_up)
            def _():
                blk_down.wait_recv()
                history_start(blk_copies, 0)

        mix_row(1 + r)
        if r == first:
            @pl.when(has_up)
            def _():
                dbl_up.start()

    bias_row = ub_ref[...].reshape(1, outs_n)
    up_bias = jnp.concatenate(
        [bias_row[:, :low], bias_row[:, :low], bias_row[:, low:], bias_row[:, low:]], axis=1
    )

    def taps_dot(row, a, start, size):
        return lax.dot_general(
            row, umat[a, :, pl.ds(start, size)], (((1,), (1,)), ((), ())), preferred_element_type=F32
        )

    def stored_row(j):
        return dbl[j].reshape(2 * cols, chans)

    def upsample_row(a, r, result):
        center = result[:, : 2 * outs_n] + up_bias
        sides = result[:, 2 * outs_n :]
        even = center[:, :low] + column_shift(sides[:, :low], cols, 1)
        uneven = center[:, low : 2 * low] + column_shift(sides[:, low : 2 * low], cols, -1)
        tail = sides[:, 2 * low :]
        lane = lax.broadcasted_iota(jnp.int32, tail.shape, 1)
        tail = center[:, 2 * low :] + jnp.where(
            lane < high, column_shift(tail, cols, 1), column_shift(tail, cols, -1)
        )
        swapped = pltpu.roll(tail, high, 1)
        for f in range(2):
            span = slice(f * cols, (f + 1) * cols)
            wide_lo[pl.ds(0, cols, stride=2), :] = even[span]
            wide_lo[pl.ds(1, cols, stride=2), :] = uneven[span]
            wide_hi[pl.ds(0, cols, stride=2), :] = tail[span]
            wide_hi[pl.ds(1, cols, stride=2), :] = swapped[span]
            out_ref[f, 2 * r + a, pl.ds(0, low), :] = wide_lo[...].T.astype(BF16)
            out_ref[f, 2 * r + a, pl.ds(low, high), :] = wide_hi[...].T[:high].astype(BF16)

    for r in range(rows):
        for a in range(2):
            if 0 < r + a < rows:
                both = jnp.concatenate([stored_row(r + a), stored_row(r + a + 1)], axis=1)
                upsample_row(a, r, taps_dot(both, a, 0, 2 * chans))

    edge[0] = taps_dot(stored_row(1), 0, chans, chans)
    edge[1] = taps_dot(stored_row(rows), 1, 0, chans)

    @pl.when(has_up)
    def _():
        newest(0)
        mix_row(0)
        edge[0] += taps_dot(stored_row(0), 0, 0, chans)

    upsample_row(0, 0, edge[0])

    @pl.when(has_down)
    def _():
        dbl_up.wait_recv()
        edge[1] += taps_dot(stored_row(rows + 1), 1, chans, chans)

    upsample_row(1, last, edge[1])

    for r in range(rows):
        history_end(act_copies, r, has_next if r == order[0] else direct)
        history_end(blk_copies, 1 + r)

    @pl.when(relays)
    def _():
        for r in order[1:]:
            to_partner(r).wait_send()
            from_partner(r).wait_send()

    @pl.when(has_up)
    def _():
        history_end(blk_copies, 0)
        part_up.wait_send()
        dbl_up.wait_send()

    @pl.when(has_down)
    def _():
        part_down.wait_send()
        blk_down.wait_send()


def local(frames, tiles, latent, gain, conv_weight, conv_bias, time_weight, time_bias, up_weight, up_bias):
    _, rows, cols, chans = latent.shape
    outs_n = up_weight.shape[3]
    low = 128
    dma = pltpu.SemaphoreType.DMA
    row = (cols, chans)
    transposed = pl.pallas_call(
        functools.partial(kernel, frames, tiles),
        out_shape=jax.ShapeDtypeStruct((2, 2 * rows, outs_n, 2 * cols), BF16),
        in_specs=[pl.BlockSpec(memory_space=pltpu.HBM)] * 8,
        out_specs=pl.BlockSpec(memory_space=pltpu.VMEM),
        scratch_shapes=[
            pltpu.VMEM((rows,) + row, BF16),
            pltpu.VMEM((rows,) + row, BF16),
            pltpu.VMEM((2, rows) + row, BF16),
            pltpu.VMEM((rows,) + row, BF16),
            pltpu.VMEM((2,) + row, BF16),
            pltpu.VMEM((2,) + row, BF16),
            pltpu.VMEM((rows + 1,) + row, BF16),
            pltpu.VMEM((2, rows + 1) + row, BF16),
            pltpu.VMEM((rows + 2, 2) + row, BF16),
            pltpu.VMEM((chans,), F32),
            pltpu.VMEM((chans,), F32),
            pltpu.VMEM((2 * chans,), F32),
            pltpu.VMEM((outs_n,), F32),
            pltpu.VMEM((3, 3, chans, 3 * chans), BF16),
            pltpu.VMEM((3, chans, 2 * chans), BF16),
            pltpu.VMEM((3, 3, outs_n, chans), BF16),
            pltpu.VMEM((2, 4 * outs_n, 2 * chans), BF16),
            pltpu.VMEM((rows * cols, 3 * chans), F32),
            pltpu.VMEM((rows + 1, cols, 2 * chans), F32),
            pltpu.VMEM((2, 2 * cols, 4 * outs_n), F32),
            pltpu.VMEM((2 * cols, low), F32),
            pltpu.VMEM((2 * cols, low), F32),
            dma(()), dma((4,)), dma((3, 3)), dma(()), dma(()),
            dma((2, rows)), dma((2, rows)), dma((rows,)),
            dma((2, rows)), dma((rows,)),
            dma((2, rows + 1)), dma((2, rows + 1)), dma((rows + 1,)),
            dma((2,)), dma((2,)), dma((2,)), dma((2,)),
        ],
        compiler_params=pltpu.CompilerParams(
            collective_id=0, has_side_effects=True, vmem_limit_bytes=48 * 1024 * 1024
        ),
    )(*(
        pltpu.with_memory_space_constraint(array, pltpu.HBM)
        for array in (
            latent, gain, conv_bias, time_bias, up_bias,
            conv_weight, time_weight, jnp.swapaxes(up_weight, 2, 3),
        )
    ))
    return jnp.swapaxes(transposed, 2, 3)


def solution(mesh):
    placed = (P("tm", "tile", None, None), P(), P(), P(), P(), P(), P(), P())
    return jax.shard_map(
        functools.partial(local, mesh.shape["tm"], mesh.shape["tile"]),
        mesh=mesh, in_specs=placed, out_specs=P("tm", "tile", None, None), check_vma=False,
    )
```

```python
import functools

import jax
import jax.numpy as jnp
from jax import lax
from jax.experimental import pallas as pl
from jax.experimental.pallas import tpu as pltpu
from jax.sharding import PartitionSpec as P

F32 = jnp.float32
BF16 = jnp.bfloat16
MESH = pl.DeviceIdType.MESH


def column_shift(flat, cols, step):
    total = flat.shape[0]
    rolled = pltpu.roll(flat, step % total, 0)
    place = lax.broadcasted_iota(jnp.int32, flat.shape, 0) % cols
    edge = 0 if step > 0 else cols - 1
    return jnp.where(place == edge, 0.0, rolled)


def kernel(
    frames, tiles,
    lat_hbm, gain_hbm, cb_hbm, tb_hbm, ub_hbm, cw_hbm, tw_hbm, uw_hbm,
    out_ref,
    lat, act, act_hist, act_relay, parts, part_in, blk, blk_hist, dbl,
    gain_ref, cb_ref, tb_ref, ub_ref, cw, tw, uw, umat, acc, mixed, edge, wide_lo, wide_hi,
    lat_sem, bias_sem, cw_sem, tw_sem, uw_sem,
    a_send, a_recv, a_fsend, r_send, r_recv, b_send, b_recv, b_fsend,
    p_down_sem, p_up_sem, b_down_sem, d_up_sem,
):
    rows, cols, chans = lat.shape
    outs_n = uw.shape[2]
    low = 128
    high = outs_n - low
    cells = rows * cols
    middle = cols // 2
    margin = 16
    t = lax.axis_index("tm")
    s = lax.axis_index("tile")
    odd = lax.rem(t, 2) == 1
    even = jnp.logical_not(odd)
    has_next = t + 2 < frames
    has_prev = t >= 2
    has_near = t >= 1
    has_up = s > 0
    has_down = s < tiles - 1

    lat_copy = pltpu.make_async_copy(lat_hbm.at[0], lat, lat_sem)
    lat_copy.start()
    bias_copies = []
    for k, (src, dst) in enumerate(
        ((gain_hbm, gain_ref), (cb_hbm, cb_ref), (tb_hbm, tb_ref), (ub_hbm, ub_ref))
    ):
        copy = pltpu.make_async_copy(src, dst, bias_sem.at[k])
        copy.start()
        bias_copies.append(copy)
    cw_copies = {}
    for dt in (2, 0, 1):
        for dh in range(3):
            copy = pltpu.make_async_copy(
                cw_hbm.at[dt, dh],
                cw.at[dt, :, :, pl.ds(dh * chans, chans)],
                cw_sem.at[dt, dh],
            )
            copy.start()
            cw_copies[dt, dh] = copy
    tw_copy = pltpu.make_async_copy(tw_hbm, tw, tw_sem)
    tw_copy.start()
    uw_copy = pltpu.make_async_copy(uw_hbm, uw, uw_sem)
    uw_copy.start()

    half = frames // 2
    partner = s + 1 - 2 * lax.rem(s, 2)
    relays = t // 2 == half // 2 - 1
    relayed = t // 2 == half // 2
    direct = jnp.logical_and(has_next, jnp.logical_not(relays))

    sibling = t + 1 - 2 * lax.rem(t, 2)
    barrier = pltpu.get_barrier_semaphore()

    def greet(condition, where):
        @pl.when(condition)
        def _():
            pl.semaphore_signal(barrier, inc=1, device_id=where, device_id_type=MESH)

    pl.semaphore_signal(barrier, inc=1, device_id={"tm": sibling}, device_id_type=MESH)
    greet(has_next, {"tm": t + 2})
    greet(has_prev, {"tm": t - 2})
    greet(relays, {"tm": t + 2, "tile": partner})
    greet(relayed, {"tm": t - 2, "tile": partner})
    greet(has_up, {"tile": s - 1})
    greet(has_down, {"tile": s + 1})

    def piece(k):
        r, right = divmod(k, 2)
        start, size = (middle + margin, middle - margin) if right else (0, middle + margin)
        return (r, pl.ds(start, size))

    def history_copies(own, hist, send, recv, fsend, at=lambda k: (k,)):
        def nearer(k):
            return pltpu.make_async_remote_copy(
                own.at[at(k)], hist.at[(1,) + at(k)], send.at[0, k], recv.at[1, k],
                device_id={"tm": sibling}, device_id_type=MESH,
            )

        def farther(k):
            return pltpu.make_async_remote_copy(
                own.at[at(k)], hist.at[(0,) + at(k)], send.at[1, k], recv.at[0, k],
                device_id={"tm": t + 2}, device_id_type=MESH,
            )

        def forward(k):
            return pltpu.make_async_remote_copy(
                hist.at[(0,) + at(k)], hist.at[(1,) + at(k)], fsend.at[k], recv.at[1, k],
                device_id={"tm": sibling}, device_id_type=MESH,
            )

        return nearer, farther, forward

    def history_start(copies, r, sends=has_next):
        nearer, farther, _ = copies

        @pl.when(sends)
        def _():
            farther(r).start()

        @pl.when(even)
        def _():
            nearer(r).start()

    def history_far(copies, r):
        _, farther, forward = copies
        farther(r).wait_recv()

        @pl.when(odd)
        def _():
            forward(r).start()

    def history_near(copies, r):
        copies[0](r).wait_recv()

    def history_end(copies, r, sends=has_next):
        nearer, farther, forward = copies

        @pl.when(sends)
        def _():
            farther(r).wait_send()

        @pl.when(even)
        def _():
            nearer(r).wait_send()

        @pl.when(jnp.logical_and(odd, has_prev))
        def _():
            forward(r).wait_send()

    def to_tile(src, dst, sems, where):
        return pltpu.make_async_remote_copy(
            src, dst, sems.at[0], sems.at[1], device_id={"tile": where}, device_id_type=MESH
        )

    first, last = 0, rows - 1
    act_copies = history_copies(act, act_hist, a_send, a_recv, a_fsend, piece)
    blk_copies = history_copies(blk, blk_hist, b_send, b_recv, b_fsend)
    half_row = [pl.ds(0, middle), pl.ds(middle, middle)]
    part_down = [
        to_tile(parts.at[1, w], part_in.at[0, w], p_down_sem.at[h], s + 1) for h, w in enumerate(half_row)
    ]
    part_up = [
        to_tile(parts.at[0, w], part_in.at[1, w], p_up_sem.at[h], s - 1) for h, w in enumerate(half_row)
    ]
    blk_down = to_tile(blk.at[rows], blk.at[0], b_down_sem, s + 1)
    dbl_up = to_tile(dbl.at[1], dbl.at[rows + 1], d_up_sem, s - 1)

    def activate(r):
        values = lat[r].astype(F32)
        meansq = jnp.mean(values * values, axis=-1, keepdims=True)
        scaled = values * lax.rsqrt(meansq + 1e-06) * gain_ref[...].reshape(1, chans)
        act[r] = (scaled * jax.nn.sigmoid(scaled)).astype(BF16)

    peers = 1
    for condition in (has_next, has_prev, relays, relayed, has_up, has_down):
        peers = peers + condition.astype(jnp.int32)

    def to_partner(k):
        return pltpu.make_async_remote_copy(
            act.at[piece(k)], act_relay.at[piece(k)], r_send.at[0, k], r_recv.at[k],
            device_id={"tile": partner}, device_id_type=MESH,
        )

    def from_partner(k):
        return pltpu.make_async_remote_copy(
            act_relay.at[piece(k)], act_hist.at[(0,) + piece(k)], r_send.at[1, k], a_recv.at[0, k],
            device_id={"tm": t + 2, "tile": partner}, device_id_type=MESH,
        )

    order = tuple(range(rows))[::-1]
    near_pieces = (2 * last, 2 * last + 1)
    relay_pieces = tuple(2 * r + h for r in order[1:] for h in range(2))
    lat_copy.wait()
    for copy in bias_copies:
        copy.wait()
    for r in order:
        activate(r)
        if r == last:
            pl.semaphore_wait(barrier, peers)
            for k in near_pieces:
                history_start(act_copies, k)
        else:
            for k in (2 * r, 2 * r + 1):
                @pl.when(relays)
                def _():
                    to_partner(k).start()

                history_start(act_copies, k, direct)

    def widen(flat):
        wide = flat.astype(F32)
        size = flat.shape[0]
        run = min(size, cols)
        before = column_shift(wide, run, 1).astype(BF16)
        after = column_shift(wide, run, -1).astype(BF16)
        return jnp.concatenate([before, flat, after], axis=1)

    def widen_half(slot, r, h):
        if h == 0:
            return widen(act_hist[slot, r, pl.ds(0, middle + margin)])[:middle]
        return widen(act_hist[slot, r, pl.ds(middle - margin, middle + margin)])[margin:]

    def conv(stacked, dt, start, size):
        taps = cw.at[dt, :, :, pl.ds(start, size)][...].reshape(3 * chans, size)
        return jnp.dot(stacked, taps, preferred_element_type=F32)

    def weights_ready(dt):
        for dh in range(3):
            cw_copies[dt, dh].wait()

    weights_ready(2)
    acc[...] = conv(widen(act[...].reshape(cells, chans)), 2, 0, 3 * chans)

    @pl.when(relays)
    def _():
        for k in relay_pieces:
            to_partner(k).wait_recv()
            from_partner(k).start()

    uw_copy.wait()
    row_sets = {(0, 0): (0,), (0, 1): (1, 2), (1, 0): (0, 1), (1, 1): (2,)}
    for (a, i), picks in row_sets.items():
        taps = []
        for kw in range(3):
            tap = uw[picks[0], kw].astype(F32)
            for kh in picks[1:]:
                tap = tap + uw[kh, kw].astype(F32)
            taps.append(tap)
        center = (taps[1] + taps[2], taps[0] + taps[1])
        sides = (taps[0], taps[2])
        lanes = pl.ds(i * chans, chans)
        for base, pair in ((0, center), (2 * outs_n, sides)):
            for b in range(2):
                value = pair[b].astype(BF16)
                umat[a, pl.ds(base + b * low, low), lanes] = value[:low]
                umat[a, pl.ds(base + 2 * low + b * high, high), lanes] = value[low:]

    weights_ready(0)
    weights_ready(1)
    for r in order:
        goes, stays = (0, chans) if r == last else (2 * chans, 0)
        out_part = 1 if r == last else 0
        for h in range(2):
            k = 2 * r + h
            span = pl.ds(r * cols + h * middle, middle)

            @pl.when(has_prev)
            def _():
                history_far(act_copies, k)
                acc[span, :] += conv(widen_half(0, r, h), 0, 0, 3 * chans)

            @pl.when(has_near)
            def _():
                history_near(act_copies, k)
                acc[span, pl.ds(goes, chans)] += conv(widen_half(1, r, h), 1, goes, chans)

            parts[out_part, half_row[h]] = acc[span, pl.ds(goes, chans)].astype(BF16)
            if r == last:
                @pl.when(has_down)
                def _():
                    part_down[h].start()
            else:
                @pl.when(has_up)
                def _():
                    part_up[h].start()

            @pl.when(has_near)
            def _():
                acc[span, pl.ds(stays, 2 * chans)] += conv(widen_half(1, r, h), 1, stays, 2 * chans)

    def finish_row(r):
        total = acc[pl.ds(r * cols, cols), pl.ds(chans, chans)]
        if r > 0:
            total = total + acc[pl.ds((r - 1) * cols, cols), pl.ds(0, chans)]
        if r < rows - 1:
            total = total + acc[pl.ds((r + 1) * cols, cols), pl.ds(2 * chans, chans)]
        total = total + cb_ref[...].reshape(1, chans) + lat[r].astype(F32)
        if r == first:
            total = total + part_in[0].astype(F32)
        if r == last:
            total = total + part_in[1].astype(F32)
        blk[1 + r] = total.astype(BF16)

    tw_copy.wait()

    def mix(row, k):
        return jnp.dot(row, tw[k], preferred_element_type=F32)

    def newest(j):
        mixed[j] = mix(blk[j], 2) + tb_ref[...].reshape(1, 2 * chans)

    def mix_row(j):
        @pl.when(has_prev)
        def _():
            history_far(blk_copies, j)
            mixed[j] += mix(blk_hist[0, j], 0)

        @pl.when(has_near)
        def _():
            history_near(blk_copies, j)
            mixed[j] += mix(blk_hist[1, j], 1)

        for f in range(2):
            dbl[j, f] = mixed[j, :, pl.ds(f * chans, chans)].astype(BF16)

    @pl.when(has_up)
    def _():
        for copy in part_down:
            copy.wait_recv()

    @pl.when(jnp.logical_not(has_up))
    def _():
        part_in[0] = jnp.zeros((cols, chans), BF16)

    for r in range(rows - 1):
        finish_row(r)
        history_start(blk_copies, 1 + r)
        newest(1 + r)

    @pl.when(has_down)
    def _():
        for copy in part_up:
            copy.wait_recv()

    @pl.when(jnp.logical_not(has_down))
    def _():
        part_in[1] = jnp.zeros((cols, chans), BF16)

    finish_row(last)

    @pl.when(has_down)
    def _():
        blk_down.start()

    history_start(blk_copies, rows)
    newest(rows)

    for r in range(rows):
        if r == last:
            @pl.when(has_up)
            def _():
                blk_down.wait_recv()
                history_start(blk_copies, 0)

        mix_row(1 + r)
        if r == first:
            @pl.when(has_up)
            def _():
                dbl_up.start()

    bias_row = ub_ref[...].reshape(1, outs_n)
    up_bias = jnp.concatenate(
        [bias_row[:, :low], bias_row[:, :low], bias_row[:, low:], bias_row[:, low:]], axis=1
    )

    def taps_dot(row, a, start, size):
        return lax.dot_general(
            row, umat[a, :, pl.ds(start, size)], (((1,), (1,)), ((), ())), preferred_element_type=F32
        )

    def stored_row(j):
        return dbl[j].reshape(2 * cols, chans)

    def upsample_row(a, r, result):
        center = result[:, : 2 * outs_n] + up_bias
        sides = result[:, 2 * outs_n :]
        even = center[:, :low] + column_shift(sides[:, :low], cols, 1)
        uneven = center[:, low : 2 * low] + column_shift(sides[:, low : 2 * low], cols, -1)
        tail = sides[:, 2 * low :]
        lane = lax.broadcasted_iota(jnp.int32, tail.shape, 1)
        tail = center[:, 2 * low :] + jnp.where(
            lane < high, column_shift(tail, cols, 1), column_shift(tail, cols, -1)
        )
        swapped = pltpu.roll(tail, high, 1)
        for f in range(2):
            span = slice(f * cols, (f + 1) * cols)
            wide_lo[pl.ds(0, cols, stride=2), :] = even[span]
            wide_lo[pl.ds(1, cols, stride=2), :] = uneven[span]
            wide_hi[pl.ds(0, cols, stride=2), :] = tail[span]
            wide_hi[pl.ds(1, cols, stride=2), :] = swapped[span]
            out_ref[f, 2 * r + a, pl.ds(0, low), :] = wide_lo[...].T.astype(BF16)
            out_ref[f, 2 * r + a, pl.ds(low, high), :] = wide_hi[...].T[:high].astype(BF16)

    for r in range(rows):
        for a in range(2):
            if 0 < r + a < rows:
                both = jnp.concatenate([stored_row(r + a), stored_row(r + a + 1)], axis=1)
                upsample_row(a, r, taps_dot(both, a, 0, 2 * chans))

    edge[0] = taps_dot(stored_row(1), 0, chans, chans)
    edge[1] = taps_dot(stored_row(rows), 1, 0, chans)

    @pl.when(has_up)
    def _():
        newest(0)
        mix_row(0)
        edge[0] += taps_dot(stored_row(0), 0, 0, chans)

    upsample_row(0, 0, edge[0])

    @pl.when(has_down)
    def _():
        dbl_up.wait_recv()
        edge[1] += taps_dot(stored_row(rows + 1), 1, chans, chans)

    upsample_row(1, last, edge[1])

    for r in range(rows):
        for k in (2 * r, 2 * r + 1):
            history_end(act_copies, k, has_next if k in near_pieces else direct)
        history_end(blk_copies, 1 + r)

    @pl.when(relays)
    def _():
        for k in relay_pieces:
            to_partner(k).wait_send()
            from_partner(k).wait_send()

    @pl.when(has_up)
    def _():
        history_end(blk_copies, 0)
        for copy in part_up:
            copy.wait_send()
        dbl_up.wait_send()

    @pl.when(has_down)
    def _():
        for copy in part_down:
            copy.wait_send()
        blk_down.wait_send()


def local(frames, tiles, latent, gain, conv_weight, conv_bias, time_weight, time_bias, up_weight, up_bias):
    _, rows, cols, chans = latent.shape
    outs_n = up_weight.shape[3]
    low = 128
    dma = pltpu.SemaphoreType.DMA
    row = (cols, chans)
    transposed = pl.pallas_call(
        functools.partial(kernel, frames, tiles),
        out_shape=jax.ShapeDtypeStruct((2, 2 * rows, outs_n, 2 * cols), BF16),
        in_specs=[pl.BlockSpec(memory_space=pltpu.HBM)] * 8,
        out_specs=pl.BlockSpec(memory_space=pltpu.VMEM),
        scratch_shapes=[
            pltpu.VMEM((rows,) + row, BF16),
            pltpu.VMEM((rows,) + row, BF16),
            pltpu.VMEM((2, rows) + row, BF16),
            pltpu.VMEM((rows,) + row, BF16),
            pltpu.VMEM((2,) + row, BF16),
            pltpu.VMEM((2,) + row, BF16),
            pltpu.VMEM((rows + 1,) + row, BF16),
            pltpu.VMEM((2, rows + 1) + row, BF16),
            pltpu.VMEM((rows + 2, 2) + row, BF16),
            pltpu.VMEM((chans,), F32),
            pltpu.VMEM((chans,), F32),
            pltpu.VMEM((2 * chans,), F32),
            pltpu.VMEM((outs_n,), F32),
            pltpu.VMEM((3, 3, chans, 3 * chans), BF16),
            pltpu.VMEM((3, chans, 2 * chans), BF16),
            pltpu.VMEM((3, 3, outs_n, chans), BF16),
            pltpu.VMEM((2, 4 * outs_n, 2 * chans), BF16),
            pltpu.VMEM((rows * cols, 3 * chans), F32),
            pltpu.VMEM((rows + 1, cols, 2 * chans), F32),
            pltpu.VMEM((2, 2 * cols, 4 * outs_n), F32),
            pltpu.VMEM((2 * cols, low), F32),
            pltpu.VMEM((2 * cols, low), F32),
            dma(()), dma((4,)), dma((3, 3)), dma(()), dma(()),
            dma((2, 2 * rows)), dma((2, 2 * rows)), dma((2 * rows,)),
            dma((2, 2 * rows)), dma((2 * rows,)),
            dma((2, rows + 1)), dma((2, rows + 1)), dma((rows + 1,)),
            dma((2, 2)), dma((2, 2)), dma((2,)), dma((2,)),
        ],
        compiler_params=pltpu.CompilerParams(
            collective_id=0, has_side_effects=True, vmem_limit_bytes=48 * 1024 * 1024
        ),
    )(*(
        pltpu.with_memory_space_constraint(array, pltpu.HBM)
        for array in (
            latent, gain, conv_bias, time_bias, up_bias,
            conv_weight, time_weight, jnp.swapaxes(up_weight, 2, 3),
        )
    ))
    return jnp.swapaxes(transposed, 2, 3)


def solution(mesh):
    placed = (P("tm", "tile", None, None), P(), P(), P(), P(), P(), P(), P())
    return jax.shard_map(
        functools.partial(local, mesh.shape["tm"], mesh.shape["tile"]),
        mesh=mesh, in_specs=placed, out_specs=P("tm", "tile", None, None), check_vma=False,
    )
```

```python
import functools

import jax
import jax.numpy as jnp
from jax import lax
from jax.experimental import pallas as pl
from jax.experimental.pallas import tpu as pltpu
from jax.sharding import PartitionSpec as P

F32 = jnp.float32
BF16 = jnp.bfloat16
MESH = pl.DeviceIdType.MESH


def column_shift(flat, cols, step):
    total = flat.shape[0]
    rolled = pltpu.roll(flat, step % total, 0)
    place = lax.broadcasted_iota(jnp.int32, flat.shape, 0) % cols
    edge = 0 if step > 0 else cols - 1
    return jnp.where(place == edge, 0.0, rolled)


def kernel(
    frames, tiles,
    lat_hbm, gain_hbm, cb_hbm, tb_hbm, ub_hbm, cw_hbm, tw_hbm, uw_hbm,
    out_ref,
    lat, act, act_hist, act_relay, parts, part_in, blk, blk_hist, blk_relay, dbl,
    gain_ref, cb_ref, tb_ref, ub_ref, cw, tw, uw, umat, acc, mixed, edge, wide_lo, wide_hi,
    lat_sem, bias_sem, cw_sem, tw_sem, uw_sem,
    a_send, a_recv, a_fsend, r_send, r_recv, b_send, b_recv, b_fsend,
    p_down_sem, p_up_sem, b_down_sem, b_up_sem, d_up_sem, q_sem,
):
    rows, cols, chans = lat.shape
    outs_n = uw.shape[2]
    low = 128
    high = outs_n - low
    cells = rows * cols
    t = lax.axis_index("tm")
    s = lax.axis_index("tile")
    odd = lax.rem(t, 2) == 1
    even = jnp.logical_not(odd)
    has_next = t + 2 < frames
    has_prev = t >= 2
    has_near = t >= 1
    starts = t < 2
    later = t >= 2
    has_up = s > 0
    has_down = s < tiles - 1

    lat_copy = pltpu.make_async_copy(lat_hbm.at[0], lat, lat_sem)
    lat_copy.start()
    bias_copies = []
    for k, (src, dst) in enumerate(
        ((gain_hbm, gain_ref), (cb_hbm, cb_ref), (tb_hbm, tb_ref), (ub_hbm, ub_ref))
    ):
        copy = pltpu.make_async_copy(src, dst, bias_sem.at[k])
        copy.start()
        bias_copies.append(copy)
    cw_copies = {}
    for dt in (2, 0, 1):
        for dh in range(3):
            copy = pltpu.make_async_copy(
                cw_hbm.at[dt, dh],
                cw.at[dt, :, :, pl.ds(dh * chans, chans)],
                cw_sem.at[dt, dh],
            )
            copy.start()
            cw_copies[dt, dh] = copy
    tw_copy = pltpu.make_async_copy(tw_hbm, tw, tw_sem)
    tw_copy.start()
    uw_copy = pltpu.make_async_copy(uw_hbm, uw, uw_sem)
    uw_copy.start()

    half = frames // 2
    partner = s + 1 - 2 * lax.rem(s, 2)
    relays = t // 2 == half // 2 - 1
    relayed = t // 2 == half // 2
    direct = jnp.logical_and(has_next, jnp.logical_not(relays))

    sibling = t + 1 - 2 * lax.rem(t, 2)
    barrier = pltpu.get_barrier_semaphore()

    def greet(condition, where):
        @pl.when(condition)
        def _():
            pl.semaphore_signal(barrier, inc=1, device_id=where, device_id_type=MESH)

    pl.semaphore_signal(barrier, inc=1, device_id={"tm": sibling}, device_id_type=MESH)
    greet(has_next, {"tm": t + 2})
    greet(has_prev, {"tm": t - 2})
    greet(relays, {"tm": t + 2, "tile": partner})
    greet(relayed, {"tm": t - 2, "tile": partner})
    greet(has_up, {"tile": s - 1})
    greet(has_down, {"tile": s + 1})

    def history_copies(own, hist, send, recv, fsend):
        def nearer(r):
            return pltpu.make_async_remote_copy(
                own.at[r], hist.at[1, r], send.at[0, r], recv.at[1, r],
                device_id={"tm": sibling}, device_id_type=MESH,
            )

        def farther(r):
            return pltpu.make_async_remote_copy(
                own.at[r], hist.at[0, r], send.at[1, r], recv.at[0, r],
                device_id={"tm": t + 2}, device_id_type=MESH,
            )

        def forward(r):
            return pltpu.make_async_remote_copy(
                hist.at[0, r], hist.at[1, r], fsend.at[r], recv.at[1, r],
                device_id={"tm": sibling}, device_id_type=MESH,
            )

        return nearer, farther, forward

    def history_start(copies, r, sends=has_next):
        nearer, farther, _ = copies

        @pl.when(sends)
        def _():
            farther(r).start()

        @pl.when(even)
        def _():
            nearer(r).start()

    def history_far(copies, r):
        _, farther, forward = copies
        farther(r).wait_recv()

        @pl.when(odd)
        def _():
            forward(r).start()

    def history_near(copies, r):
        copies[0](r).wait_recv()

    def history_end(copies, r, sends=has_next):
        nearer, farther, forward = copies

        @pl.when(sends)
        def _():
            farther(r).wait_send()

        @pl.when(even)
        def _():
            nearer(r).wait_send()

        @pl.when(jnp.logical_and(odd, has_prev))
        def _():
            forward(r).wait_send()

    def to_tile(src, dst, sems, where):
        return pltpu.make_async_remote_copy(
            src, dst, sems.at[0], sems.at[1], device_id={"tile": where}, device_id_type=MESH
        )

    first, last = 0, rows - 1
    act_copies = history_copies(act, act_hist, a_send, a_recv, a_fsend)
    blk_copies = history_copies(blk, blk_hist, b_send, b_recv, b_fsend)
    part_down = to_tile(parts.at[1], part_in.at[0], p_down_sem, s + 1)
    part_up = to_tile(parts.at[0], part_in.at[1], p_up_sem, s - 1)
    blk_down = to_tile(blk.at[rows], blk.at[0], b_down_sem, s + 1)
    blk_up = to_tile(blk.at[1], blk.at[rows + 1], b_up_sem, s - 1)
    dbl_up = to_tile(dbl.at[1], dbl.at[rows + 1], d_up_sem, s - 1)

    def activate(r):
        values = lat[r].astype(F32)
        meansq = jnp.mean(values * values, axis=-1, keepdims=True)
        scaled = values * lax.rsqrt(meansq + 1e-06) * gain_ref[...].reshape(1, chans)
        act[r] = (scaled * jax.nn.sigmoid(scaled)).astype(BF16)

    peers = 1
    for condition in (has_next, has_prev, relays, relayed, has_up, has_down):
        peers = peers + condition.astype(jnp.int32)

    def to_partner(r):
        return pltpu.make_async_remote_copy(
            act.at[r], act_relay.at[r], r_send.at[0, r], r_recv.at[r],
            device_id={"tile": partner}, device_id_type=MESH,
        )

    def from_partner(r):
        return pltpu.make_async_remote_copy(
            act_relay.at[r], act_hist.at[0, r], r_send.at[1, r], a_recv.at[0, r],
            device_id={"tm": t + 2, "tile": partner}, device_id_type=MESH,
        )

    blk_to_partner = pltpu.make_async_remote_copy(
        blk.at[rows], blk_relay, q_sem.at[0], q_sem.at[1], device_id={"tile": partner}, device_id_type=MESH
    )
    blk_from_partner = pltpu.make_async_remote_copy(
        blk_relay, blk_hist.at[0, rows], q_sem.at[2], b_recv.at[0, rows],
        device_id={"tm": t + 2, "tile": partner}, device_id_type=MESH,
    )

    order = tuple(range(rows))[::-1]
    lat_copy.wait()
    for copy in bias_copies:
        copy.wait()
    for r in order:
        activate(r)
        if r == order[0]:
            pl.semaphore_wait(barrier, peers)
        if r == order[0]:
            history_start(act_copies, r)
        else:
            @pl.when(relays)
            def _():
                to_partner(r).start()

            history_start(act_copies, r, direct)

    def widen(frame):
        flat = frame.reshape(-1, chans)
        wide = flat.astype(F32)
        before = column_shift(wide, cols, 1).astype(BF16)
        after = column_shift(wide, cols, -1).astype(BF16)
        return jnp.concatenate([before, flat, after], axis=1)

    def conv(stacked, dt, start, size):
        taps = cw.at[dt, :, :, pl.ds(start, size)][...].reshape(3 * chans, size)
        return jnp.dot(stacked, taps, preferred_element_type=F32)

    def weights_ready(dt):
        for dh in range(3):
            cw_copies[dt, dh].wait()

    weights_ready(2)
    acc[...] = conv(widen(act[...]), 2, 0, 3 * chans)
    @pl.when(relays)
    def _():
        for r in order[1:]:
            to_partner(r).wait_recv()
            from_partner(r).start()

    uw_copy.wait()
    row_sets = {(0, 0): (0,), (0, 1): (1, 2), (1, 0): (0, 1), (1, 1): (2,)}
    for (a, i), picks in row_sets.items():
        taps = []
        for kw in range(3):
            tap = uw[picks[0], kw].astype(F32)
            for kh in picks[1:]:
                tap = tap + uw[kh, kw].astype(F32)
            taps.append(tap)
        center = (taps[1] + taps[2], taps[0] + taps[1])
        sides = (taps[0], taps[2])
        lanes = pl.ds(i * chans, chans)
        for base, pair in ((0, center), (2 * outs_n, sides)):
            for b in range(2):
                value = pair[b].astype(BF16)
                umat[a, pl.ds(base + b * low, low), lanes] = value[:low]
                umat[a, pl.ds(base + 2 * low + b * high, high), lanes] = value[low:]

    weights_ready(0)
    weights_ready(1)
    for r in order:
        span = pl.ds(r * cols, cols)
        goes, stays = (0, chans) if r == last else (2 * chans, 0)
        out_part = 1 if r == last else 0

        @pl.when(has_prev)
        def _():
            history_far(act_copies, r)
            acc[span, :] += conv(widen(act_hist[0, r]), 0, 0, 3 * chans)

        @pl.when(has_near)
        def _():
            history_near(act_copies, r)
            acc[span, pl.ds(goes, chans)] += conv(widen(act_hist[1, r]), 1, goes, chans)

        parts[out_part] = acc[span, pl.ds(goes, chans)].astype(BF16)
        if r == last:
            @pl.when(has_down)
            def _():
                part_down.start()
        else:
            @pl.when(has_up)
            def _():
                part_up.start()

        @pl.when(has_near)
        def _():
            acc[span, pl.ds(stays, 2 * chans)] += conv(widen(act_hist[1, r]), 1, stays, 2 * chans)

    def finish_row(r):
        total = acc[pl.ds(r * cols, cols), pl.ds(chans, chans)]
        if r > 0:
            total = total + acc[pl.ds((r - 1) * cols, cols), pl.ds(0, chans)]
        if r < rows - 1:
            total = total + acc[pl.ds((r + 1) * cols, cols), pl.ds(2 * chans, chans)]
        total = total + cb_ref[...].reshape(1, chans) + lat[r].astype(F32)
        if r == first:
            total = total + part_in[0].astype(F32)
        if r == last:
            total = total + part_in[1].astype(F32)
        blk[1 + r] = total.astype(BF16)

    tw_copy.wait()

    def mix(row, k):
        return jnp.dot(row, tw[k], preferred_element_type=F32)

    def newest(j):
        mixed[j] = mix(blk[j], 2) + tb_ref[...].reshape(1, 2 * chans)

    def mix_row(j):
        @pl.when(has_prev)
        def _():
            history_far(blk_copies, j)
            mixed[j] += mix(blk_hist[0, j], 0)

        @pl.when(has_near)
        def _():
            history_near(blk_copies, j)
            mixed[j] += mix(blk_hist[1, j], 1)

        for f in range(2):
            dbl[j, f] = mixed[j, :, pl.ds(f * chans, chans)].astype(BF16)

    @pl.when(has_up)
    def _():
        part_down.wait_recv()

    @pl.when(jnp.logical_not(has_up))
    def _():
        part_in[0] = jnp.zeros((cols, chans), BF16)

    for r in range(rows - 1):
        finish_row(r)

        if r == first:
            @pl.when(has_up & starts)
            def _():
                blk_up.start()

        history_start(blk_copies, 1 + r)
        newest(1 + r)

    @pl.when(has_down)
    def _():
        part_up.wait_recv()

    @pl.when(jnp.logical_not(has_down))
    def _():
        part_in[1] = jnp.zeros((cols, chans), BF16)

    finish_row(last)

    @pl.when(has_down)
    def _():
        blk_down.start()

    @pl.when(relays)
    def _():
        blk_to_partner.start()

    history_start(blk_copies, rows, direct)
    newest(rows)

    for r in range(rows):
        if r == last:
            @pl.when(relays)
            def _():
                blk_to_partner.wait_recv()
                blk_from_partner.start()

            @pl.when(has_up)
            def _():
                blk_down.wait_recv()
                history_start(blk_copies, 0)

        mix_row(1 + r)
        if r == first:
            @pl.when(has_up & later)
            def _():
                dbl_up.start()

            @pl.when(has_down & (t == 0))
            def _():
                blk_up.wait_recv()
                blk_copies[0](rows + 1).start()

    bias_row = ub_ref[...].reshape(1, outs_n)
    up_bias = jnp.concatenate(
        [bias_row[:, :low], bias_row[:, :low], bias_row[:, low:], bias_row[:, low:]], axis=1
    )

    def taps_dot(row, a, start, size):
        return lax.dot_general(
            row, umat[a, :, pl.ds(start, size)], (((1,), (1,)), ((), ())), preferred_element_type=F32
        )

    def stored_row(j):
        return dbl[j].reshape(2 * cols, chans)

    def upsample_row(a, r, result):
        center = result[:, : 2 * outs_n] + up_bias
        sides = result[:, 2 * outs_n :]
        even = center[:, :low] + column_shift(sides[:, :low], cols, 1)
        uneven = center[:, low : 2 * low] + column_shift(sides[:, low : 2 * low], cols, -1)
        tail = sides[:, 2 * low :]
        lane = lax.broadcasted_iota(jnp.int32, tail.shape, 1)
        tail = center[:, 2 * low :] + jnp.where(
            lane < high, column_shift(tail, cols, 1), column_shift(tail, cols, -1)
        )
        swapped = pltpu.roll(tail, high, 1)
        for f in range(2):
            span = slice(f * cols, (f + 1) * cols)
            wide_lo[pl.ds(0, cols, stride=2), :] = even[span]
            wide_lo[pl.ds(1, cols, stride=2), :] = uneven[span]
            wide_hi[pl.ds(0, cols, stride=2), :] = tail[span]
            wide_hi[pl.ds(1, cols, stride=2), :] = swapped[span]
            out_ref[f, 2 * r + a, pl.ds(0, low), :] = wide_lo[...].T.astype(BF16)
            out_ref[f, 2 * r + a, pl.ds(low, high), :] = wide_hi[...].T[:high].astype(BF16)

    for r in range(rows):
        for a in range(2):
            if 0 < r + a < rows:
                both = jnp.concatenate([stored_row(r + a), stored_row(r + a + 1)], axis=1)
                upsample_row(a, r, taps_dot(both, a, 0, 2 * chans))

    edge[0] = taps_dot(stored_row(1), 0, chans, chans)
    edge[1] = taps_dot(stored_row(rows), 1, 0, chans)

    @pl.when(has_up)
    def _():
        newest(0)
        mix_row(0)
        edge[0] += taps_dot(stored_row(0), 0, 0, chans)

    upsample_row(0, 0, edge[0])

    @pl.when(has_down & starts)
    def _():
        @pl.when(t == 1)
        def _():
            blk_up.wait_recv()

        newest(rows + 1)

        @pl.when(t == 1)
        def _():
            history_near(blk_copies, rows + 1)
            mixed[rows + 1] += mix(blk_hist[1, rows + 1], 1)

        for f in range(2):
            dbl[rows + 1, f] = mixed[rows + 1, :, pl.ds(f * chans, chans)].astype(BF16)

    @pl.when(has_down & later)
    def _():
        dbl_up.wait_recv()

    @pl.when(has_down)
    def _():
        edge[1] += taps_dot(stored_row(rows + 1), 1, chans, chans)

    upsample_row(1, last, edge[1])

    for r in range(rows):
        history_end(act_copies, r, has_next if r == order[0] else direct)
        history_end(blk_copies, 1 + r, direct if r == last else has_next)

    @pl.when(relays)
    def _():
        for r in order[1:]:
            to_partner(r).wait_send()
            from_partner(r).wait_send()
        blk_to_partner.wait_send()
        blk_from_partner.wait_send()

    @pl.when(has_up)
    def _():
        history_end(blk_copies, 0)
        part_up.wait_send()

        @pl.when(later)
        def _():
            dbl_up.wait_send()

        @pl.when(starts)
        def _():
            blk_up.wait_send()

    @pl.when(has_down)
    def _():
        part_down.wait_send()
        blk_down.wait_send()

        @pl.when(t == 0)
        def _():
            blk_copies[0](rows + 1).wait_send()


def local(frames, tiles, latent, gain, conv_weight, conv_bias, time_weight, time_bias, up_weight, up_bias):
    _, rows, cols, chans = latent.shape
    outs_n = up_weight.shape[3]
    low = 128
    dma = pltpu.SemaphoreType.DMA
    row = (cols, chans)
    transposed = pl.pallas_call(
        functools.partial(kernel, frames, tiles),
        out_shape=jax.ShapeDtypeStruct((2, 2 * rows, outs_n, 2 * cols), BF16),
        in_specs=[pl.BlockSpec(memory_space=pltpu.HBM)] * 8,
        out_specs=pl.BlockSpec(memory_space=pltpu.VMEM),
        scratch_shapes=[
            pltpu.VMEM((rows,) + row, BF16),
            pltpu.VMEM((rows,) + row, BF16),
            pltpu.VMEM((2, rows) + row, BF16),
            pltpu.VMEM((rows,) + row, BF16),
            pltpu.VMEM((2,) + row, BF16),
            pltpu.VMEM((2,) + row, BF16),
            pltpu.VMEM((rows + 2,) + row, BF16),
            pltpu.VMEM((2, rows + 2) + row, BF16),
            pltpu.VMEM(row, BF16),
            pltpu.VMEM((rows + 2, 2) + row, BF16),
            pltpu.VMEM((chans,), F32),
            pltpu.VMEM((chans,), F32),
            pltpu.VMEM((2 * chans,), F32),
            pltpu.VMEM((outs_n,), F32),
            pltpu.VMEM((3, 3, chans, 3 * chans), BF16),
            pltpu.VMEM((3, chans, 2 * chans), BF16),
            pltpu.VMEM((3, 3, outs_n, chans), BF16),
            pltpu.VMEM((2, 4 * outs_n, 2 * chans), BF16),
            pltpu.VMEM((rows * cols, 3 * chans), F32),
            pltpu.VMEM((rows + 2, cols, 2 * chans), F32),
            pltpu.VMEM((2, 2 * cols, 4 * outs_n), F32),
            pltpu.VMEM((2 * cols, low), F32),
            pltpu.VMEM((2 * cols, low), F32),
            dma(()), dma((4,)), dma((3, 3)), dma(()), dma(()),
            dma((2, rows)), dma((2, rows)), dma((rows,)),
            dma((2, rows)), dma((rows,)),
            dma((2, rows + 2)), dma((2, rows + 2)), dma((rows + 2,)),
            dma((2,)), dma((2,)), dma((2,)), dma((2,)), dma((2,)), dma((3,)),
        ],
        compiler_params=pltpu.CompilerParams(
            collective_id=0, has_side_effects=True, vmem_limit_bytes=48 * 1024 * 1024
        ),
    )(*(
        pltpu.with_memory_space_constraint(array, pltpu.HBM)
        for array in (
            latent, gain, conv_bias, time_bias, up_bias,
            conv_weight, time_weight, jnp.swapaxes(up_weight, 2, 3),
        )
    ))
    return jnp.swapaxes(transposed, 2, 3)


def solution(mesh):
    placed = (P("tm", "tile", None, None), P(), P(), P(), P(), P(), P(), P())
    return jax.shard_map(
        functools.partial(local, mesh.shape["tm"], mesh.shape["tile"]),
        mesh=mesh, in_specs=placed, out_specs=P("tm", "tile", None, None), check_vma=False,
    )
```

```python
import functools

import jax
import jax.numpy as jnp
from jax import lax
from jax.experimental import pallas as pl
from jax.experimental.pallas import tpu as pltpu
from jax.sharding import PartitionSpec as P

F32 = jnp.float32
BF16 = jnp.bfloat16
MESH = pl.DeviceIdType.MESH


def column_shift(flat, cols, step):
    total = flat.shape[0]
    rolled = pltpu.roll(flat, step % total, 0)
    place = lax.broadcasted_iota(jnp.int32, flat.shape, 0) % cols
    edge = 0 if step > 0 else cols - 1
    return jnp.where(place == edge, 0.0, rolled)


def kernel(
    frames, tiles,
    lat_hbm, gain_hbm, cb_hbm, tb_hbm, ub_hbm, cw_hbm, tw_hbm, uw_hbm,
    out_ref,
    lat, act, act_hist, act_relay, parts, part_in, blk, blk_hist, dbl,
    gain_ref, cb_ref, tb_ref, ub_ref, cw, tw, uw, umat, acc, mixed, edge, wide_lo, wide_hi,
    lat_sem, bias_sem, cw_sem, tw_sem, uw_sem,
    a_send, a_recv, a_fsend, r_send, r_recv, b_send, b_recv, b_fsend,
    p_down_sem, p_up_sem, b_down_sem, b_up_sem, d_up_sem,
):
    rows, cols, chans = lat.shape
    outs_n = uw.shape[2]
    low = 128
    high = outs_n - low
    cells = rows * cols
    t = lax.axis_index("tm")
    s = lax.axis_index("tile")
    odd = lax.rem(t, 2) == 1
    even = jnp.logical_not(odd)
    has_next = t + 2 < frames
    has_prev = t >= 2
    has_near = t >= 1
    starts = t < 2
    later = t >= 2
    has_up = s > 0
    has_down = s < tiles - 1

    lat_copy = pltpu.make_async_copy(lat_hbm.at[0], lat, lat_sem)
    lat_copy.start()
    bias_copies = []
    for k, (src, dst) in enumerate(
        ((gain_hbm, gain_ref), (cb_hbm, cb_ref), (tb_hbm, tb_ref), (ub_hbm, ub_ref))
    ):
        copy = pltpu.make_async_copy(src, dst, bias_sem.at[k])
        copy.start()
        bias_copies.append(copy)
    cw_copies = {}
    for dt in (2, 0, 1):
        for dh in range(3):
            copy = pltpu.make_async_copy(
                cw_hbm.at[dt, dh],
                cw.at[dt, :, :, pl.ds(dh * chans, chans)],
                cw_sem.at[dt, dh],
            )
            copy.start()
            cw_copies[dt, dh] = copy
    tw_copy = pltpu.make_async_copy(tw_hbm, tw, tw_sem)
    tw_copy.start()
    uw_copy = pltpu.make_async_copy(uw_hbm, uw, uw_sem)
    uw_copy.start()

    half = frames // 2
    partner = s + 1 - 2 * lax.rem(s, 2)
    relays = t // 2 == half // 2 - 1
    relayed = t // 2 == half // 2
    direct = jnp.logical_and(has_next, jnp.logical_not(relays))

    sibling = t + 1 - 2 * lax.rem(t, 2)
    barrier = pltpu.get_barrier_semaphore()

    def greet(condition, where):
        @pl.when(condition)
        def _():
            pl.semaphore_signal(barrier, inc=1, device_id=where, device_id_type=MESH)

    pl.semaphore_signal(barrier, inc=1, device_id={"tm": sibling}, device_id_type=MESH)
    greet(has_next, {"tm": t + 2})
    greet(has_prev, {"tm": t - 2})
    greet(relays, {"tm": t + 2, "tile": partner})
    greet(relayed, {"tm": t - 2, "tile": partner})
    greet(has_up, {"tile": s - 1})
    greet(has_down, {"tile": s + 1})

    def history_copies(own, hist, send, recv, fsend):
        def nearer(r):
            return pltpu.make_async_remote_copy(
                own.at[r], hist.at[1, r], send.at[0, r], recv.at[1, r],
                device_id={"tm": sibling}, device_id_type=MESH,
            )

        def farther(r):
            return pltpu.make_async_remote_copy(
                own.at[r], hist.at[0, r], send.at[1, r], recv.at[0, r],
                device_id={"tm": t + 2}, device_id_type=MESH,
            )

        def forward(r):
            return pltpu.make_async_remote_copy(
                hist.at[0, r], hist.at[1, r], fsend.at[r], recv.at[1, r],
                device_id={"tm": sibling}, device_id_type=MESH,
            )

        return nearer, farther, forward

    def history_start(copies, r, sends=has_next):
        nearer, farther, _ = copies

        @pl.when(sends)
        def _():
            farther(r).start()

        @pl.when(even)
        def _():
            nearer(r).start()

    def history_far(copies, r):
        _, farther, forward = copies
        farther(r).wait_recv()

        @pl.when(odd)
        def _():
            forward(r).start()

    def history_near(copies, r):
        copies[0](r).wait_recv()

    def history_end(copies, r, sends=has_next):
        nearer, farther, forward = copies

        @pl.when(sends)
        def _():
            farther(r).wait_send()

        @pl.when(even)
        def _():
            nearer(r).wait_send()

        @pl.when(jnp.logical_and(odd, has_prev))
        def _():
            forward(r).wait_send()

    def to_tile(src, dst, sems, where):
        return pltpu.make_async_remote_copy(
            src, dst, sems.at[0], sems.at[1], device_id={"tile": where}, device_id_type=MESH
        )

    first, last = 0, rows - 1
    act_copies = history_copies(act, act_hist, a_send, a_recv, a_fsend)
    blk_copies = history_copies(blk, blk_hist, b_send, b_recv, b_fsend)
    part_down = to_tile(parts.at[1], part_in.at[0], p_down_sem, s + 1)
    part_up = to_tile(parts.at[0], part_in.at[1], p_up_sem, s - 1)
    blk_down = to_tile(blk.at[rows], blk.at[0], b_down_sem, s + 1)
    blk_up = to_tile(blk.at[1], blk.at[rows + 1], b_up_sem, s - 1)
    dbl_up = to_tile(dbl.at[1], dbl.at[rows + 1], d_up_sem, s - 1)

    def activate(r):
        values = lat[r].astype(F32)
        meansq = jnp.mean(values * values, axis=-1, keepdims=True)
        scaled = values * lax.rsqrt(meansq + 1e-06) * gain_ref[...].reshape(1, chans)
        act[r] = (scaled * jax.nn.sigmoid(scaled)).astype(BF16)

    peers = 1
    for condition in (has_next, has_prev, relays, relayed, has_up, has_down):
        peers = peers + condition.astype(jnp.int32)

    def to_partner(r):
        return pltpu.make_async_remote_copy(
            act.at[r], act_relay.at[r], r_send.at[0, r], r_recv.at[r],
            device_id={"tile": partner}, device_id_type=MESH,
        )

    def from_partner(r):
        return pltpu.make_async_remote_copy(
            act_relay.at[r], act_hist.at[0, r], r_send.at[1, r], a_recv.at[0, r],
            device_id={"tm": t + 2, "tile": partner}, device_id_type=MESH,
        )

    order = tuple(range(rows))[::-1]
    lat_copy.wait()
    for copy in bias_copies:
        copy.wait()
    for r in order:
        activate(r)
        if r == order[0]:
            pl.semaphore_wait(barrier, peers)
        if r == order[0]:
            history_start(act_copies, r)
        else:
            @pl.when(relays)
            def _():
                to_partner(r).start()

            history_start(act_copies, r, direct)

    def widen(frame):
        flat = frame.reshape(-1, chans)
        wide = flat.astype(F32)
        before = column_shift(wide, cols, 1).astype(BF16)
        after = column_shift(wide, cols, -1).astype(BF16)
        return jnp.concatenate([before, flat, after], axis=1)

    def conv(stacked, dt, start, size):
        taps = cw.at[dt, :, :, pl.ds(start, size)][...].reshape(3 * chans, size)
        return jnp.dot(stacked, taps, preferred_element_type=F32)

    def weights_ready(dt):
        for dh in range(3):
            cw_copies[dt, dh].wait()

    weights_ready(2)
    acc[...] = conv(widen(act[...]), 2, 0, 3 * chans)
    @pl.when(relays)
    def _():
        for r in order[1:]:
            to_partner(r).wait_recv()
            from_partner(r).start()

    uw_copy.wait()
    row_sets = {(0, 0): (0,), (0, 1): (1, 2), (1, 0): (0, 1), (1, 1): (2,)}
    for (a, i), picks in row_sets.items():
        taps = []
        for kw in range(3):
            tap = uw[picks[0], kw].astype(F32)
            for kh in picks[1:]:
                tap = tap + uw[kh, kw].astype(F32)
            taps.append(tap)
        center = (taps[1] + taps[2], taps[0] + taps[1])
        sides = (taps[0], taps[2])
        lanes = pl.ds(i * chans, chans)
        for base, pair in ((0, center), (2 * outs_n, sides)):
            for b in range(2):
                value = pair[b].astype(BF16)
                umat[a, pl.ds(base + b * low, low), lanes] = value[:low]
                umat[a, pl.ds(base + 2 * low + b * high, high), lanes] = value[low:]

    weights_ready(0)
    weights_ready(1)
    for r in order:
        span = pl.ds(r * cols, cols)
        goes, stays = (0, chans) if r == last else (2 * chans, 0)
        out_part = 1 if r == last else 0

        @pl.when(has_prev)
        def _():
            history_far(act_copies, r)
            acc[span, :] += conv(widen(act_hist[0, r]), 0, 0, 3 * chans)

        @pl.when(has_near)
        def _():
            history_near(act_copies, r)
            acc[span, pl.ds(goes, chans)] += conv(widen(act_hist[1, r]), 1, goes, chans)

        parts[out_part] = acc[span, pl.ds(goes, chans)].astype(BF16)
        if r == last:
            @pl.when(has_down)
            def _():
                part_down.start()
        else:
            @pl.when(has_up)
            def _():
                part_up.start()

        @pl.when(has_near)
        def _():
            acc[span, pl.ds(stays, 2 * chans)] += conv(widen(act_hist[1, r]), 1, stays, 2 * chans)

    def finish_row(r):
        total = acc[pl.ds(r * cols, cols), pl.ds(chans, chans)]
        if r > 0:
            total = total + acc[pl.ds((r - 1) * cols, cols), pl.ds(0, chans)]
        if r < rows - 1:
            total = total + acc[pl.ds((r + 1) * cols, cols), pl.ds(2 * chans, chans)]
        total = total + cb_ref[...].reshape(1, chans) + lat[r].astype(F32)
        if r == first:
            total = total + part_in[0].astype(F32)
        if r == last:
            total = total + part_in[1].astype(F32)
        blk[1 + r] = total.astype(BF16)

    tw_copy.wait()

    def mix(row, k):
        return jnp.dot(row, tw[k], preferred_element_type=F32)

    def newest(j):
        mixed[j] = mix(blk[j], 2) + tb_ref[...].reshape(1, 2 * chans)

    def mix_row(j):
        @pl.when(has_prev)
        def _():
            history_far(blk_copies, j)
            mixed[j] += mix(blk_hist[0, j], 0)

        @pl.when(has_near)
        def _():
            history_near(blk_copies, j)
            mixed[j] += mix(blk_hist[1, j], 1)

        for f in range(2):
            dbl[j, f] = mixed[j, :, pl.ds(f * chans, chans)].astype(BF16)

    @pl.when(has_up)
    def _():
        part_down.wait_recv()

    @pl.when(jnp.logical_not(has_up))
    def _():
        part_in[0] = jnp.zeros((cols, chans), BF16)

    for r in range(rows - 1):
        finish_row(r)

        if r == first:
            @pl.when(has_up & starts)
            def _():
                blk_up.start()

        history_start(blk_copies, 1 + r)
        newest(1 + r)

    @pl.when(has_down)
    def _():
        part_up.wait_recv()

    @pl.when(jnp.logical_not(has_down))
    def _():
        part_in[1] = jnp.zeros((cols, chans), BF16)

    finish_row(last)

    @pl.when(has_down)
    def _():
        blk_down.start()

    history_start(blk_copies, rows)
    newest(rows)

    for r in range(rows):
        if r == last:
            @pl.when(has_up)
            def _():
                blk_down.wait_recv()
                history_start(blk_copies, 0)

        mix_row(1 + r)
        if r == first:
            @pl.when(has_up & later)
            def _():
                dbl_up.start()

            @pl.when(has_down & (t == 0))
            def _():
                blk_up.wait_recv()
                blk_copies[0](rows + 1).start()

    bias_row = ub_ref[...].reshape(1, outs_n)
    up_bias = jnp.concatenate(
        [bias_row[:, :low], bias_row[:, :low], bias_row[:, low:], bias_row[:, low:]], axis=1
    )

    def taps_dot(row, a, start, size):
        return lax.dot_general(
            row, umat[a, :, pl.ds(start, size)], (((1,), (1,)), ((), ())), preferred_element_type=F32
        )

    def stored_row(j):
        return dbl[j].reshape(2 * cols, chans)

    def upsample_row(a, r, result):
        center = result[:, : 2 * outs_n] + up_bias
        sides = result[:, 2 * outs_n :]
        even = center[:, :low] + column_shift(sides[:, :low], cols, 1)
        uneven = center[:, low : 2 * low] + column_shift(sides[:, low : 2 * low], cols, -1)
        tail = sides[:, 2 * low :]
        lane = lax.broadcasted_iota(jnp.int32, tail.shape, 1)
        tail = center[:, 2 * low :] + jnp.where(
            lane < high, column_shift(tail, cols, 1), column_shift(tail, cols, -1)
        )
        swapped = pltpu.roll(tail, high, 1)
        for f in range(2):
            span = slice(f * cols, (f + 1) * cols)
            wide_lo[pl.ds(0, cols, stride=2), :] = even[span]
            wide_lo[pl.ds(1, cols, stride=2), :] = uneven[span]
            wide_hi[pl.ds(0, cols, stride=2), :] = tail[span]
            wide_hi[pl.ds(1, cols, stride=2), :] = swapped[span]
            out_ref[f, 2 * r + a, pl.ds(0, low), :] = wide_lo[...].T.astype(BF16)
            out_ref[f, 2 * r + a, pl.ds(low, high), :] = wide_hi[...].T[:high].astype(BF16)

    for r in range(rows):
        for a in range(2):
            if 0 < r + a < rows:
                both = jnp.concatenate([stored_row(r + a), stored_row(r + a + 1)], axis=1)
                upsample_row(a, r, taps_dot(both, a, 0, 2 * chans))

    edge[0] = taps_dot(stored_row(1), 0, chans, chans)
    edge[1] = taps_dot(stored_row(rows), 1, 0, chans)

    @pl.when(has_up)
    def _():
        newest(0)
        mix_row(0)
        edge[0] += taps_dot(stored_row(0), 0, 0, chans)

    upsample_row(0, 0, edge[0])

    @pl.when(has_down & starts)
    def _():
        @pl.when(t == 1)
        def _():
            blk_up.wait_recv()

        newest(rows + 1)

        @pl.when(t == 1)
        def _():
            history_near(blk_copies, rows + 1)
            mixed[rows + 1] += mix(blk_hist[1, rows + 1], 1)

        for f in range(2):
            dbl[rows + 1, f] = mixed[rows + 1, :, pl.ds(f * chans, chans)].astype(BF16)

    @pl.when(has_down & later)
    def _():
        dbl_up.wait_recv()

    @pl.when(has_down)
    def _():
        edge[1] += taps_dot(stored_row(rows + 1), 1, chans, chans)

    upsample_row(1, last, edge[1])

    for r in range(rows):
        history_end(act_copies, r, has_next if r == order[0] else direct)
        history_end(blk_copies, 1 + r)

    @pl.when(relays)
    def _():
        for r in order[1:]:
            to_partner(r).wait_send()
            from_partner(r).wait_send()

    @pl.when(has_up)
    def _():
        history_end(blk_copies, 0)
        part_up.wait_send()

        @pl.when(later)
        def _():
            dbl_up.wait_send()

        @pl.when(starts)
        def _():
            blk_up.wait_send()

    @pl.when(has_down)
    def _():
        part_down.wait_send()
        blk_down.wait_send()

        @pl.when(t == 0)
        def _():
            blk_copies[0](rows + 1).wait_send()


def local(frames, tiles, latent, gain, conv_weight, conv_bias, time_weight, time_bias, up_weight, up_bias):
    _, rows, cols, chans = latent.shape
    outs_n = up_weight.shape[3]
    low = 128
    dma = pltpu.SemaphoreType.DMA
    row = (cols, chans)
    transposed = pl.pallas_call(
        functools.partial(kernel, frames, tiles),
        out_shape=jax.ShapeDtypeStruct((2, 2 * rows, outs_n, 2 * cols), BF16),
        in_specs=[pl.BlockSpec(memory_space=pltpu.HBM)] * 8,
        out_specs=pl.BlockSpec(memory_space=pltpu.VMEM),
        scratch_shapes=[
            pltpu.VMEM((rows,) + row, BF16),
            pltpu.VMEM((rows,) + row, BF16),
            pltpu.VMEM((2, rows) + row, BF16),
            pltpu.VMEM((rows,) + row, BF16),
            pltpu.VMEM((2,) + row, BF16),
            pltpu.VMEM((2,) + row, BF16),
            pltpu.VMEM((rows + 2,) + row, BF16),
            pltpu.VMEM((2, rows + 2) + row, BF16),
            pltpu.VMEM((rows + 2, 2) + row, BF16),
            pltpu.VMEM((chans,), F32),
            pltpu.VMEM((chans,), F32),
            pltpu.VMEM((2 * chans,), F32),
            pltpu.VMEM((outs_n,), F32),
            pltpu.VMEM((3, 3, chans, 3 * chans), BF16),
            pltpu.VMEM((3, chans, 2 * chans), BF16),
            pltpu.VMEM((3, 3, outs_n, chans), BF16),
            pltpu.VMEM((2, 4 * outs_n, 2 * chans), BF16),
            pltpu.VMEM((rows * cols, 3 * chans), F32),
            pltpu.VMEM((rows + 2, cols, 2 * chans), F32),
            pltpu.VMEM((2, 2 * cols, 4 * outs_n), F32),
            pltpu.VMEM((2 * cols, low), F32),
            pltpu.VMEM((2 * cols, low), F32),
            dma(()), dma((4,)), dma((3, 3)), dma(()), dma(()),
            dma((2, rows)), dma((2, rows)), dma((rows,)),
            dma((2, rows)), dma((rows,)),
            dma((2, rows + 2)), dma((2, rows + 2)), dma((rows + 2,)),
            dma((2,)), dma((2,)), dma((2,)), dma((2,)), dma((2,)),
        ],
        compiler_params=pltpu.CompilerParams(
            collective_id=0, has_side_effects=True, vmem_limit_bytes=48 * 1024 * 1024
        ),
    )(*(
        pltpu.with_memory_space_constraint(array, pltpu.HBM)
        for array in (
            latent, gain, conv_bias, time_bias, up_bias,
            conv_weight, time_weight, jnp.swapaxes(up_weight, 2, 3),
        )
    ))
    return jnp.swapaxes(transposed, 2, 3)


def solution(mesh):
    placed = (P("tm", "tile", None, None), P(), P(), P(), P(), P(), P(), P())
    return jax.shard_map(
        functools.partial(local, mesh.shape["tm"], mesh.shape["tile"]),
        mesh=mesh, in_specs=placed, out_specs=P("tm", "tile", None, None), check_vma=False,
    )
```

```python
import functools

import jax
import jax.numpy as jnp
from jax import lax
from jax.experimental import pallas as pl
from jax.experimental.pallas import tpu as pltpu
from jax.sharding import PartitionSpec as P

F32 = jnp.float32
BF16 = jnp.bfloat16
MESH = pl.DeviceIdType.MESH


def column_shift(flat, cols, step):
    total = flat.shape[0]
    rolled = pltpu.roll(flat, step % total, 0)
    place = lax.broadcasted_iota(jnp.int32, flat.shape, 0) % cols
    edge = 0 if step > 0 else cols - 1
    return jnp.where(place == edge, 0.0, rolled)


def kernel(
    frames, tiles,
    lat_hbm, gain_hbm, cb_hbm, tb_hbm, ub_hbm, cw_hbm, tw_hbm, uw_hbm,
    out_ref,
    lat, act, act_hist, act_relay, parts, part_in, blk, blk_hist, dbl,
    gain_ref, cb_ref, tb_ref, ub_ref, cw, tw, uw, umat, acc, mixed, edge, wide_lo, wide_hi,
    lat_sem, bias_sem, cw_sem, tw_sem, uw_sem,
    a_send, a_recv, a_fsend, r_send, r_recv, b_send, b_recv, b_fsend,
    p_down_sem, p_up_sem, b_down_sem, b_up_sem, d_up_sem,
):
    rows, cols, chans = lat.shape
    outs_n = uw.shape[2]
    low = 128
    high = outs_n - low
    cells = rows * cols
    t = lax.axis_index("tm")
    s = lax.axis_index("tile")
    odd = lax.rem(t, 2) == 1
    even = jnp.logical_not(odd)
    has_next = t + 2 < frames
    has_prev = t >= 2
    has_near = t >= 1
    starts = t < 2
    later = t >= 2
    has_up = s > 0
    has_down = s < tiles - 1

    lat_copy = pltpu.make_async_copy(lat_hbm.at[0], lat, lat_sem)
    lat_copy.start()
    bias_copies = []
    for k, (src, dst) in enumerate(
        ((gain_hbm, gain_ref), (cb_hbm, cb_ref), (tb_hbm, tb_ref), (ub_hbm, ub_ref))
    ):
        copy = pltpu.make_async_copy(src, dst, bias_sem.at[k])
        copy.start()
        bias_copies.append(copy)
    half = frames // 2
    partner = s + 1 - 2 * lax.rem(s, 2)
    relays = t // 2 == half // 2 - 1
    relayed = t // 2 == half // 2
    direct = jnp.logical_and(has_next, jnp.logical_not(relays))

    sibling = t + 1 - 2 * lax.rem(t, 2)
    barrier = pltpu.get_barrier_semaphore()

    def greet(condition, where):
        @pl.when(condition)
        def _():
            pl.semaphore_signal(barrier, inc=1, device_id=where, device_id_type=MESH)

    pl.semaphore_signal(barrier, inc=1, device_id={"tm": sibling}, device_id_type=MESH)
    greet(has_next, {"tm": t + 2})
    greet(has_prev, {"tm": t - 2})
    greet(relays, {"tm": t + 2, "tile": partner})
    greet(relayed, {"tm": t - 2, "tile": partner})
    greet(has_up, {"tile": s - 1})
    greet(has_down, {"tile": s + 1})

    cw_copies = {}
    for dt in (2, 0, 1):
        for dh in range(3):
            copy = pltpu.make_async_copy(
                cw_hbm.at[dt, dh],
                cw.at[dt, :, :, pl.ds(dh * chans, chans)],
                cw_sem.at[dt, dh],
            )
            copy.start()
            cw_copies[dt, dh] = copy
    tw_copy = pltpu.make_async_copy(tw_hbm, tw, tw_sem)
    tw_copy.start()
    uw_copy = pltpu.make_async_copy(uw_hbm, uw, uw_sem)
    uw_copy.start()

    def history_copies(own, hist, send, recv, fsend):
        def nearer(r):
            return pltpu.make_async_remote_copy(
                own.at[r], hist.at[1, r], send.at[0, r], recv.at[1, r],
                device_id={"tm": sibling}, device_id_type=MESH,
            )

        def farther(r):
            return pltpu.make_async_remote_copy(
                own.at[r], hist.at[0, r], send.at[1, r], recv.at[0, r],
                device_id={"tm": t + 2}, device_id_type=MESH,
            )

        def forward(r):
            return pltpu.make_async_remote_copy(
                hist.at[0, r], hist.at[1, r], fsend.at[r], recv.at[1, r],
                device_id={"tm": sibling}, device_id_type=MESH,
            )

        return nearer, farther, forward

    def history_start(copies, r, sends=has_next):
        nearer, farther, _ = copies

        @pl.when(sends)
        def _():
            farther(r).start()

        @pl.when(even)
        def _():
            nearer(r).start()

    def history_far(copies, r):
        _, farther, forward = copies
        farther(r).wait_recv()

        @pl.when(odd)
        def _():
            forward(r).start()

    def history_near(copies, r):
        copies[0](r).wait_recv()

    def history_end(copies, r, sends=has_next):
        nearer, farther, forward = copies

        @pl.when(sends)
        def _():
            farther(r).wait_send()

        @pl.when(even)
        def _():
            nearer(r).wait_send()

        @pl.when(jnp.logical_and(odd, has_prev))
        def _():
            forward(r).wait_send()

    def to_tile(src, dst, sems, where):
        return pltpu.make_async_remote_copy(
            src, dst, sems.at[0], sems.at[1], device_id={"tile": where}, device_id_type=MESH
        )

    first, last = 0, rows - 1
    act_copies = history_copies(act, act_hist, a_send, a_recv, a_fsend)
    blk_copies = history_copies(blk, blk_hist, b_send, b_recv, b_fsend)
    part_down = to_tile(parts.at[1], part_in.at[0], p_down_sem, s + 1)
    part_up = to_tile(parts.at[0], part_in.at[1], p_up_sem, s - 1)
    blk_down = to_tile(blk.at[rows], blk.at[0], b_down_sem, s + 1)
    blk_up = to_tile(blk.at[1], blk.at[rows + 1], b_up_sem, s - 1)
    dbl_up = to_tile(dbl.at[1], dbl.at[rows + 1], d_up_sem, s - 1)

    def activate(r):
        values = lat[r].astype(F32)
        meansq = jnp.mean(values * values, axis=-1, keepdims=True)
        scaled = values * lax.rsqrt(meansq + 1e-06) * gain_ref[...].reshape(1, chans)
        act[r] = (scaled * jax.nn.sigmoid(scaled)).astype(BF16)

    peers = 1
    for condition in (has_next, has_prev, relays, relayed, has_up, has_down):
        peers = peers + condition.astype(jnp.int32)

    def to_partner(r):
        return pltpu.make_async_remote_copy(
            act.at[r], act_relay.at[r], r_send.at[0, r], r_recv.at[r],
            device_id={"tile": partner}, device_id_type=MESH,
        )

    def from_partner(r):
        return pltpu.make_async_remote_copy(
            act_relay.at[r], act_hist.at[0, r], r_send.at[1, r], a_recv.at[0, r],
            device_id={"tm": t + 2, "tile": partner}, device_id_type=MESH,
        )

    order = tuple(range(rows))[::-1]
    lat_copy.wait()
    for copy in bias_copies:
        copy.wait()
    for r in order:
        activate(r)
        if r == order[0]:
            pl.semaphore_wait(barrier, peers)
        if r == order[0]:
            history_start(act_copies, r)
        else:
            @pl.when(relays)
            def _():
                to_partner(r).start()

            history_start(act_copies, r, direct)

    def widen(frame):
        flat = frame.reshape(-1, chans)
        wide = flat.astype(F32)
        before = column_shift(wide, cols, 1).astype(BF16)
        after = column_shift(wide, cols, -1).astype(BF16)
        return jnp.concatenate([before, flat, after], axis=1)

    def conv(stacked, dt, start, size):
        taps = cw.at[dt, :, :, pl.ds(start, size)][...].reshape(3 * chans, size)
        return jnp.dot(stacked, taps, preferred_element_type=F32)

    def weights_ready(dt):
        for dh in range(3):
            cw_copies[dt, dh].wait()

    weights_ready(2)
    acc[...] = conv(widen(act[...]), 2, 0, 3 * chans)
    @pl.when(relays)
    def _():
        for r in order[1:]:
            to_partner(r).wait_recv()
            from_partner(r).start()

    uw_copy.wait()
    row_sets = {(0, 0): (0,), (0, 1): (1, 2), (1, 0): (0, 1), (1, 1): (2,)}
    for (a, i), picks in row_sets.items():
        taps = []
        for kw in range(3):
            tap = uw[picks[0], kw].astype(F32)
            for kh in picks[1:]:
                tap = tap + uw[kh, kw].astype(F32)
            taps.append(tap)
        center = (taps[1] + taps[2], taps[0] + taps[1])
        sides = (taps[0], taps[2])
        lanes = pl.ds(i * chans, chans)
        for base, pair in ((0, center), (2 * outs_n, sides)):
            for b in range(2):
                value = pair[b].astype(BF16)
                umat[a, pl.ds(base + b * low, low), lanes] = value[:low]
                umat[a, pl.ds(base + 2 * low + b * high, high), lanes] = value[low:]

    weights_ready(0)
    weights_ready(1)
    for r in order:
        span = pl.ds(r * cols, cols)
        goes, stays = (0, chans) if r == last else (2 * chans, 0)
        out_part = 1 if r == last else 0

        @pl.when(has_prev)
        def _():
            history_far(act_copies, r)
            acc[span, :] += conv(widen(act_hist[0, r]), 0, 0, 3 * chans)

        @pl.when(has_near)
        def _():
            history_near(act_copies, r)
            acc[span, pl.ds(goes, chans)] += conv(widen(act_hist[1, r]), 1, goes, chans)

        parts[out_part] = acc[span, pl.ds(goes, chans)].astype(BF16)
        if r == last:
            @pl.when(has_down)
            def _():
                part_down.start()
        else:
            @pl.when(has_up)
            def _():
                part_up.start()

        @pl.when(has_near)
        def _():
            acc[span, pl.ds(stays, 2 * chans)] += conv(widen(act_hist[1, r]), 1, stays, 2 * chans)

    def finish_row(r):
        total = acc[pl.ds(r * cols, cols), pl.ds(chans, chans)]
        if r > 0:
            total = total + acc[pl.ds((r - 1) * cols, cols), pl.ds(0, chans)]
        if r < rows - 1:
            total = total + acc[pl.ds((r + 1) * cols, cols), pl.ds(2 * chans, chans)]
        total = total + cb_ref[...].reshape(1, chans) + lat[r].astype(F32)
        if r == first:
            total = total + part_in[0].astype(F32)
        if r == last:
            total = total + part_in[1].astype(F32)
        blk[1 + r] = total.astype(BF16)

    tw_copy.wait()

    def mix(row, k):
        return jnp.dot(row, tw[k], preferred_element_type=F32)

    def newest(j):
        mixed[j] = mix(blk[j], 2) + tb_ref[...].reshape(1, 2 * chans)

    def mix_far(j):
        @pl.when(has_prev)
        def _():
            history_far(blk_copies, j)
            mixed[j] += mix(blk_hist[0, j], 0)

    def mix_near(j):
        @pl.when(has_near)
        def _():
            history_near(blk_copies, j)
            mixed[j] += mix(blk_hist[1, j], 1)

        for f in range(2):
            dbl[j, f] = mixed[j, :, pl.ds(f * chans, chans)].astype(BF16)

    def taps_dot(row, a, start, size):
        return lax.dot_general(
            row, umat[a, :, pl.ds(start, size)], (((1,), (1,)), ((), ())), preferred_element_type=F32
        )

    def stored_row(j):
        return dbl[j].reshape(2 * cols, chans)

    @pl.when(has_up)
    def _():
        part_down.wait_recv()

    @pl.when(jnp.logical_not(has_up))
    def _():
        part_in[0] = jnp.zeros((cols, chans), BF16)

    for r in range(rows - 1):
        finish_row(r)

        if r == first:
            @pl.when(has_up & starts)
            def _():
                blk_up.start()

        history_start(blk_copies, 1 + r)
        newest(1 + r)

    @pl.when(has_down)
    def _():
        part_up.wait_recv()

    @pl.when(jnp.logical_not(has_down))
    def _():
        part_in[1] = jnp.zeros((cols, chans), BF16)

    finish_row(last)

    @pl.when(has_down)
    def _():
        blk_down.start()

    history_start(blk_copies, rows)
    newest(rows)

    for r in range(rows):
        if r == last:
            @pl.when(has_up)
            def _():
                blk_down.wait_recv()
                history_start(blk_copies, 0)

        mix_far(1 + r)
        mix_near(1 + r)
        if r == first:
            @pl.when(has_up & later)
            def _():
                dbl_up.start()

            @pl.when(has_down & (t == 0))
            def _():
                blk_up.wait_recv()
                blk_copies[0](rows + 1).start()

            edge[0] = taps_dot(stored_row(1), 0, chans, chans)

    bias_row = ub_ref[...].reshape(1, outs_n)
    up_bias = jnp.concatenate(
        [bias_row[:, :low], bias_row[:, :low], bias_row[:, low:], bias_row[:, low:]], axis=1
    )

    def upsample_row(a, r, result):
        center = result[:, : 2 * outs_n] + up_bias
        sides = result[:, 2 * outs_n :]
        even = center[:, :low] + column_shift(sides[:, :low], cols, 1)
        uneven = center[:, low : 2 * low] + column_shift(sides[:, low : 2 * low], cols, -1)
        tail = sides[:, 2 * low :]
        lane = lax.broadcasted_iota(jnp.int32, tail.shape, 1)
        tail = center[:, 2 * low :] + jnp.where(
            lane < high, column_shift(tail, cols, 1), column_shift(tail, cols, -1)
        )
        swapped = pltpu.roll(tail, high, 1)
        for f in range(2):
            span = slice(f * cols, (f + 1) * cols)
            wide_lo[pl.ds(0, cols, stride=2), :] = even[span]
            wide_lo[pl.ds(1, cols, stride=2), :] = uneven[span]
            wide_hi[pl.ds(0, cols, stride=2), :] = tail[span]
            wide_hi[pl.ds(1, cols, stride=2), :] = swapped[span]
            out_ref[f, 2 * r + a, pl.ds(0, low), :] = wide_lo[...].T.astype(BF16)
            out_ref[f, 2 * r + a, pl.ds(low, high), :] = wide_hi[...].T[:high].astype(BF16)

    for r in range(rows):
        for a in range(2):
            if 0 < r + a < rows:
                both = jnp.concatenate([stored_row(r + a), stored_row(r + a + 1)], axis=1)
                upsample_row(a, r, taps_dot(both, a, 0, 2 * chans))

    @pl.when(has_up)
    def _():
        newest(0)
        mix_far(0)

    edge[1] = taps_dot(stored_row(rows), 1, 0, chans)

    @pl.when(has_down & starts)
    def _():
        @pl.when(t == 1)
        def _():
            blk_up.wait_recv()

        newest(rows + 1)

        @pl.when(t == 1)
        def _():
            history_near(blk_copies, rows + 1)
            mixed[rows + 1] += mix(blk_hist[1, rows + 1], 1)

        for f in range(2):
            dbl[rows + 1, f] = mixed[rows + 1, :, pl.ds(f * chans, chans)].astype(BF16)

    @pl.when(has_down & later)
    def _():
        dbl_up.wait_recv()

    @pl.when(has_down)
    def _():
        edge[1] += taps_dot(stored_row(rows + 1), 1, chans, chans)

    upsample_row(1, last, edge[1])

    @pl.when(has_up)
    def _():
        mix_near(0)
        edge[0] += taps_dot(stored_row(0), 0, 0, chans)

    upsample_row(0, 0, edge[0])

    for r in range(rows):
        history_end(act_copies, r, has_next if r == order[0] else direct)
        history_end(blk_copies, 1 + r)

    @pl.when(relays)
    def _():
        for r in order[1:]:
            to_partner(r).wait_send()
            from_partner(r).wait_send()

    @pl.when(has_up)
    def _():
        history_end(blk_copies, 0)
        part_up.wait_send()

        @pl.when(later)
        def _():
            dbl_up.wait_send()

        @pl.when(starts)
        def _():
            blk_up.wait_send()

    @pl.when(has_down)
    def _():
        part_down.wait_send()
        blk_down.wait_send()

        @pl.when(t == 0)
        def _():
            blk_copies[0](rows + 1).wait_send()


def local(frames, tiles, latent, gain, conv_weight, conv_bias, time_weight, time_bias, up_weight, up_bias):
    _, rows, cols, chans = latent.shape
    outs_n = up_weight.shape[3]
    low = 128
    dma = pltpu.SemaphoreType.DMA
    row = (cols, chans)
    transposed = pl.pallas_call(
        functools.partial(kernel, frames, tiles),
        out_shape=jax.ShapeDtypeStruct((2, 2 * rows, outs_n, 2 * cols), BF16),
        in_specs=[pl.BlockSpec(memory_space=pltpu.HBM)] * 8,
        out_specs=pl.BlockSpec(memory_space=pltpu.VMEM),
        scratch_shapes=[
            pltpu.VMEM((rows,) + row, BF16),
            pltpu.VMEM((rows,) + row, BF16),
            pltpu.VMEM((2, rows) + row, BF16),
            pltpu.VMEM((rows,) + row, BF16),
            pltpu.VMEM((2,) + row, BF16),
            pltpu.VMEM((2,) + row, BF16),
            pltpu.VMEM((rows + 2,) + row, BF16),
            pltpu.VMEM((2, rows + 2) + row, BF16),
            pltpu.VMEM((rows + 2, 2) + row, BF16),
            pltpu.VMEM((chans,), F32),
            pltpu.VMEM((chans,), F32),
            pltpu.VMEM((2 * chans,), F32),
            pltpu.VMEM((outs_n,), F32),
            pltpu.VMEM((3, 3, chans, 3 * chans), BF16),
            pltpu.VMEM((3, chans, 2 * chans), BF16),
            pltpu.VMEM((3, 3, outs_n, chans), BF16),
            pltpu.VMEM((2, 4 * outs_n, 2 * chans), BF16),
            pltpu.VMEM((rows * cols, 3 * chans), F32),
            pltpu.VMEM((rows + 2, cols, 2 * chans), F32),
            pltpu.VMEM((2, 2 * cols, 4 * outs_n), F32),
            pltpu.VMEM((2 * cols, low), F32),
            pltpu.VMEM((2 * cols, low), F32),
            dma(()), dma((4,)), dma((3, 3)), dma(()), dma(()),
            dma((2, rows)), dma((2, rows)), dma((rows,)),
            dma((2, rows)), dma((rows,)),
            dma((2, rows + 2)), dma((2, rows + 2)), dma((rows + 2,)),
            dma((2,)), dma((2,)), dma((2,)), dma((2,)), dma((2,)),
        ],
        compiler_params=pltpu.CompilerParams(
            collective_id=0, has_side_effects=True, vmem_limit_bytes=48 * 1024 * 1024
        ),
    )(*(
        pltpu.with_memory_space_constraint(array, pltpu.HBM)
        for array in (
            latent, gain, conv_bias, time_bias, up_bias,
            conv_weight, time_weight, jnp.swapaxes(up_weight, 2, 3),
        )
    ))
    return jnp.swapaxes(transposed, 2, 3)


def solution(mesh):
    placed = (P("tm", "tile", None, None), P(), P(), P(), P(), P(), P(), P())
    return jax.shard_map(
        functools.partial(local, mesh.shape["tm"], mesh.shape["tile"]),
        mesh=mesh, in_specs=placed, out_specs=P("tm", "tile", None, None), check_vma=False,
    )
```

```python
import functools

import jax
import jax.numpy as jnp
from jax import lax
from jax.experimental import pallas as pl
from jax.experimental.pallas import tpu as pltpu
from jax.sharding import PartitionSpec as P

F32 = jnp.float32
BF16 = jnp.bfloat16
MESH = pl.DeviceIdType.MESH


def column_shift(flat, cols, step):
    total = flat.shape[0]
    rolled = pltpu.roll(flat, step % total, 0)
    place = lax.broadcasted_iota(jnp.int32, flat.shape, 0) % cols
    edge = 0 if step > 0 else cols - 1
    return jnp.where(place == edge, 0.0, rolled)


def kernel(
    frames, tiles,
    lat_hbm, gain_hbm, cb_hbm, tb_hbm, ub_hbm, cw_hbm, tw_hbm, uw_hbm,
    out_ref,
    lat, act, act_hist, act_relay, parts, part_in, blk, blk_hist, dbl,
    gain_ref, cb_ref, tb_ref, ub_ref, cw, tw, uw, umat, acc, mixed, edge, wide_lo, wide_hi,
    lat_sem, bias_sem, cw_sem, tw_sem, uw_sem,
    a_send, a_recv, a_fsend, r_send, r_recv, b_send, b_recv, b_fsend,
    p_down_sem, p_up_sem, b_down_sem, b_up_sem, d_up_sem,
):
    rows, cols, chans = lat.shape
    outs_n = uw.shape[2]
    low = 128
    high = outs_n - low
    cells = rows * cols
    t = lax.axis_index("tm")
    s = lax.axis_index("tile")
    odd = lax.rem(t, 2) == 1
    even = jnp.logical_not(odd)
    has_next = t + 2 < frames
    has_prev = t >= 2
    has_near = t >= 1
    starts = t < 2
    later = t >= 2
    has_up = s > 0
    has_down = s < tiles - 1

    lat_copy = pltpu.make_async_copy(lat_hbm.at[0], lat, lat_sem)
    lat_copy.start()
    bias_copies = []
    for k, (src, dst) in enumerate(
        ((gain_hbm, gain_ref), (cb_hbm, cb_ref), (tb_hbm, tb_ref), (ub_hbm, ub_ref))
    ):
        copy = pltpu.make_async_copy(src, dst, bias_sem.at[k])
        copy.start()
        bias_copies.append(copy)
    half = frames // 2
    partner = s + 1 - 2 * lax.rem(s, 2)
    relays = t // 2 == half // 2 - 1
    relayed = t // 2 == half // 2
    direct = jnp.logical_and(has_next, jnp.logical_not(relays))

    sibling = t + 1 - 2 * lax.rem(t, 2)
    barrier = pltpu.get_barrier_semaphore()

    def greet(condition, where):
        @pl.when(condition)
        def _():
            pl.semaphore_signal(barrier, inc=1, device_id=where, device_id_type=MESH)

    pl.semaphore_signal(barrier, inc=1, device_id={"tm": sibling}, device_id_type=MESH)
    greet(has_next, {"tm": t + 2})
    greet(has_prev, {"tm": t - 2})
    greet(relays, {"tm": t + 2, "tile": partner})
    greet(relayed, {"tm": t - 2, "tile": partner})
    greet(has_up, {"tile": s - 1})
    greet(has_down, {"tile": s + 1})

    cw_copies = {}
    for dt in (2, 0, 1):
        for dh in range(3):
            copy = pltpu.make_async_copy(
                cw_hbm.at[dt, dh],
                cw.at[dt, :, :, pl.ds(dh * chans, chans)],
                cw_sem.at[dt, dh],
            )
            copy.start()
            cw_copies[dt, dh] = copy
    tw_copy = pltpu.make_async_copy(tw_hbm, tw, tw_sem)
    tw_copy.start()
    uw_copy = pltpu.make_async_copy(uw_hbm, uw, uw_sem)
    uw_copy.start()

    def history_copies(own, hist, send, recv, fsend):
        def nearer(r):
            return pltpu.make_async_remote_copy(
                own.at[r], hist.at[1, r], send.at[0, r], recv.at[1, r],
                device_id={"tm": sibling}, device_id_type=MESH,
            )

        def farther(r):
            return pltpu.make_async_remote_copy(
                own.at[r], hist.at[0, r], send.at[1, r], recv.at[0, r],
                device_id={"tm": t + 2}, device_id_type=MESH,
            )

        def forward(r):
            return pltpu.make_async_remote_copy(
                hist.at[0, r], hist.at[1, r], fsend.at[r], recv.at[1, r],
                device_id={"tm": sibling}, device_id_type=MESH,
            )

        return nearer, farther, forward

    def history_start(copies, r, sends=has_next):
        nearer, farther, _ = copies

        @pl.when(sends)
        def _():
            farther(r).start()

        @pl.when(even)
        def _():
            nearer(r).start()

    def history_far(copies, r):
        _, farther, forward = copies
        farther(r).wait_recv()

        @pl.when(odd)
        def _():
            forward(r).start()

    def history_near(copies, r):
        copies[0](r).wait_recv()

    def history_end(copies, r, sends=has_next):
        nearer, farther, forward = copies

        @pl.when(sends)
        def _():
            farther(r).wait_send()

        @pl.when(even)
        def _():
            nearer(r).wait_send()

        @pl.when(jnp.logical_and(odd, has_prev))
        def _():
            forward(r).wait_send()

    def to_tile(src, dst, sems, where):
        return pltpu.make_async_remote_copy(
            src, dst, sems.at[0], sems.at[1], device_id={"tile": where}, device_id_type=MESH
        )

    first, last = 0, rows - 1
    act_copies = history_copies(act, act_hist, a_send, a_recv, a_fsend)
    blk_copies = history_copies(blk, blk_hist, b_send, b_recv, b_fsend)
    part_down = to_tile(parts.at[1], part_in.at[0], p_down_sem, s + 1)
    part_up = to_tile(parts.at[0], part_in.at[1], p_up_sem, s - 1)
    blk_down = to_tile(blk.at[rows], blk.at[0], b_down_sem, s + 1)
    blk_up = to_tile(blk.at[1], blk.at[rows + 1], b_up_sem, s - 1)
    dbl_up = to_tile(dbl.at[1], dbl.at[rows + 1], d_up_sem, s - 1)

    def activate(r):
        values = lat[r].astype(F32)
        meansq = jnp.mean(values * values, axis=-1, keepdims=True)
        scaled = values * lax.rsqrt(meansq + 1e-06) * gain_ref[...].reshape(1, chans)
        act[r] = (scaled * jax.nn.sigmoid(scaled)).astype(BF16)

    peers = 1
    for condition in (has_next, has_prev, relays, relayed, has_up, has_down):
        peers = peers + condition.astype(jnp.int32)

    def to_partner(r):
        return pltpu.make_async_remote_copy(
            act.at[r], act_relay.at[r], r_send.at[0, r], r_recv.at[r],
            device_id={"tile": partner}, device_id_type=MESH,
        )

    def from_partner(r):
        return pltpu.make_async_remote_copy(
            act_relay.at[r], act_hist.at[0, r], r_send.at[1, r], a_recv.at[0, r],
            device_id={"tm": t + 2, "tile": partner}, device_id_type=MESH,
        )

    order = tuple(range(rows))[::-1]
    lat_copy.wait()
    for copy in bias_copies:
        copy.wait()
    for r in order:
        activate(r)
        if r == order[0]:
            pl.semaphore_wait(barrier, peers)
        if r == order[0]:
            history_start(act_copies, r)
        else:
            @pl.when(relays)
            def _():
                to_partner(r).start()

            history_start(act_copies, r, direct)

    def widen(frame):
        flat = frame.reshape(-1, chans)
        wide = flat.astype(F32)
        before = column_shift(wide, cols, 1).astype(BF16)
        after = column_shift(wide, cols, -1).astype(BF16)
        return jnp.concatenate([before, flat, after], axis=1)

    def conv(stacked, dt, start, size):
        taps = cw.at[dt, :, :, pl.ds(start, size)][...].reshape(3 * chans, size)
        return jnp.dot(stacked, taps, preferred_element_type=F32)

    def weights_ready(dt):
        for dh in range(3):
            cw_copies[dt, dh].wait()

    weights_ready(2)
    acc[...] = conv(widen(act[...]), 2, 0, 3 * chans)
    @pl.when(relays)
    def _():
        for r in order[1:]:
            to_partner(r).wait_recv()
            from_partner(r).start()

    def sum_taps():
        uw_copy.wait()
        row_sets = {(0, 0): (0,), (0, 1): (1, 2), (1, 0): (0, 1), (1, 1): (2,)}
        for (a, i), picks in row_sets.items():
            taps = []
            for kw in range(3):
                tap = uw[picks[0], kw].astype(F32)
                for kh in picks[1:]:
                    tap = tap + uw[kh, kw].astype(F32)
                taps.append(tap)
            center = (taps[1] + taps[2], taps[0] + taps[1])
            sides = (taps[0], taps[2])
            lanes = pl.ds(i * chans, chans)
            for base, pair in ((0, center), (2 * outs_n, sides)):
                for b in range(2):
                    value = pair[b].astype(BF16)
                    umat[a, pl.ds(base + b * low, low), lanes] = value[:low]
                    umat[a, pl.ds(base + 2 * low + b * high, high), lanes] = value[low:]

    @pl.when(later)
    def _():
        sum_taps()
        weights_ready(0)
        weights_ready(1)

    for r in order:
        span = pl.ds(r * cols, cols)
        goes, stays = (0, chans) if r == last else (2 * chans, 0)
        out_part = 1 if r == last else 0

        @pl.when(has_prev)
        def _():
            history_far(act_copies, r)
            acc[span, :] += conv(widen(act_hist[0, r]), 0, 0, 3 * chans)

        @pl.when(has_near)
        def _():
            if r == order[0]:
                @pl.when(starts)
                def _():
                    weights_ready(1)

            history_near(act_copies, r)
            acc[span, pl.ds(goes, chans)] += conv(widen(act_hist[1, r]), 1, goes, chans)

        parts[out_part] = acc[span, pl.ds(goes, chans)].astype(BF16)
        if r == last:
            @pl.when(has_down)
            def _():
                part_down.start()
        else:
            @pl.when(has_up)
            def _():
                part_up.start()

        @pl.when(has_near)
        def _():
            acc[span, pl.ds(stays, 2 * chans)] += conv(widen(act_hist[1, r]), 1, stays, 2 * chans)

    def finish_row(r):
        total = acc[pl.ds(r * cols, cols), pl.ds(chans, chans)]
        if r > 0:
            total = total + acc[pl.ds((r - 1) * cols, cols), pl.ds(0, chans)]
        if r < rows - 1:
            total = total + acc[pl.ds((r + 1) * cols, cols), pl.ds(2 * chans, chans)]
        total = total + cb_ref[...].reshape(1, chans) + lat[r].astype(F32)
        if r == first:
            total = total + part_in[0].astype(F32)
        if r == last:
            total = total + part_in[1].astype(F32)
        blk[1 + r] = total.astype(BF16)

    tw_copy.wait()

    def mix(row, k):
        return jnp.dot(row, tw[k], preferred_element_type=F32)

    def newest(j):
        mixed[j] = mix(blk[j], 2) + tb_ref[...].reshape(1, 2 * chans)

    def mix_far(j):
        @pl.when(has_prev)
        def _():
            history_far(blk_copies, j)
            mixed[j] += mix(blk_hist[0, j], 0)

    def mix_near(j):
        @pl.when(has_near)
        def _():
            history_near(blk_copies, j)
            mixed[j] += mix(blk_hist[1, j], 1)

        for f in range(2):
            dbl[j, f] = mixed[j, :, pl.ds(f * chans, chans)].astype(BF16)

    def taps_dot(row, a, start, size):
        return lax.dot_general(
            row, umat[a, :, pl.ds(start, size)], (((1,), (1,)), ((), ())), preferred_element_type=F32
        )

    def stored_row(j):
        return dbl[j].reshape(2 * cols, chans)

    @pl.when(has_up)
    def _():
        part_down.wait_recv()

    @pl.when(jnp.logical_not(has_up))
    def _():
        part_in[0] = jnp.zeros((cols, chans), BF16)

    for r in range(rows - 1):
        finish_row(r)

        if r == first:
            @pl.when(has_up & starts)
            def _():
                blk_up.start()

        history_start(blk_copies, 1 + r)
        newest(1 + r)

    @pl.when(has_down)
    def _():
        part_up.wait_recv()

    @pl.when(jnp.logical_not(has_down))
    def _():
        part_in[1] = jnp.zeros((cols, chans), BF16)

    finish_row(last)

    @pl.when(has_down)
    def _():
        blk_down.start()

    history_start(blk_copies, rows)

    @pl.when(starts)
    def _():
        sum_taps()
        weights_ready(0)

        @pl.when(t == 0)
        def _():
            weights_ready(1)

    newest(rows)

    for r in range(rows):
        if r == last:
            @pl.when(has_up)
            def _():
                blk_down.wait_recv()
                history_start(blk_copies, 0)

        mix_far(1 + r)
        mix_near(1 + r)
        if r == first:
            @pl.when(has_up & later)
            def _():
                dbl_up.start()

            @pl.when(has_down & (t == 0))
            def _():
                blk_up.wait_recv()
                blk_copies[0](rows + 1).start()

            edge[0] = taps_dot(stored_row(1), 0, chans, chans)

    bias_row = ub_ref[...].reshape(1, outs_n)
    up_bias = jnp.concatenate(
        [bias_row[:, :low], bias_row[:, :low], bias_row[:, low:], bias_row[:, low:]], axis=1
    )

    def upsample_row(a, r, result):
        center = result[:, : 2 * outs_n] + up_bias
        sides = result[:, 2 * outs_n :]
        even = center[:, :low] + column_shift(sides[:, :low], cols, 1)
        uneven = center[:, low : 2 * low] + column_shift(sides[:, low : 2 * low], cols, -1)
        tail = sides[:, 2 * low :]
        lane = lax.broadcasted_iota(jnp.int32, tail.shape, 1)
        tail = center[:, 2 * low :] + jnp.where(
            lane < high, column_shift(tail, cols, 1), column_shift(tail, cols, -1)
        )
        swapped = pltpu.roll(tail, high, 1)
        for f in range(2):
            span = slice(f * cols, (f + 1) * cols)
            wide_lo[pl.ds(0, cols, stride=2), :] = even[span]
            wide_lo[pl.ds(1, cols, stride=2), :] = uneven[span]
            wide_hi[pl.ds(0, cols, stride=2), :] = tail[span]
            wide_hi[pl.ds(1, cols, stride=2), :] = swapped[span]
            out_ref[f, 2 * r + a, pl.ds(0, low), :] = wide_lo[...].T.astype(BF16)
            out_ref[f, 2 * r + a, pl.ds(low, high), :] = wide_hi[...].T[:high].astype(BF16)

    for r in range(rows):
        for a in range(2):
            if 0 < r + a < rows:
                both = jnp.concatenate([stored_row(r + a), stored_row(r + a + 1)], axis=1)
                upsample_row(a, r, taps_dot(both, a, 0, 2 * chans))

    @pl.when(has_up)
    def _():
        newest(0)
        mix_far(0)

    edge[1] = taps_dot(stored_row(rows), 1, 0, chans)

    @pl.when(has_down & starts)
    def _():
        @pl.when(t == 1)
        def _():
            blk_up.wait_recv()

        newest(rows + 1)

        @pl.when(t == 1)
        def _():
            history_near(blk_copies, rows + 1)
            mixed[rows + 1] += mix(blk_hist[1, rows + 1], 1)

        for f in range(2):
            dbl[rows + 1, f] = mixed[rows + 1, :, pl.ds(f * chans, chans)].astype(BF16)

    @pl.when(has_down & later)
    def _():
        dbl_up.wait_recv()

    @pl.when(has_down)
    def _():
        edge[1] += taps_dot(stored_row(rows + 1), 1, chans, chans)

    upsample_row(1, last, edge[1])

    @pl.when(has_up)
    def _():
        mix_near(0)
        edge[0] += taps_dot(stored_row(0), 0, 0, chans)

    upsample_row(0, 0, edge[0])

    for r in range(rows):
        history_end(act_copies, r, has_next if r == order[0] else direct)
        history_end(blk_copies, 1 + r)

    @pl.when(relays)
    def _():
        for r in order[1:]:
            to_partner(r).wait_send()
            from_partner(r).wait_send()

    @pl.when(has_up)
    def _():
        history_end(blk_copies, 0)
        part_up.wait_send()

        @pl.when(later)
        def _():
            dbl_up.wait_send()

        @pl.when(starts)
        def _():
            blk_up.wait_send()

    @pl.when(has_down)
    def _():
        part_down.wait_send()
        blk_down.wait_send()

        @pl.when(t == 0)
        def _():
            blk_copies[0](rows + 1).wait_send()


def local(frames, tiles, latent, gain, conv_weight, conv_bias, time_weight, time_bias, up_weight, up_bias):
    _, rows, cols, chans = latent.shape
    outs_n = up_weight.shape[3]
    low = 128
    dma = pltpu.SemaphoreType.DMA
    row = (cols, chans)
    transposed = pl.pallas_call(
        functools.partial(kernel, frames, tiles),
        out_shape=jax.ShapeDtypeStruct((2, 2 * rows, outs_n, 2 * cols), BF16),
        in_specs=[pl.BlockSpec(memory_space=pltpu.HBM)] * 8,
        out_specs=pl.BlockSpec(memory_space=pltpu.VMEM),
        scratch_shapes=[
            pltpu.VMEM((rows,) + row, BF16),
            pltpu.VMEM((rows,) + row, BF16),
            pltpu.VMEM((2, rows) + row, BF16),
            pltpu.VMEM((rows,) + row, BF16),
            pltpu.VMEM((2,) + row, BF16),
            pltpu.VMEM((2,) + row, BF16),
            pltpu.VMEM((rows + 2,) + row, BF16),
            pltpu.VMEM((2, rows + 2) + row, BF16),
            pltpu.VMEM((rows + 2, 2) + row, BF16),
            pltpu.VMEM((chans,), F32),
            pltpu.VMEM((chans,), F32),
            pltpu.VMEM((2 * chans,), F32),
            pltpu.VMEM((outs_n,), F32),
            pltpu.VMEM((3, 3, chans, 3 * chans), BF16),
            pltpu.VMEM((3, chans, 2 * chans), BF16),
            pltpu.VMEM((3, 3, outs_n, chans), BF16),
            pltpu.VMEM((2, 4 * outs_n, 2 * chans), BF16),
            pltpu.VMEM((rows * cols, 3 * chans), F32),
            pltpu.VMEM((rows + 2, cols, 2 * chans), F32),
            pltpu.VMEM((2, 2 * cols, 4 * outs_n), F32),
            pltpu.VMEM((2 * cols, low), F32),
            pltpu.VMEM((2 * cols, low), F32),
            dma(()), dma((4,)), dma((3, 3)), dma(()), dma(()),
            dma((2, rows)), dma((2, rows)), dma((rows,)),
            dma((2, rows)), dma((rows,)),
            dma((2, rows + 2)), dma((2, rows + 2)), dma((rows + 2,)),
            dma((2,)), dma((2,)), dma((2,)), dma((2,)), dma((2,)),
        ],
        compiler_params=pltpu.CompilerParams(
            collective_id=0, has_side_effects=True, vmem_limit_bytes=48 * 1024 * 1024
        ),
    )(*(
        pltpu.with_memory_space_constraint(array, pltpu.HBM)
        for array in (
            latent, gain, conv_bias, time_bias, up_bias,
            conv_weight, time_weight, jnp.swapaxes(up_weight, 2, 3),
        )
    ))
    return jnp.swapaxes(transposed, 2, 3)


def solution(mesh):
    placed = (P("tm", "tile", None, None), P(), P(), P(), P(), P(), P(), P())
    return jax.shard_map(
        functools.partial(local, mesh.shape["tm"], mesh.shape["tile"]),
        mesh=mesh, in_specs=placed, out_specs=P("tm", "tile", None, None), check_vma=False,
    )
```

```python
import functools

import jax
import jax.numpy as jnp
from jax import lax
from jax.experimental import pallas as pl
from jax.experimental.pallas import tpu as pltpu
from jax.sharding import PartitionSpec as P

F32 = jnp.float32
BF16 = jnp.bfloat16
MESH = pl.DeviceIdType.MESH


def column_shift(flat, cols, step):
    total = flat.shape[0]
    rolled = pltpu.roll(flat, step % total, 0)
    place = lax.broadcasted_iota(jnp.int32, flat.shape, 0) % cols
    edge = 0 if step > 0 else cols - 1
    return jnp.where(place == edge, 0.0, rolled)


def kernel(
    frames, tiles,
    lat_hbm, gain_hbm, cb_hbm, tb_hbm, ub_hbm, cw_hbm, tw_hbm, uw_hbm,
    out_ref,
    lat, act, act_hist, act_relay, parts, part_in, blk, blk_hist, dbl,
    gain_ref, cb_ref, tb_ref, ub_ref, cw, tw, uw, umat, acc, mixed, edge, wide_lo, wide_hi,
    lat_sem, bias_sem, cw_sem, tw_sem, uw_sem,
    a_send, a_recv, a_fsend, r_send, r_recv, b_send, b_recv, b_fsend,
    p_down_sem, p_up_sem, b_down_sem, b_up_sem, d_up_sem,
):
    rows, cols, chans = lat.shape
    outs_n = uw.shape[2]
    low = 128
    high = outs_n - low
    cells = rows * cols
    t = lax.axis_index("tm")
    s = lax.axis_index("tile")
    parity = lax.rem(t, 2)
    odd = parity == 1
    even = jnp.logical_not(odd)
    following = t + 2 - parity
    has_next = following < frames
    has_prev = t >= 2
    has_near = t >= 1
    starts = t < 2
    later = t >= 2
    has_up = s > 0
    has_down = s < tiles - 1

    lat_copy = pltpu.make_async_copy(lat_hbm.at[0], lat, lat_sem)
    lat_copy.start()
    bias_copies = []
    for k, (src, dst) in enumerate(
        ((gain_hbm, gain_ref), (cb_hbm, cb_ref), (tb_hbm, tb_ref), (ub_hbm, ub_ref))
    ):
        copy = pltpu.make_async_copy(src, dst, bias_sem.at[k])
        copy.start()
        bias_copies.append(copy)
    half = frames // 2
    partner = s + 1 - 2 * lax.rem(s, 2)
    relays = t // 2 == half // 2 - 1
    relayed = t == half
    receives = jnp.logical_and(even, t >= 2)
    direct = jnp.logical_and(has_next, jnp.logical_not(relays))

    sibling = t + 1 - 2 * lax.rem(t, 2)
    barrier = pltpu.get_barrier_semaphore()

    def greet(condition, where):
        @pl.when(condition)
        def _():
            pl.semaphore_signal(barrier, inc=1, device_id=where, device_id_type=MESH)

    pl.semaphore_signal(barrier, inc=1, device_id={"tm": sibling}, device_id_type=MESH)
    greet(has_next, {"tm": following})
    greet(receives, {"tm": t - 2})
    greet(receives, {"tm": t - 1})
    greet(relays, {"tm": following, "tile": partner})
    greet(relayed, {"tm": t - 2, "tile": partner})
    greet(relayed, {"tm": t - 1, "tile": partner})
    greet(has_up, {"tile": s - 1})
    greet(has_down, {"tile": s + 1})

    cw_copies = {}
    for dt in (2, 0, 1):
        for dh in range(3):
            copy = pltpu.make_async_copy(
                cw_hbm.at[dt, dh],
                cw.at[dt, :, :, pl.ds(dh * chans, chans)],
                cw_sem.at[dt, dh],
            )
            copy.start()
            cw_copies[dt, dh] = copy
    tw_copy = pltpu.make_async_copy(tw_hbm, tw, tw_sem)
    tw_copy.start()
    uw_copy = pltpu.make_async_copy(uw_hbm, uw, uw_sem)
    uw_copy.start()

    def history_copies(own, hist, send, recv, fsend):
        def nearer(r):
            return pltpu.make_async_remote_copy(
                own.at[r], hist.at[1, r], send.at[0, r], recv.at[1, r],
                device_id={"tm": sibling}, device_id_type=MESH,
            )

        def farther(r):
            return pltpu.make_async_remote_copy(
                own.at[r], hist.at[parity, r], send.at[1, r], recv.at[parity, r],
                device_id={"tm": following}, device_id_type=MESH,
            )

        def forward(r):
            return pltpu.make_async_remote_copy(
                hist.at[1, r], hist.at[0, r], fsend.at[r], recv.at[0, r],
                device_id={"tm": sibling}, device_id_type=MESH,
            )

        return nearer, farther, forward

    def history_start(copies, r, sends=has_next):
        nearer, farther, _ = copies

        @pl.when(sends)
        def _():
            farther(r).start()

        @pl.when(even)
        def _():
            nearer(r).start()

    def history_near(copies, r):
        nearer, _, forward = copies
        nearer(r).wait_recv()

        @pl.when(receives)
        def _():
            forward(r).start()

    def history_far(copies, r):
        copies[2](r).wait_recv()

    def history_end(copies, r, sends=has_next):
        nearer, farther, forward = copies

        @pl.when(sends)
        def _():
            farther(r).wait_send()

        @pl.when(even)
        def _():
            nearer(r).wait_send()

        @pl.when(receives)
        def _():
            forward(r).wait_send()

    def to_tile(src, dst, sems, where):
        return pltpu.make_async_remote_copy(
            src, dst, sems.at[0], sems.at[1], device_id={"tile": where}, device_id_type=MESH
        )

    first, last = 0, rows - 1
    act_copies = history_copies(act, act_hist, a_send, a_recv, a_fsend)
    blk_copies = history_copies(blk, blk_hist, b_send, b_recv, b_fsend)
    part_down = to_tile(parts.at[1], part_in.at[0], p_down_sem, s + 1)
    part_up = to_tile(parts.at[0], part_in.at[1], p_up_sem, s - 1)
    blk_down = to_tile(blk.at[rows], blk.at[0], b_down_sem, s + 1)
    blk_up = to_tile(blk.at[1], blk.at[rows + 1], b_up_sem, s - 1)
    dbl_up = to_tile(dbl.at[1], dbl.at[rows + 1], d_up_sem, s - 1)

    def activate(r):
        values = lat[r].astype(F32)
        meansq = jnp.mean(values * values, axis=-1, keepdims=True)
        scaled = values * lax.rsqrt(meansq + 1e-06) * gain_ref[...].reshape(1, chans)
        act[r] = (scaled * jax.nn.sigmoid(scaled)).astype(BF16)

    peers = 1
    for condition in (has_next, receives, receives, relays, relayed, relayed, has_up, has_down):
        peers = peers + condition.astype(jnp.int32)

    def to_partner(r):
        return pltpu.make_async_remote_copy(
            act.at[r], act_relay.at[r], r_send.at[0, r], r_recv.at[r],
            device_id={"tile": partner}, device_id_type=MESH,
        )

    def from_partner(r):
        return pltpu.make_async_remote_copy(
            act_relay.at[r], act_hist.at[parity, r], r_send.at[1, r], a_recv.at[parity, r],
            device_id={"tm": following, "tile": partner}, device_id_type=MESH,
        )

    order = tuple(range(rows))[::-1]
    lat_copy.wait()
    for copy in bias_copies:
        copy.wait()
    for r in order:
        activate(r)
        if r == order[0]:
            pl.semaphore_wait(barrier, peers)
        if r == order[0]:
            history_start(act_copies, r)
        else:
            @pl.when(relays)
            def _():
                to_partner(r).start()

            history_start(act_copies, r, direct)

    def widen(frame):
        flat = frame.reshape(-1, chans)
        wide = flat.astype(F32)
        before = column_shift(wide, cols, 1).astype(BF16)
        after = column_shift(wide, cols, -1).astype(BF16)
        return jnp.concatenate([before, flat, after], axis=1)

    def conv(stacked, dt, start, size):
        taps = cw.at[dt, :, :, pl.ds(start, size)][...].reshape(3 * chans, size)
        return jnp.dot(stacked, taps, preferred_element_type=F32)

    def weights_ready(dt):
        for dh in range(3):
            cw_copies[dt, dh].wait()

    weights_ready(2)
    acc[...] = conv(widen(act[...]), 2, 0, 3 * chans)
    @pl.when(relays)
    def _():
        for r in order[1:]:
            to_partner(r).wait_recv()
            from_partner(r).start()

    def sum_taps():
        uw_copy.wait()
        row_sets = {(0, 0): (0,), (0, 1): (1, 2), (1, 0): (0, 1), (1, 1): (2,)}
        for (a, i), picks in row_sets.items():
            taps = []
            for kw in range(3):
                tap = uw[picks[0], kw].astype(F32)
                for kh in picks[1:]:
                    tap = tap + uw[kh, kw].astype(F32)
                taps.append(tap)
            center = (taps[1] + taps[2], taps[0] + taps[1])
            sides = (taps[0], taps[2])
            lanes = pl.ds(i * chans, chans)
            for base, pair in ((0, center), (2 * outs_n, sides)):
                for b in range(2):
                    value = pair[b].astype(BF16)
                    umat[a, pl.ds(base + b * low, low), lanes] = value[:low]
                    umat[a, pl.ds(base + 2 * low + b * high, high), lanes] = value[low:]

    @pl.when(later)
    def _():
        sum_taps()
        weights_ready(0)
        weights_ready(1)

    for r in order:
        span = pl.ds(r * cols, cols)
        goes, stays = (0, chans) if r == last else (2 * chans, 0)
        out_part = 1 if r == last else 0

        @pl.when(has_near)
        def _():
            if r == order[0]:
                @pl.when(starts)
                def _():
                    weights_ready(1)

            history_near(act_copies, r)
            acc[span, :] += conv(widen(act_hist[1, r]), 1, 0, 3 * chans)

        @pl.when(has_prev)
        def _():
            history_far(act_copies, r)
            acc[span, pl.ds(goes, chans)] += conv(widen(act_hist[0, r]), 0, goes, chans)

        parts[out_part] = acc[span, pl.ds(goes, chans)].astype(BF16)
        if r == last:
            @pl.when(has_down)
            def _():
                part_down.start()
        else:
            @pl.when(has_up)
            def _():
                part_up.start()

        @pl.when(has_prev)
        def _():
            acc[span, pl.ds(stays, 2 * chans)] += conv(widen(act_hist[0, r]), 0, stays, 2 * chans)

    def finish_row(r):
        total = acc[pl.ds(r * cols, cols), pl.ds(chans, chans)]
        if r > 0:
            total = total + acc[pl.ds((r - 1) * cols, cols), pl.ds(0, chans)]
        if r < rows - 1:
            total = total + acc[pl.ds((r + 1) * cols, cols), pl.ds(2 * chans, chans)]
        total = total + cb_ref[...].reshape(1, chans) + lat[r].astype(F32)
        if r == first:
            total = total + part_in[0].astype(F32)
        if r == last:
            total = total + part_in[1].astype(F32)
        blk[1 + r] = total.astype(BF16)

    tw_copy.wait()

    def mix(row, k):
        return jnp.dot(row, tw[k], preferred_element_type=F32)

    def newest(j):
        mixed[j] = mix(blk[j], 2) + tb_ref[...].reshape(1, 2 * chans)

    def mix_near(j):
        @pl.when(has_near)
        def _():
            history_near(blk_copies, j)
            mixed[j] += mix(blk_hist[1, j], 1)

    def mix_far(j):
        @pl.when(has_prev)
        def _():
            history_far(blk_copies, j)
            mixed[j] += mix(blk_hist[0, j], 0)

        for f in range(2):
            dbl[j, f] = mixed[j, :, pl.ds(f * chans, chans)].astype(BF16)

    def taps_dot(row, a, start, size):
        return lax.dot_general(
            row, umat[a, :, pl.ds(start, size)], (((1,), (1,)), ((), ())), preferred_element_type=F32
        )

    def stored_row(j):
        return dbl[j].reshape(2 * cols, chans)

    @pl.when(has_up)
    def _():
        part_down.wait_recv()

    @pl.when(jnp.logical_not(has_up))
    def _():
        part_in[0] = jnp.zeros((cols, chans), BF16)

    for r in range(rows - 1):
        finish_row(r)

        if r == first:
            @pl.when(has_up & starts)
            def _():
                blk_up.start()

        history_start(blk_copies, 1 + r)
        newest(1 + r)

    @pl.when(has_down)
    def _():
        part_up.wait_recv()

    @pl.when(jnp.logical_not(has_down))
    def _():
        part_in[1] = jnp.zeros((cols, chans), BF16)

    finish_row(last)

    @pl.when(has_down)
    def _():
        blk_down.start()

    history_start(blk_copies, rows)

    @pl.when(starts)
    def _():
        sum_taps()
        weights_ready(0)

        @pl.when(t == 0)
        def _():
            weights_ready(1)

    newest(rows)

    for r in range(rows):
        if r == last:
            @pl.when(has_up)
            def _():
                blk_down.wait_recv()
                history_start(blk_copies, 0)

        mix_near(1 + r)
        mix_far(1 + r)
        if r == first:
            @pl.when(has_up & later)
            def _():
                dbl_up.start()

            @pl.when(has_down & (t == 0))
            def _():
                blk_up.wait_recv()
                blk_copies[0](rows + 1).start()

            edge[0] = taps_dot(stored_row(1), 0, chans, chans)

    bias_row = ub_ref[...].reshape(1, outs_n)
    up_bias = jnp.concatenate(
        [bias_row[:, :low], bias_row[:, :low], bias_row[:, low:], bias_row[:, low:]], axis=1
    )

    def upsample_row(a, r, result):
        center = result[:, : 2 * outs_n] + up_bias
        sides = result[:, 2 * outs_n :]
        even = center[:, :low] + column_shift(sides[:, :low], cols, 1)
        uneven = center[:, low : 2 * low] + column_shift(sides[:, low : 2 * low], cols, -1)
        tail = sides[:, 2 * low :]
        lane = lax.broadcasted_iota(jnp.int32, tail.shape, 1)
        tail = center[:, 2 * low :] + jnp.where(
            lane < high, column_shift(tail, cols, 1), column_shift(tail, cols, -1)
        )
        swapped = pltpu.roll(tail, high, 1)
        for f in range(2):
            span = slice(f * cols, (f + 1) * cols)
            wide_lo[pl.ds(0, cols, stride=2), :] = even[span]
            wide_lo[pl.ds(1, cols, stride=2), :] = uneven[span]
            wide_hi[pl.ds(0, cols, stride=2), :] = tail[span]
            wide_hi[pl.ds(1, cols, stride=2), :] = swapped[span]
            out_ref[f, 2 * r + a, pl.ds(0, low), :] = wide_lo[...].T.astype(BF16)
            out_ref[f, 2 * r + a, pl.ds(low, high), :] = wide_hi[...].T[:high].astype(BF16)

    for r in range(rows):
        for a in range(2):
            if 0 < r + a < rows:
                both = jnp.concatenate([stored_row(r + a), stored_row(r + a + 1)], axis=1)
                upsample_row(a, r, taps_dot(both, a, 0, 2 * chans))

    @pl.when(has_up)
    def _():
        newest(0)
        mix_near(0)

    edge[1] = taps_dot(stored_row(rows), 1, 0, chans)

    @pl.when(has_down & starts)
    def _():
        @pl.when(t == 1)
        def _():
            blk_up.wait_recv()

        newest(rows + 1)

        @pl.when(t == 1)
        def _():
            history_near(blk_copies, rows + 1)
            mixed[rows + 1] += mix(blk_hist[1, rows + 1], 1)

        for f in range(2):
            dbl[rows + 1, f] = mixed[rows + 1, :, pl.ds(f * chans, chans)].astype(BF16)

    @pl.when(has_down & later)
    def _():
        dbl_up.wait_recv()

    @pl.when(has_down)
    def _():
        edge[1] += taps_dot(stored_row(rows + 1), 1, chans, chans)

    upsample_row(1, last, edge[1])

    @pl.when(has_up)
    def _():
        mix_far(0)
        edge[0] += taps_dot(stored_row(0), 0, 0, chans)

    upsample_row(0, 0, edge[0])

    for r in range(rows):
        history_end(act_copies, r, has_next if r == order[0] else direct)
        history_end(blk_copies, 1 + r)

    @pl.when(relays)
    def _():
        for r in order[1:]:
            to_partner(r).wait_send()
            from_partner(r).wait_send()

    @pl.when(has_up)
    def _():
        history_end(blk_copies, 0)
        part_up.wait_send()

        @pl.when(later)
        def _():
            dbl_up.wait_send()

        @pl.when(starts)
        def _():
            blk_up.wait_send()

    @pl.when(has_down)
    def _():
        part_down.wait_send()
        blk_down.wait_send()

        @pl.when(t == 0)
        def _():
            blk_copies[0](rows + 1).wait_send()


def local(frames, tiles, latent, gain, conv_weight, conv_bias, time_weight, time_bias, up_weight, up_bias):
    _, rows, cols, chans = latent.shape
    outs_n = up_weight.shape[3]
    low = 128
    dma = pltpu.SemaphoreType.DMA
    row = (cols, chans)
    transposed = pl.pallas_call(
        functools.partial(kernel, frames, tiles),
        out_shape=jax.ShapeDtypeStruct((2, 2 * rows, outs_n, 2 * cols), BF16),
        in_specs=[pl.BlockSpec(memory_space=pltpu.HBM)] * 8,
        out_specs=pl.BlockSpec(memory_space=pltpu.VMEM),
        scratch_shapes=[
            pltpu.VMEM((rows,) + row, BF16),
            pltpu.VMEM((rows,) + row, BF16),
            pltpu.VMEM((2, rows) + row, BF16),
            pltpu.VMEM((rows,) + row, BF16),
            pltpu.VMEM((2,) + row, BF16),
            pltpu.VMEM((2,) + row, BF16),
            pltpu.VMEM((rows + 2,) + row, BF16),
            pltpu.VMEM((2, rows + 2) + row, BF16),
            pltpu.VMEM((rows + 2, 2) + row, BF16),
            pltpu.VMEM((chans,), F32),
            pltpu.VMEM((chans,), F32),
            pltpu.VMEM((2 * chans,), F32),
            pltpu.VMEM((outs_n,), F32),
            pltpu.VMEM((3, 3, chans, 3 * chans), BF16),
            pltpu.VMEM((3, chans, 2 * chans), BF16),
            pltpu.VMEM((3, 3, outs_n, chans), BF16),
            pltpu.VMEM((2, 4 * outs_n, 2 * chans), BF16),
            pltpu.VMEM((rows * cols, 3 * chans), F32),
            pltpu.VMEM((rows + 2, cols, 2 * chans), F32),
            pltpu.VMEM((2, 2 * cols, 4 * outs_n), F32),
            pltpu.VMEM((2 * cols, low), F32),
            pltpu.VMEM((2 * cols, low), F32),
            dma(()), dma((4,)), dma((3, 3)), dma(()), dma(()),
            dma((2, rows)), dma((2, rows)), dma((rows,)),
            dma((2, rows)), dma((rows,)),
            dma((2, rows + 2)), dma((2, rows + 2)), dma((rows + 2,)),
            dma((2,)), dma((2,)), dma((2,)), dma((2,)), dma((2,)),
        ],
        compiler_params=pltpu.CompilerParams(
            collective_id=0, has_side_effects=True, vmem_limit_bytes=48 * 1024 * 1024
        ),
    )(*(
        pltpu.with_memory_space_constraint(array, pltpu.HBM)
        for array in (
            latent, gain, conv_bias, time_bias, up_bias,
            conv_weight, time_weight, jnp.swapaxes(up_weight, 2, 3),
        )
    ))
    return jnp.swapaxes(transposed, 2, 3)


def solution(mesh):
    placed = (P("tm", "tile", None, None), P(), P(), P(), P(), P(), P(), P())
    return jax.shard_map(
        functools.partial(local, mesh.shape["tm"], mesh.shape["tile"]),
        mesh=mesh, in_specs=placed, out_specs=P("tm", "tile", None, None), check_vma=False,
    )
```

```python
import functools

import jax
import jax.numpy as jnp
from jax import lax
from jax.experimental import pallas as pl
from jax.experimental.pallas import tpu as pltpu
from jax.sharding import PartitionSpec as P

F32 = jnp.float32
BF16 = jnp.bfloat16
MESH = pl.DeviceIdType.MESH


def column_shift(flat, cols, step):
    total = flat.shape[0]
    rolled = pltpu.roll(flat, step % total, 0)
    place = lax.broadcasted_iota(jnp.int32, flat.shape, 0) % cols
    edge = 0 if step > 0 else cols - 1
    return jnp.where(place == edge, 0.0, rolled)


def kernel(
    frames, tiles,
    lat_hbm, gain_hbm, cb_hbm, tb_hbm, ub_hbm, cw_hbm, tw_hbm, uw_hbm,
    out_ref,
    lat, act, act_hist, act_relay, parts, part_in, blk, blk_hist, dbl,
    gain_ref, cb_ref, tb_ref, ub_ref, cw, tw, uw, umat, acc, mixed, edge, wide_lo, wide_hi,
    lat_sem, bias_sem, cw_sem, tw_sem, uw_sem,
    a_send, a_recv, a_fsend, r_send, r_recv, b_send, b_recv, b_fsend,
    p_down_sem, p_up_sem, b_down_sem, b_up_sem, d_up_sem,
):
    rows, cols, chans = lat.shape
    outs_n = uw.shape[2]
    low = 128
    high = outs_n - low
    cells = rows * cols
    t = lax.axis_index("tm")
    s = lax.axis_index("tile")
    odd = lax.rem(t, 2) == 1
    even = jnp.logical_not(odd)
    has_next = t + 2 < frames
    has_prev = t >= 2
    has_near = t >= 1
    starts = t < 2
    later = t >= 2
    has_up = s > 0
    has_down = s < tiles - 1

    lat_copy = pltpu.make_async_copy(lat_hbm.at[0], lat, lat_sem)
    lat_copy.start()
    bias_copies = []
    for k, (src, dst) in enumerate(
        ((gain_hbm, gain_ref), (cb_hbm, cb_ref), (tb_hbm, tb_ref), (ub_hbm, ub_ref))
    ):
        copy = pltpu.make_async_copy(src, dst, bias_sem.at[k])
        copy.start()
        bias_copies.append(copy)
    half = frames // 2
    partner = s + 1 - 2 * lax.rem(s, 2)
    relays = t // 2 == half // 2 - 1
    relayed = t // 2 == half // 2
    direct = jnp.logical_and(has_next, jnp.logical_not(relays))

    sibling = t + 1 - 2 * lax.rem(t, 2)
    barrier = pltpu.get_barrier_semaphore()

    def greet(condition, where):
        @pl.when(condition)
        def _():
            pl.semaphore_signal(barrier, inc=1, device_id=where, device_id_type=MESH)

    pl.semaphore_signal(barrier, inc=1, device_id={"tm": sibling}, device_id_type=MESH)
    greet(has_next, {"tm": t + 2})
    greet(has_prev, {"tm": t - 2})
    greet(relays, {"tm": t + 2, "tile": partner})
    greet(relayed, {"tm": t - 2, "tile": partner})
    greet(has_up, {"tile": s - 1})
    greet(has_down, {"tile": s + 1})

    cw_copies = {}
    for dt in (2, 0, 1):
        for dh in range(3):
            copy = pltpu.make_async_copy(
                cw_hbm.at[dt, dh],
                cw.at[dt, :, :, pl.ds(dh * chans, chans)],
                cw_sem.at[dt, dh],
            )
            copy.start()
            cw_copies[dt, dh] = copy
    tw_copy = pltpu.make_async_copy(tw_hbm, tw, tw_sem)
    tw_copy.start()
    uw_copy = pltpu.make_async_copy(uw_hbm, uw, uw_sem)
    uw_copy.start()

    def history_copies(own, hist, send, recv, fsend):
        def nearer(r):
            return pltpu.make_async_remote_copy(
                own.at[r], hist.at[1, r], send.at[0, r], recv.at[1, r],
                device_id={"tm": sibling}, device_id_type=MESH,
            )

        def farther(r):
            return pltpu.make_async_remote_copy(
                own.at[r], hist.at[0, r], send.at[1, r], recv.at[0, r],
                device_id={"tm": t + 2}, device_id_type=MESH,
            )

        def forward(r):
            return pltpu.make_async_remote_copy(
                hist.at[0, r], hist.at[1, r], fsend.at[r], recv.at[1, r],
                device_id={"tm": sibling}, device_id_type=MESH,
            )

        return nearer, farther, forward

    def history_start(copies, r, sends=has_next):
        nearer, farther, _ = copies

        @pl.when(sends)
        def _():
            farther(r).start()

        @pl.when(even)
        def _():
            nearer(r).start()

    def history_far(copies, r):
        _, farther, forward = copies
        farther(r).wait_recv()

        @pl.when(odd)
        def _():
            forward(r).start()

    def history_near(copies, r):
        copies[0](r).wait_recv()

    def history_end(copies, r, sends=has_next):
        nearer, farther, forward = copies

        @pl.when(sends)
        def _():
            farther(r).wait_send()

        @pl.when(even)
        def _():
            nearer(r).wait_send()

        @pl.when(jnp.logical_and(odd, has_prev))
        def _():
            forward(r).wait_send()

    def to_tile(src, dst, sems, where):
        return pltpu.make_async_remote_copy(
            src, dst, sems.at[0], sems.at[1], device_id={"tile": where}, device_id_type=MESH
        )

    first, last = 0, rows - 1
    act_copies = history_copies(act, act_hist, a_send, a_recv, a_fsend)
    blk_copies = history_copies(blk, blk_hist, b_send, b_recv, b_fsend)
    part_down = to_tile(parts.at[1], part_in.at[0], p_down_sem, s + 1)
    part_up = to_tile(parts.at[0], part_in.at[1], p_up_sem, s - 1)
    blk_down = to_tile(blk.at[rows], blk.at[0], b_down_sem, s + 1)
    blk_up = to_tile(blk.at[1], blk.at[rows + 1], b_up_sem, s - 1)
    dbl_up = [to_tile(dbl.at[1, f], dbl.at[rows + 1, f], d_up_sem.at[f], s - 1) for f in range(2)]

    def activate(r):
        values = lat[r].astype(F32)
        meansq = jnp.mean(values * values, axis=-1, keepdims=True)
        scaled = values * lax.rsqrt(meansq + 1e-06) * gain_ref[...].reshape(1, chans)
        act[r] = (scaled * jax.nn.sigmoid(scaled)).astype(BF16)

    peers = 1
    for condition in (has_next, has_prev, relays, relayed, has_up, has_down):
        peers = peers + condition.astype(jnp.int32)

    def to_partner(r):
        return pltpu.make_async_remote_copy(
            act.at[r], act_relay.at[r], r_send.at[0, r], r_recv.at[r],
            device_id={"tile": partner}, device_id_type=MESH,
        )

    def from_partner(r):
        return pltpu.make_async_remote_copy(
            act_relay.at[r], act_hist.at[0, r], r_send.at[1, r], a_recv.at[0, r],
            device_id={"tm": t + 2, "tile": partner}, device_id_type=MESH,
        )

    order = tuple(range(rows))[::-1]
    lat_copy.wait()
    bias_copies[0].wait()
    for r in order:
        activate(r)
        if r == order[0]:
            pl.semaphore_wait(barrier, peers)
        if r == order[0]:
            history_start(act_copies, r)
        else:
            @pl.when(relays)
            def _():
                to_partner(r).start()

            history_start(act_copies, r, direct)

    def widen(frame):
        flat = frame.reshape(-1, chans)
        wide = flat.astype(F32)
        before = column_shift(wide, cols, 1).astype(BF16)
        after = column_shift(wide, cols, -1).astype(BF16)
        return jnp.concatenate([before, flat, after], axis=1)

    def conv(stacked, dt, start, size):
        taps = cw.at[dt, :, :, pl.ds(start, size)][...].reshape(3 * chans, size)
        return jnp.dot(stacked, taps, preferred_element_type=F32)

    def weights_ready(dt):
        for dh in range(3):
            cw_copies[dt, dh].wait()

    weights_ready(2)
    acc[...] = conv(widen(act[...]), 2, 0, 3 * chans)
    @pl.when(relays)
    def _():
        for r in order[1:]:
            to_partner(r).wait_recv()
            from_partner(r).start()

    def sum_taps():
        uw_copy.wait()
        row_sets = {(0, 0): (0,), (0, 1): (1, 2), (1, 0): (0, 1), (1, 1): (2,)}
        for (a, i), picks in row_sets.items():
            taps = []
            for kw in range(3):
                tap = uw[picks[0], kw].astype(F32)
                for kh in picks[1:]:
                    tap = tap + uw[kh, kw].astype(F32)
                taps.append(tap)
            center = (taps[1] + taps[2], taps[0] + taps[1])
            sides = (taps[0], taps[2])
            lanes = pl.ds(i * chans, chans)
            for base, pair in ((0, center), (2 * outs_n, sides)):
                for b in range(2):
                    value = pair[b].astype(BF16)
                    umat[a, pl.ds(base + b * low, low), lanes] = value[:low]
                    umat[a, pl.ds(base + 2 * low + b * high, high), lanes] = value[low:]

    @pl.when(later)
    def _():
        sum_taps()
        weights_ready(0)
        weights_ready(1)

    for r in order:
        span = pl.ds(r * cols, cols)
        goes, stays = (0, chans) if r == last else (2 * chans, 0)
        out_part = 1 if r == last else 0

        @pl.when(has_prev)
        def _():
            history_far(act_copies, r)
            acc[span, :] += conv(widen(act_hist[0, r]), 0, 0, 3 * chans)

        @pl.when(has_near)
        def _():
            if r == order[0]:
                @pl.when(starts)
                def _():
                    weights_ready(1)

            history_near(act_copies, r)
            acc[span, pl.ds(goes, chans)] += conv(widen(act_hist[1, r]), 1, goes, chans)

        parts[out_part] = acc[span, pl.ds(goes, chans)].astype(BF16)
        if r == last:
            @pl.when(has_down)
            def _():
                part_down.start()
        else:
            @pl.when(has_up)
            def _():
                part_up.start()

        @pl.when(has_near)
        def _():
            acc[span, pl.ds(stays, 2 * chans)] += conv(widen(act_hist[1, r]), 1, stays, 2 * chans)

    def finish_row(r):
        total = acc[pl.ds(r * cols, cols), pl.ds(chans, chans)]
        if r > 0:
            total = total + acc[pl.ds((r - 1) * cols, cols), pl.ds(0, chans)]
        if r < rows - 1:
            total = total + acc[pl.ds((r + 1) * cols, cols), pl.ds(2 * chans, chans)]
        total = total + cb_ref[...].reshape(1, chans) + lat[r].astype(F32)
        if r == first:
            total = total + part_in[0].astype(F32)
        if r == last:
            total = total + part_in[1].astype(F32)
        blk[1 + r] = total.astype(BF16)

    for copy in bias_copies[1:]:
        copy.wait()
    tw_copy.wait()

    def mix(row, k):
        return jnp.dot(row, tw[k], preferred_element_type=F32)

    def newest(j):
        mixed[j] = mix(blk[j], 2) + tb_ref[...].reshape(1, 2 * chans)

    def mix_far(j):
        @pl.when(has_prev)
        def _():
            history_far(blk_copies, j)
            mixed[j] += mix(blk_hist[0, j], 0)

    def mix_near(j):
        @pl.when(has_near)
        def _():
            history_near(blk_copies, j)
            mixed[j] += mix(blk_hist[1, j], 1)

        for f in range(2):
            dbl[j, f] = mixed[j, :, pl.ds(f * chans, chans)].astype(BF16)

    def taps_dot(row, a, start, size):
        return lax.dot_general(
            row, umat[a, :, pl.ds(start, size)], (((1,), (1,)), ((), ())), preferred_element_type=F32
        )

    def stored_row(j):
        return dbl[j].reshape(2 * cols, chans)

    @pl.when(has_up)
    def _():
        part_down.wait_recv()

    @pl.when(jnp.logical_not(has_up))
    def _():
        part_in[0] = jnp.zeros((cols, chans), BF16)

    for r in range(rows - 1):
        finish_row(r)

        if r == first:
            @pl.when(has_up & starts)
            def _():
                blk_up.start()

        history_start(blk_copies, 1 + r)
        newest(1 + r)

    @pl.when(has_down)
    def _():
        part_up.wait_recv()

    @pl.when(jnp.logical_not(has_down))
    def _():
        part_in[1] = jnp.zeros((cols, chans), BF16)

    finish_row(last)

    @pl.when(has_down)
    def _():
        blk_down.start()

    history_start(blk_copies, rows)

    @pl.when(starts)
    def _():
        sum_taps()
        weights_ready(0)

        @pl.when(t == 0)
        def _():
            weights_ready(1)

    newest(rows)

    for r in range(rows):
        if r == last:
            @pl.when(has_up)
            def _():
                blk_down.wait_recv()
                history_start(blk_copies, 0)

        mix_far(1 + r)
        mix_near(1 + r)
        if r == first:
            @pl.when(has_up & later)
            def _():
                for copy in dbl_up:
                    copy.start()

            @pl.when(has_down & (t == 0))
            def _():
                blk_up.wait_recv()
                blk_copies[0](rows + 1).start()

            edge[0] = taps_dot(stored_row(1), 0, chans, chans)

    bias_row = ub_ref[...].reshape(1, outs_n)
    up_bias = jnp.concatenate(
        [bias_row[:, :low], bias_row[:, :low], bias_row[:, low:], bias_row[:, low:]], axis=1
    )

    def upsample_row(a, r, result, which=(0, 1)):
        center = result[:, : 2 * outs_n] + up_bias
        sides = result[:, 2 * outs_n :]
        even = center[:, :low] + column_shift(sides[:, :low], cols, 1)
        uneven = center[:, low : 2 * low] + column_shift(sides[:, low : 2 * low], cols, -1)
        tail = sides[:, 2 * low :]
        lane = lax.broadcasted_iota(jnp.int32, tail.shape, 1)
        tail = center[:, 2 * low :] + jnp.where(
            lane < high, column_shift(tail, cols, 1), column_shift(tail, cols, -1)
        )
        swapped = pltpu.roll(tail, high, 1)
        for k, f in enumerate(which):
            span = slice(k * cols, (k + 1) * cols)
            wide_lo[pl.ds(0, cols, stride=2), :] = even[span]
            wide_lo[pl.ds(1, cols, stride=2), :] = uneven[span]
            wide_hi[pl.ds(0, cols, stride=2), :] = tail[span]
            wide_hi[pl.ds(1, cols, stride=2), :] = swapped[span]
            out_ref[f, 2 * r + a, pl.ds(0, low), :] = wide_lo[...].T.astype(BF16)
            out_ref[f, 2 * r + a, pl.ds(low, high), :] = wide_hi[...].T[:high].astype(BF16)

    for r in range(rows):
        for a in range(2):
            if 0 < r + a < rows:
                both = jnp.concatenate([stored_row(r + a), stored_row(r + a + 1)], axis=1)
                upsample_row(a, r, taps_dot(both, a, 0, 2 * chans))

    @pl.when(has_up)
    def _():
        newest(0)
        mix_far(0)

    edge[1] = taps_dot(stored_row(rows), 1, 0, chans)

    @pl.when(has_up)
    def _():
        mix_near(0)
        edge[0] += taps_dot(stored_row(0), 0, 0, chans)

    upsample_row(0, 0, edge[0])

    @pl.when(has_down & starts)
    def _():
        @pl.when(t == 1)
        def _():
            blk_up.wait_recv()

        newest(rows + 1)

        @pl.when(t == 1)
        def _():
            history_near(blk_copies, rows + 1)
            mixed[rows + 1] += mix(blk_hist[1, rows + 1], 1)

        for f in range(2):
            dbl[rows + 1, f] = mixed[rows + 1, :, pl.ds(f * chans, chans)].astype(BF16)

    for f in range(2):
        frame = pl.ds(f * cols, cols)

        @pl.when(has_down & later)
        def _():
            dbl_up[f].wait_recv()

        @pl.when(has_down)
        def _():
            edge[1, frame] += taps_dot(dbl[rows + 1, f], 1, chans, chans)

        upsample_row(1, last, edge[1, frame], (f,))

    for r in range(rows):
        history_end(act_copies, r, has_next if r == order[0] else direct)
        history_end(blk_copies, 1 + r)

    @pl.when(relays)
    def _():
        for r in order[1:]:
            to_partner(r).wait_send()
            from_partner(r).wait_send()

    @pl.when(has_up)
    def _():
        history_end(blk_copies, 0)
        part_up.wait_send()

        @pl.when(later)
        def _():
            for copy in dbl_up:
                copy.wait_send()

        @pl.when(starts)
        def _():
            blk_up.wait_send()

    @pl.when(has_down)
    def _():
        part_down.wait_send()
        blk_down.wait_send()

        @pl.when(t == 0)
        def _():
            blk_copies[0](rows + 1).wait_send()


def local(frames, tiles, latent, gain, conv_weight, conv_bias, time_weight, time_bias, up_weight, up_bias):
    _, rows, cols, chans = latent.shape
    outs_n = up_weight.shape[3]
    low = 128
    dma = pltpu.SemaphoreType.DMA
    row = (cols, chans)
    transposed = pl.pallas_call(
        functools.partial(kernel, frames, tiles),
        out_shape=jax.ShapeDtypeStruct((2, 2 * rows, outs_n, 2 * cols), BF16),
        in_specs=[pl.BlockSpec(memory_space=pltpu.HBM)] * 8,
        out_specs=pl.BlockSpec(memory_space=pltpu.VMEM),
        scratch_shapes=[
            pltpu.VMEM((rows,) + row, BF16),
            pltpu.VMEM((rows,) + row, BF16),
            pltpu.VMEM((2, rows) + row, BF16),
            pltpu.VMEM((rows,) + row, BF16),
            pltpu.VMEM((2,) + row, BF16),
            pltpu.VMEM((2,) + row, BF16),
            pltpu.VMEM((rows + 2,) + row, BF16),
            pltpu.VMEM((2, rows + 2) + row, BF16),
            pltpu.VMEM((rows + 2, 2) + row, BF16),
            pltpu.VMEM((chans,), F32),
            pltpu.VMEM((chans,), F32),
            pltpu.VMEM((2 * chans,), F32),
            pltpu.VMEM((outs_n,), F32),
            pltpu.VMEM((3, 3, chans, 3 * chans), BF16),
            pltpu.VMEM((3, chans, 2 * chans), BF16),
            pltpu.VMEM((3, 3, outs_n, chans), BF16),
            pltpu.VMEM((2, 4 * outs_n, 2 * chans), BF16),
            pltpu.VMEM((rows * cols, 3 * chans), F32),
            pltpu.VMEM((rows + 2, cols, 2 * chans), F32),
            pltpu.VMEM((2, 2 * cols, 4 * outs_n), F32),
            pltpu.VMEM((2 * cols, low), F32),
            pltpu.VMEM((2 * cols, low), F32),
            dma(()), dma((4,)), dma((3, 3)), dma(()), dma(()),
            dma((2, rows)), dma((2, rows)), dma((rows,)),
            dma((2, rows)), dma((rows,)),
            dma((2, rows + 2)), dma((2, rows + 2)), dma((rows + 2,)),
            dma((2,)), dma((2,)), dma((2,)), dma((2,)), dma((2, 2)),
        ],
        compiler_params=pltpu.CompilerParams(
            collective_id=0, has_side_effects=True, vmem_limit_bytes=48 * 1024 * 1024
        ),
    )(*(
        pltpu.with_memory_space_constraint(array, pltpu.HBM)
        for array in (
            latent, gain, conv_bias, time_bias, up_bias,
            conv_weight, time_weight, jnp.swapaxes(up_weight, 2, 3),
        )
    ))
    return jnp.swapaxes(transposed, 2, 3)


def solution(mesh):
    placed = (P("tm", "tile", None, None), P(), P(), P(), P(), P(), P(), P())
    return jax.shard_map(
        functools.partial(local, mesh.shape["tm"], mesh.shape["tile"]),
        mesh=mesh, in_specs=placed, out_specs=P("tm", "tile", None, None), check_vma=False,
    )
```

```python
import functools

import jax
import jax.numpy as jnp
from jax import lax
from jax.experimental import pallas as pl
from jax.experimental.pallas import tpu as pltpu
from jax.sharding import PartitionSpec as P

F32 = jnp.float32
BF16 = jnp.bfloat16
MESH = pl.DeviceIdType.MESH


def column_shift(flat, cols, step):
    total = flat.shape[0]
    rolled = pltpu.roll(flat, step % total, 0)
    place = lax.broadcasted_iota(jnp.int32, flat.shape, 0) % cols
    edge = 0 if step > 0 else cols - 1
    return jnp.where(place == edge, 0.0, rolled)


def kernel(
    frames, tiles,
    lat_hbm, gain_hbm, cb_hbm, tb_hbm, ub_hbm, cw_hbm, tw_hbm, uw_hbm,
    out_ref,
    lat, act, act_hist, act_relay, parts, part_in, blk, blk_hist, dbl,
    gain_ref, cb_ref, tb_ref, ub_ref, cw, tw, uw, umat, acc, mixed, edge, wide_lo, wide_hi,
    lat_sem, bias_sem, cw_sem, tw_sem, uw_sem,
    a_send, a_recv, a_fsend, r_send, r_recv, b_send, b_recv, b_fsend,
    p_down_sem, p_up_sem, b_down_sem, b_up_sem, d_up_sem,
):
    rows, cols, chans = lat.shape
    outs_n = uw.shape[2]
    low = 128
    high = outs_n - low
    cells = rows * cols
    t = lax.axis_index("tm")
    s = lax.axis_index("tile")
    odd = lax.rem(t, 2) == 1
    even = jnp.logical_not(odd)
    has_next = t + 2 < frames
    has_prev = t >= 2
    has_near = t >= 1
    starts = t < 2
    later = t >= 2
    has_up = s > 0
    has_down = s < tiles - 1

    lat_copy = pltpu.make_async_copy(lat_hbm.at[0], lat, lat_sem)
    lat_copy.start()
    bias_copies = []
    for k, (src, dst) in enumerate(
        ((gain_hbm, gain_ref), (cb_hbm, cb_ref), (tb_hbm, tb_ref), (ub_hbm, ub_ref))
    ):
        copy = pltpu.make_async_copy(src, dst, bias_sem.at[k])
        copy.start()
        bias_copies.append(copy)
    half = frames // 2
    partner = s + 1 - 2 * lax.rem(s, 2)
    relays = t // 2 == half // 2 - 1
    relayed = t // 2 == half // 2
    direct = jnp.logical_and(has_next, jnp.logical_not(relays))

    sibling = t + 1 - 2 * lax.rem(t, 2)
    barrier = pltpu.get_barrier_semaphore()

    def greet(condition, where):
        @pl.when(condition)
        def _():
            pl.semaphore_signal(barrier, inc=1, device_id=where, device_id_type=MESH)

    pl.semaphore_signal(barrier, inc=1, device_id={"tm": sibling}, device_id_type=MESH)
    greet(has_next, {"tm": t + 2})
    greet(has_prev, {"tm": t - 2})
    greet(relays, {"tm": t + 2, "tile": partner})
    greet(relayed, {"tm": t - 2, "tile": partner})
    greet(has_up, {"tile": s - 1})
    greet(has_down, {"tile": s + 1})

    cw_copies = {}
    for dt in (2, 0, 1):
        for dh in range(3):
            copy = pltpu.make_async_copy(
                cw_hbm.at[dt, dh],
                cw.at[dt, :, :, pl.ds(dh * chans, chans)],
                cw_sem.at[dt, dh],
            )
            copy.start()
            cw_copies[dt, dh] = copy
    tw_copy = pltpu.make_async_copy(tw_hbm, tw, tw_sem)
    tw_copy.start()
    uw_copy = pltpu.make_async_copy(uw_hbm, uw, uw_sem)
    uw_copy.start()

    def history_copies(own, hist, send, recv, fsend):
        def nearer(r):
            return pltpu.make_async_remote_copy(
                own.at[r], hist.at[1, r], send.at[0, r], recv.at[1, r],
                device_id={"tm": sibling}, device_id_type=MESH,
            )

        def farther(r):
            return pltpu.make_async_remote_copy(
                own.at[r], hist.at[0, r], send.at[1, r], recv.at[0, r],
                device_id={"tm": t + 2}, device_id_type=MESH,
            )

        def forward(r):
            return pltpu.make_async_remote_copy(
                hist.at[0, r], hist.at[1, r], fsend.at[r], recv.at[1, r],
                device_id={"tm": sibling}, device_id_type=MESH,
            )

        return nearer, farther, forward

    def history_start(copies, r, sends=has_next):
        nearer, farther, _ = copies

        @pl.when(sends)
        def _():
            farther(r).start()

        @pl.when(even)
        def _():
            nearer(r).start()

    def history_far(copies, r):
        _, farther, forward = copies
        farther(r).wait_recv()

        @pl.when(odd)
        def _():
            forward(r).start()

    def history_near(copies, r):
        copies[0](r).wait_recv()

    def history_end(copies, r, sends=has_next):
        nearer, farther, forward = copies

        @pl.when(sends)
        def _():
            farther(r).wait_send()

        @pl.when(even)
        def _():
            nearer(r).wait_send()

        @pl.when(jnp.logical_and(odd, has_prev))
        def _():
            forward(r).wait_send()

    def to_tile(src, dst, sems, where):
        return pltpu.make_async_remote_copy(
            src, dst, sems.at[0], sems.at[1], device_id={"tile": where}, device_id_type=MESH
        )

    first, last = 0, rows - 1
    act_copies = history_copies(act, act_hist, a_send, a_recv, a_fsend)
    blk_copies = history_copies(blk, blk_hist, b_send, b_recv, b_fsend)
    part_down = to_tile(parts.at[1], part_in.at[0], p_down_sem, s + 1)
    part_up = to_tile(parts.at[0], part_in.at[1], p_up_sem, s - 1)
    blk_down = to_tile(blk.at[rows], blk.at[0], b_down_sem, s + 1)
    blk_up = to_tile(blk.at[1], blk.at[rows + 1], b_up_sem, s - 1)
    dbl_up = [to_tile(dbl.at[1, f], dbl.at[rows + 1, f], d_up_sem.at[f], s - 1) for f in range(2)]

    def activate(r):
        values = lat[r].astype(F32)
        meansq = jnp.mean(values * values, axis=-1, keepdims=True)
        scaled = values * lax.rsqrt(meansq + 1e-06) * gain_ref[...].reshape(1, chans)
        act[r] = (scaled * jax.nn.sigmoid(scaled)).astype(BF16)

    peers = 1
    for condition in (has_next, has_prev, relays, relayed, has_up, has_down):
        peers = peers + condition.astype(jnp.int32)

    def to_partner(r):
        return pltpu.make_async_remote_copy(
            act.at[r], act_relay.at[r], r_send.at[0, r], r_recv.at[r],
            device_id={"tile": partner}, device_id_type=MESH,
        )

    def from_partner(r):
        return pltpu.make_async_remote_copy(
            act_relay.at[r], act_hist.at[0, r], r_send.at[1, r], a_recv.at[0, r],
            device_id={"tm": t + 2, "tile": partner}, device_id_type=MESH,
        )

    order = tuple(range(rows))[::-1]
    lat_copy.wait()
    bias_copies[0].wait()
    for r in order:
        activate(r)
        if r == order[0]:
            pl.semaphore_wait(barrier, peers)
        if r == order[0]:
            history_start(act_copies, r)
        else:
            @pl.when(relays)
            def _():
                to_partner(r).start()

            history_start(act_copies, r, direct)

    def widen(frame):
        flat = frame.reshape(-1, chans)
        wide = flat.astype(F32)
        before = column_shift(wide, cols, 1).astype(BF16)
        after = column_shift(wide, cols, -1).astype(BF16)
        return jnp.concatenate([before, flat, after], axis=1)

    def conv(stacked, dt, start, size):
        taps = cw.at[dt, :, :, pl.ds(start, size)][...].reshape(3 * chans, size)
        return jnp.dot(stacked, taps, preferred_element_type=F32)

    def weights_ready(dt):
        for dh in range(3):
            cw_copies[dt, dh].wait()

    weights_ready(2)
    acc[...] = conv(widen(act[...]), 2, 0, 3 * chans)
    @pl.when(relays)
    def _():
        for r in order[1:]:
            to_partner(r).wait_recv()
            from_partner(r).start()

    def sum_taps():
        uw_copy.wait()
        row_sets = {(0, 0): (0,), (0, 1): (1, 2), (1, 0): (0, 1), (1, 1): (2,)}
        for (a, i), picks in row_sets.items():
            taps = []
            for kw in range(3):
                tap = uw[picks[0], kw].astype(F32)
                for kh in picks[1:]:
                    tap = tap + uw[kh, kw].astype(F32)
                taps.append(tap)
            center = (taps[1] + taps[2], taps[0] + taps[1])
            sides = (taps[0], taps[2])
            lanes = pl.ds(i * chans, chans)
            for base, pair in ((0, center), (2 * outs_n, sides)):
                for b in range(2):
                    value = pair[b].astype(BF16)
                    umat[a, pl.ds(base + b * low, low), lanes] = value[:low]
                    umat[a, pl.ds(base + 2 * low + b * high, high), lanes] = value[low:]

    @pl.when(later)
    def _():
        sum_taps()
        weights_ready(0)
        weights_ready(1)

    for r in order:
        span = pl.ds(r * cols, cols)
        goes, stays = (0, chans) if r == last else (2 * chans, 0)
        out_part = 1 if r == last else 0

        @pl.when(has_prev)
        def _():
            history_far(act_copies, r)
            acc[span, :] += conv(widen(act_hist[0, r]), 0, 0, 3 * chans)

        @pl.when(has_near)
        def _():
            if r == order[0]:
                @pl.when(starts)
                def _():
                    weights_ready(1)

            history_near(act_copies, r)
            acc[span, pl.ds(goes, chans)] += conv(widen(act_hist[1, r]), 1, goes, chans)

        parts[out_part] = acc[span, pl.ds(goes, chans)].astype(BF16)
        if r == last:
            @pl.when(has_down)
            def _():
                part_down.start()
        else:
            @pl.when(has_up)
            def _():
                part_up.start()

        @pl.when(has_near)
        def _():
            acc[span, pl.ds(stays, 2 * chans)] += conv(widen(act_hist[1, r]), 1, stays, 2 * chans)

    def finish_row(r):
        total = acc[pl.ds(r * cols, cols), pl.ds(chans, chans)]
        if r > 0:
            total = total + acc[pl.ds((r - 1) * cols, cols), pl.ds(0, chans)]
        if r < rows - 1:
            total = total + acc[pl.ds((r + 1) * cols, cols), pl.ds(2 * chans, chans)]
        total = total + cb_ref[...].reshape(1, chans) + lat[r].astype(F32)
        if r == first:
            total = total + part_in[0].astype(F32)
        if r == last:
            total = total + part_in[1].astype(F32)
        blk[1 + r] = total.astype(BF16)

    for copy in bias_copies[1:]:
        copy.wait()
    tw_copy.wait()

    def mix(row, k):
        return jnp.dot(row, tw[k], preferred_element_type=F32)

    def newest(j):
        mixed[j] = mix(blk[j], 2) + tb_ref[...].reshape(1, 2 * chans)

    def mix_far(j):
        @pl.when(has_prev)
        def _():
            history_far(blk_copies, j)
            mixed[j] += mix(blk_hist[0, j], 0)

    def mix_near(j):
        @pl.when(has_near)
        def _():
            history_near(blk_copies, j)
            mixed[j] += mix(blk_hist[1, j], 1)

        for f in range(2):
            dbl[j, f] = mixed[j, :, pl.ds(f * chans, chans)].astype(BF16)

    def taps_dot(row, a, start, size):
        return lax.dot_general(
            row, umat[a, :, pl.ds(start, size)], (((1,), (1,)), ((), ())), preferred_element_type=F32
        )

    def stored_row(j):
        return dbl[j].reshape(2 * cols, chans)

    @pl.when(has_up)
    def _():
        part_down.wait_recv()

    @pl.when(jnp.logical_not(has_up))
    def _():
        part_in[0] = jnp.zeros((cols, chans), BF16)

    for r in range(rows - 1):
        finish_row(r)

        if r == first:
            @pl.when(has_up & starts)
            def _():
                blk_up.start()

        history_start(blk_copies, 1 + r)
        newest(1 + r)

    @pl.when(has_down)
    def _():
        part_up.wait_recv()

    @pl.when(jnp.logical_not(has_down))
    def _():
        part_in[1] = jnp.zeros((cols, chans), BF16)

    finish_row(last)

    @pl.when(has_down)
    def _():
        blk_down.start()

    history_start(blk_copies, rows)

    @pl.when(starts)
    def _():
        sum_taps()
        weights_ready(0)

        @pl.when(t == 0)
        def _():
            weights_ready(1)

    newest(rows)

    for r in range(rows):
        if r == last:
            @pl.when(has_up)
            def _():
                blk_down.wait_recv()
                history_start(blk_copies, 0)

        mix_far(1 + r)
        mix_near(1 + r)
        if r == first:
            @pl.when(has_up & later)
            def _():
                for copy in dbl_up:
                    copy.start()

            @pl.when(has_down & (t == 0))
            def _():
                blk_up.wait_recv()
                blk_copies[0](rows + 1).start()

            edge[0] = taps_dot(stored_row(1), 0, chans, chans)

    bias_row = ub_ref[...].reshape(1, outs_n)
    up_bias = jnp.concatenate(
        [bias_row[:, :low], bias_row[:, :low], bias_row[:, low:], bias_row[:, low:]], axis=1
    )

    def upsample_row(a, r, result, which=(0, 1)):
        center = result[:, : 2 * outs_n] + up_bias
        sides = result[:, 2 * outs_n :]
        even = center[:, :low] + column_shift(sides[:, :low], cols, 1)
        uneven = center[:, low : 2 * low] + column_shift(sides[:, low : 2 * low], cols, -1)
        tail = sides[:, 2 * low :]
        lane = lax.broadcasted_iota(jnp.int32, tail.shape, 1)
        tail = center[:, 2 * low :] + jnp.where(
            lane < high, column_shift(tail, cols, 1), column_shift(tail, cols, -1)
        )
        swapped = pltpu.roll(tail, high, 1)
        for k, f in enumerate(which):
            span = slice(k * cols, (k + 1) * cols)
            wide_lo[pl.ds(0, cols, stride=2), :] = even[span]
            wide_lo[pl.ds(1, cols, stride=2), :] = uneven[span]
            wide_hi[pl.ds(0, cols, stride=2), :] = tail[span]
            wide_hi[pl.ds(1, cols, stride=2), :] = swapped[span]
            out_ref[f, 2 * r + a, pl.ds(0, low), :] = wide_lo[...].T.astype(BF16)
            out_ref[f, 2 * r + a, pl.ds(low, high), :] = wide_hi[...].T[:high].astype(BF16)

    for r in range(rows):
        for a in range(2):
            if 0 < r + a < rows:
                both = jnp.concatenate([stored_row(r + a), stored_row(r + a + 1)], axis=1)
                upsample_row(a, r, taps_dot(both, a, 0, 2 * chans))

    @pl.when(has_up)
    def _():
        newest(0)
        mix_far(0)

    edge[1] = taps_dot(stored_row(rows), 1, 0, chans)

    @pl.when(has_down & starts)
    def _():
        @pl.when(t == 1)
        def _():
            blk_up.wait_recv()

        newest(rows + 1)

        @pl.when(t == 1)
        def _():
            history_near(blk_copies, rows + 1)
            mixed[rows + 1] += mix(blk_hist[1, rows + 1], 1)

        for f in range(2):
            dbl[rows + 1, f] = mixed[rows + 1, :, pl.ds(f * chans, chans)].astype(BF16)

    for f in range(2):
        frame = pl.ds(f * cols, cols)

        @pl.when(has_down & later)
        def _():
            dbl_up[f].wait_recv()

        @pl.when(has_down)
        def _():
            edge[1, frame] += taps_dot(dbl[rows + 1, f], 1, chans, chans)

        upsample_row(1, last, edge[1, frame], (f,))

    @pl.when(has_up)
    def _():
        mix_near(0)
        edge[0] += taps_dot(stored_row(0), 0, 0, chans)

    upsample_row(0, 0, edge[0])

    for r in range(rows):
        history_end(act_copies, r, has_next if r == order[0] else direct)
        history_end(blk_copies, 1 + r)

    @pl.when(relays)
    def _():
        for r in order[1:]:
            to_partner(r).wait_send()
            from_partner(r).wait_send()

    @pl.when(has_up)
    def _():
        history_end(blk_copies, 0)
        part_up.wait_send()

        @pl.when(later)
        def _():
            for copy in dbl_up:
                copy.wait_send()

        @pl.when(starts)
        def _():
            blk_up.wait_send()

    @pl.when(has_down)
    def _():
        part_down.wait_send()
        blk_down.wait_send()

        @pl.when(t == 0)
        def _():
            blk_copies[0](rows + 1).wait_send()


def local(frames, tiles, latent, gain, conv_weight, conv_bias, time_weight, time_bias, up_weight, up_bias):
    _, rows, cols, chans = latent.shape
    outs_n = up_weight.shape[3]
    low = 128
    dma = pltpu.SemaphoreType.DMA
    row = (cols, chans)
    transposed = pl.pallas_call(
        functools.partial(kernel, frames, tiles),
        out_shape=jax.ShapeDtypeStruct((2, 2 * rows, outs_n, 2 * cols), BF16),
        in_specs=[pl.BlockSpec(memory_space=pltpu.HBM)] * 8,
        out_specs=pl.BlockSpec(memory_space=pltpu.VMEM),
        scratch_shapes=[
            pltpu.VMEM((rows,) + row, BF16),
            pltpu.VMEM((rows,) + row, BF16),
            pltpu.VMEM((2, rows) + row, BF16),
            pltpu.VMEM((rows,) + row, BF16),
            pltpu.VMEM((2,) + row, BF16),
            pltpu.VMEM((2,) + row, BF16),
            pltpu.VMEM((rows + 2,) + row, BF16),
            pltpu.VMEM((2, rows + 2) + row, BF16),
            pltpu.VMEM((rows + 2, 2) + row, BF16),
            pltpu.VMEM((chans,), F32),
            pltpu.VMEM((chans,), F32),
            pltpu.VMEM((2 * chans,), F32),
            pltpu.VMEM((outs_n,), F32),
            pltpu.VMEM((3, 3, chans, 3 * chans), BF16),
            pltpu.VMEM((3, chans, 2 * chans), BF16),
            pltpu.VMEM((3, 3, outs_n, chans), BF16),
            pltpu.VMEM((2, 4 * outs_n, 2 * chans), BF16),
            pltpu.VMEM((rows * cols, 3 * chans), F32),
            pltpu.VMEM((rows + 2, cols, 2 * chans), F32),
            pltpu.VMEM((2, 2 * cols, 4 * outs_n), F32),
            pltpu.VMEM((2 * cols, low), F32),
            pltpu.VMEM((2 * cols, low), F32),
            dma(()), dma((4,)), dma((3, 3)), dma(()), dma(()),
            dma((2, rows)), dma((2, rows)), dma((rows,)),
            dma((2, rows)), dma((rows,)),
            dma((2, rows + 2)), dma((2, rows + 2)), dma((rows + 2,)),
            dma((2,)), dma((2,)), dma((2,)), dma((2,)), dma((2, 2)),
        ],
        compiler_params=pltpu.CompilerParams(
            collective_id=0, has_side_effects=True, vmem_limit_bytes=48 * 1024 * 1024
        ),
    )(*(
        pltpu.with_memory_space_constraint(array, pltpu.HBM)
        for array in (
            latent, gain, conv_bias, time_bias, up_bias,
            conv_weight, time_weight, jnp.swapaxes(up_weight, 2, 3),
        )
    ))
    return jnp.swapaxes(transposed, 2, 3)


def solution(mesh):
    placed = (P("tm", "tile", None, None), P(), P(), P(), P(), P(), P(), P())
    return jax.shard_map(
        functools.partial(local, mesh.shape["tm"], mesh.shape["tile"]),
        mesh=mesh, in_specs=placed, out_specs=P("tm", "tile", None, None), check_vma=False,
    )
```

```python
import functools

import jax
import jax.numpy as jnp
from jax import lax
from jax.experimental import pallas as pl
from jax.experimental.pallas import tpu as pltpu
from jax.sharding import PartitionSpec as P

F32 = jnp.float32
BF16 = jnp.bfloat16
MESH = pl.DeviceIdType.MESH


def column_shift(flat, cols, step):
    total = flat.shape[0]
    rolled = pltpu.roll(flat, step % total, 0)
    place = lax.broadcasted_iota(jnp.int32, flat.shape, 0) % cols
    edge = 0 if step > 0 else cols - 1
    return jnp.where(place == edge, 0.0, rolled)


def kernel(
    frames, tiles,
    lat_hbm, gain_hbm, cb_hbm, tb_hbm, ub_hbm, cw_hbm, tw_hbm, uw_hbm,
    out_ref,
    lat, act, act_hist, act_relay, parts, part_in, blk, blk_hist, dbl,
    gain_ref, cb_ref, tb_ref, ub_ref, cw, tw, uw, umat, acc, mixed, edge, wide_lo, wide_hi,
    lat_sem, bias_sem, cw_sem, tw_sem, uw_sem,
    a_send, a_recv, a_fsend, r_send, r_recv, b_send, b_recv, b_fsend,
    p_down_sem, p_up_sem, b_down_sem, b_up_sem, d_up_sem,
):
    rows, cols, chans = lat.shape
    outs_n = uw.shape[2]
    low = 128
    high = outs_n - low
    cells = rows * cols
    t = lax.axis_index("tm")
    s = lax.axis_index("tile")
    odd = lax.rem(t, 2) == 1
    even = jnp.logical_not(odd)
    has_next = t + 2 < frames
    has_prev = t >= 2
    has_near = t >= 1
    starts = t < 2
    later = t >= 2
    has_up = s > 0
    has_down = s < tiles - 1

    lat_copy = pltpu.make_async_copy(lat_hbm.at[0], lat, lat_sem)
    lat_copy.start()
    bias_copies = []
    for k, (src, dst) in enumerate(
        ((gain_hbm, gain_ref), (cb_hbm, cb_ref), (tb_hbm, tb_ref), (ub_hbm, ub_ref))
    ):
        copy = pltpu.make_async_copy(src, dst, bias_sem.at[k])
        copy.start()
        bias_copies.append(copy)
    half = frames // 2
    partner = s + 1 - 2 * lax.rem(s, 2)
    relays = t // 2 == half // 2 - 1
    relayed = t // 2 == half // 2
    direct = jnp.logical_and(has_next, jnp.logical_not(relays))

    sibling = t + 1 - 2 * lax.rem(t, 2)
    barrier = pltpu.get_barrier_semaphore()

    def greet(condition, where):
        @pl.when(condition)
        def _():
            pl.semaphore_signal(barrier, inc=1, device_id=where, device_id_type=MESH)

    pl.semaphore_signal(barrier, inc=1, device_id={"tm": sibling}, device_id_type=MESH)
    greet(has_next, {"tm": t + 2})
    greet(has_prev, {"tm": t - 2})
    greet(relays, {"tm": t + 2, "tile": partner})
    greet(relayed, {"tm": t - 2, "tile": partner})
    greet(has_up, {"tile": s - 1})
    greet(has_down, {"tile": s + 1})

    cw_copies = {}
    for dt in (2, 0, 1):
        for dh in range(3):
            copy = pltpu.make_async_copy(
                cw_hbm.at[dt, dh],
                cw.at[dt, :, :, pl.ds(dh * chans, chans)],
                cw_sem.at[dt, dh],
            )
            copy.start()
            cw_copies[dt, dh] = copy
    tw_copy = pltpu.make_async_copy(tw_hbm, tw, tw_sem)
    tw_copy.start()
    uw_copy = pltpu.make_async_copy(uw_hbm, uw, uw_sem)
    uw_copy.start()

    def history_copies(own, hist, send, recv, fsend):
        def nearer(r):
            return pltpu.make_async_remote_copy(
                own.at[r], hist.at[1, r], send.at[0, r], recv.at[1, r],
                device_id={"tm": sibling}, device_id_type=MESH,
            )

        def farther(r):
            return pltpu.make_async_remote_copy(
                own.at[r], hist.at[0, r], send.at[1, r], recv.at[0, r],
                device_id={"tm": t + 2}, device_id_type=MESH,
            )

        def forward(r):
            return pltpu.make_async_remote_copy(
                hist.at[0, r], hist.at[1, r], fsend.at[r], recv.at[1, r],
                device_id={"tm": sibling}, device_id_type=MESH,
            )

        return nearer, farther, forward

    def history_start(copies, r, sends=has_next):
        nearer, farther, _ = copies

        @pl.when(sends)
        def _():
            farther(r).start()

        @pl.when(even)
        def _():
            nearer(r).start()

    def history_far(copies, r):
        _, farther, forward = copies
        farther(r).wait_recv()

        @pl.when(odd)
        def _():
            forward(r).start()

    def history_near(copies, r):
        copies[0](r).wait_recv()

    def history_end(copies, r, sends=has_next):
        nearer, farther, forward = copies

        @pl.when(sends)
        def _():
            farther(r).wait_send()

        @pl.when(even)
        def _():
            nearer(r).wait_send()

        @pl.when(jnp.logical_and(odd, has_prev))
        def _():
            forward(r).wait_send()

    def to_tile(src, dst, sems, where):
        return pltpu.make_async_remote_copy(
            src, dst, sems.at[0], sems.at[1], device_id={"tile": where}, device_id_type=MESH
        )

    first, last = 0, rows - 1
    act_copies = history_copies(act, act_hist, a_send, a_recv, a_fsend)
    blk_copies = history_copies(blk, blk_hist, b_send, b_recv, b_fsend)
    part_down = to_tile(parts.at[1], part_in.at[0], p_down_sem, s + 1)
    part_up = to_tile(parts.at[0], part_in.at[1], p_up_sem, s - 1)
    blk_down = to_tile(blk.at[rows], blk.at[0], b_down_sem, s + 1)
    blk_up = to_tile(blk.at[1], blk.at[rows + 1], b_up_sem, s - 1)
    dbl_up = to_tile(dbl.at[1], dbl.at[rows + 1], d_up_sem, s - 1)

    def activate(r):
        values = lat[r].astype(F32)
        meansq = jnp.mean(values * values, axis=-1, keepdims=True)
        scaled = values * lax.rsqrt(meansq + 1e-06) * gain_ref[...].reshape(1, chans)
        act[r] = (scaled * jax.nn.sigmoid(scaled)).astype(BF16)

    peers = 1
    for condition in (has_next, has_prev, relays, relayed, has_up, has_down):
        peers = peers + condition.astype(jnp.int32)

    def to_partner(r):
        return pltpu.make_async_remote_copy(
            act.at[r], act_relay.at[r], r_send.at[0, r], r_recv.at[r],
            device_id={"tile": partner}, device_id_type=MESH,
        )

    def from_partner(r):
        return pltpu.make_async_remote_copy(
            act_relay.at[r], act_hist.at[0, r], r_send.at[1, r], a_recv.at[0, r],
            device_id={"tm": t + 2, "tile": partner}, device_id_type=MESH,
        )

    order = tuple(range(rows))[::-1]
    lat_copy.wait()
    bias_copies[0].wait()
    for r in order:
        activate(r)
        if r == order[0]:
            pl.semaphore_wait(barrier, peers)
        if r == order[0]:
            history_start(act_copies, r)
        else:
            @pl.when(relays)
            def _():
                to_partner(r).start()

            history_start(act_copies, r, direct)

    def widen(frame):
        flat = frame.reshape(-1, chans)
        wide = flat.astype(F32)
        before = column_shift(wide, cols, 1).astype(BF16)
        after = column_shift(wide, cols, -1).astype(BF16)
        return jnp.concatenate([before, flat, after], axis=1)

    def conv(stacked, dt, start, size):
        taps = cw.at[dt, :, :, pl.ds(start, size)][...].reshape(3 * chans, size)
        return jnp.dot(stacked, taps, preferred_element_type=F32)

    def weights_ready(dt):
        for dh in range(3):
            cw_copies[dt, dh].wait()

    weights_ready(2)
    acc[...] = conv(widen(act[...]), 2, 0, 3 * chans)
    @pl.when(relays)
    def _():
        for r in order[1:]:
            to_partner(r).wait_recv()
            from_partner(r).start()

    def sum_taps():
        uw_copy.wait()
        row_sets = {(0, 0): (0,), (0, 1): (1, 2), (1, 0): (0, 1), (1, 1): (2,)}
        for (a, i), picks in row_sets.items():
            taps = []
            for kw in range(3):
                tap = uw[picks[0], kw].astype(F32)
                for kh in picks[1:]:
                    tap = tap + uw[kh, kw].astype(F32)
                taps.append(tap)
            center = (taps[1] + taps[2], taps[0] + taps[1])
            sides = (taps[0], taps[2])
            lanes = pl.ds(i * chans, chans)
            for base, pair in ((0, center), (2 * outs_n, sides)):
                for b in range(2):
                    value = pair[b].astype(BF16)
                    umat[a, pl.ds(base + b * low, low), lanes] = value[:low]
                    umat[a, pl.ds(base + 2 * low + b * high, high), lanes] = value[low:]

    @pl.when(later)
    def _():
        sum_taps()
        weights_ready(0)
        weights_ready(1)

    for r in order:
        span = pl.ds(r * cols, cols)
        goes, stays = (0, chans) if r == last else (2 * chans, 0)
        out_part = 1 if r == last else 0

        @pl.when(has_prev)
        def _():
            history_far(act_copies, r)
            acc[span, :] += conv(widen(act_hist[0, r]), 0, 0, 3 * chans)

        @pl.when(has_near)
        def _():
            if r == order[0]:
                @pl.when(starts)
                def _():
                    weights_ready(1)

            history_near(act_copies, r)
            acc[span, pl.ds(goes, chans)] += conv(widen(act_hist[1, r]), 1, goes, chans)

        parts[out_part] = acc[span, pl.ds(goes, chans)].astype(BF16)
        if r == last:
            @pl.when(has_down)
            def _():
                part_down.start()
        else:
            @pl.when(has_up)
            def _():
                part_up.start()

        @pl.when(has_near)
        def _():
            acc[span, pl.ds(stays, 2 * chans)] += conv(widen(act_hist[1, r]), 1, stays, 2 * chans)

    def finish_row(r):
        total = acc[pl.ds(r * cols, cols), pl.ds(chans, chans)]
        if r > 0:
            total = total + acc[pl.ds((r - 1) * cols, cols), pl.ds(0, chans)]
        if r < rows - 1:
            total = total + acc[pl.ds((r + 1) * cols, cols), pl.ds(2 * chans, chans)]
        total = total + cb_ref[...].reshape(1, chans) + lat[r].astype(F32)
        if r == first:
            total = total + part_in[0].astype(F32)
        if r == last:
            total = total + part_in[1].astype(F32)
        blk[1 + r] = total.astype(BF16)

    for copy in bias_copies[1:]:
        copy.wait()
    tw_copy.wait()

    def mix(row, k):
        return jnp.dot(row, tw[k], preferred_element_type=F32)

    def newest(j):
        mixed[j] = mix(blk[j], 2) + tb_ref[...].reshape(1, 2 * chans)

    def mix_far(j):
        @pl.when(has_prev)
        def _():
            history_far(blk_copies, j)
            mixed[j] += mix(blk_hist[0, j], 0)

    def mix_near(j):
        @pl.when(has_near)
        def _():
            history_near(blk_copies, j)
            mixed[j] += mix(blk_hist[1, j], 1)

        for f in range(2):
            dbl[j, f] = mixed[j, :, pl.ds(f * chans, chans)].astype(BF16)

    def taps_dot(row, a, start, size):
        return lax.dot_general(
            row, umat[a, :, pl.ds(start, size)], (((1,), (1,)), ((), ())), preferred_element_type=F32
        )

    def stored_row(j):
        return dbl[j].reshape(2 * cols, chans)

    @pl.when(has_up)
    def _():
        part_down.wait_recv()

    @pl.when(jnp.logical_not(has_up))
    def _():
        part_in[0] = jnp.zeros((cols, chans), BF16)

    for r in range(rows - 1):
        finish_row(r)

        if r == first:
            @pl.when(has_up & starts)
            def _():
                blk_up.start()

        history_start(blk_copies, 1 + r)
        newest(1 + r)

    @pl.when(has_down)
    def _():
        part_up.wait_recv()

    @pl.when(jnp.logical_not(has_down))
    def _():
        part_in[1] = jnp.zeros((cols, chans), BF16)

    finish_row(last)

    @pl.when(has_down)
    def _():
        blk_down.start()

    history_start(blk_copies, rows)

    @pl.when(starts)
    def _():
        sum_taps()
        weights_ready(0)

        @pl.when(t == 0)
        def _():
            weights_ready(1)

    newest(rows)

    for r in range(rows):
        if r == last:
            @pl.when(has_up)
            def _():
                blk_down.wait_recv()
                history_start(blk_copies, 0)

            edge[0] = taps_dot(stored_row(1), 0, chans, chans)

        mix_far(1 + r)
        mix_near(1 + r)
        if r == first:
            @pl.when(has_up & later)
            def _():
                dbl_up.start()

            @pl.when(has_down & (t == 0))
            def _():
                blk_up.wait_recv()
                blk_copies[0](rows + 1).start()

    bias_row = ub_ref[...].reshape(1, outs_n)
    up_bias = jnp.concatenate(
        [bias_row[:, :low], bias_row[:, :low], bias_row[:, low:], bias_row[:, low:]], axis=1
    )

    def upsample_row(a, r, result):
        center = result[:, : 2 * outs_n] + up_bias
        sides = result[:, 2 * outs_n :]
        even = center[:, :low] + column_shift(sides[:, :low], cols, 1)
        uneven = center[:, low : 2 * low] + column_shift(sides[:, low : 2 * low], cols, -1)
        tail = sides[:, 2 * low :]
        lane = lax.broadcasted_iota(jnp.int32, tail.shape, 1)
        tail = center[:, 2 * low :] + jnp.where(
            lane < high, column_shift(tail, cols, 1), column_shift(tail, cols, -1)
        )
        swapped = pltpu.roll(tail, high, 1)
        for f in range(2):
            span = slice(f * cols, (f + 1) * cols)
            wide_lo[pl.ds(0, cols, stride=2), :] = even[span]
            wide_lo[pl.ds(1, cols, stride=2), :] = uneven[span]
            wide_hi[pl.ds(0, cols, stride=2), :] = tail[span]
            wide_hi[pl.ds(1, cols, stride=2), :] = swapped[span]
            out_ref[f, 2 * r + a, pl.ds(0, low), :] = wide_lo[...].T.astype(BF16)
            out_ref[f, 2 * r + a, pl.ds(low, high), :] = wide_hi[...].T[:high].astype(BF16)

    for r in range(rows):
        for a in range(2):
            if 0 < r + a < rows:
                both = jnp.concatenate([stored_row(r + a), stored_row(r + a + 1)], axis=1)
                upsample_row(a, r, taps_dot(both, a, 0, 2 * chans))

    @pl.when(has_up)
    def _():
        newest(0)
        mix_far(0)

    edge[1] = taps_dot(stored_row(rows), 1, 0, chans)

    @pl.when(has_down & starts)
    def _():
        @pl.when(t == 1)
        def _():
            blk_up.wait_recv()

        newest(rows + 1)

        @pl.when(t == 1)
        def _():
            history_near(blk_copies, rows + 1)
            mixed[rows + 1] += mix(blk_hist[1, rows + 1], 1)

        for f in range(2):
            dbl[rows + 1, f] = mixed[rows + 1, :, pl.ds(f * chans, chans)].astype(BF16)

    @pl.when(has_down & later)
    def _():
        dbl_up.wait_recv()

    @pl.when(has_down)
    def _():
        edge[1] += taps_dot(stored_row(rows + 1), 1, chans, chans)

    upsample_row(1, last, edge[1])

    @pl.when(has_up)
    def _():
        mix_near(0)
        edge[0] += taps_dot(stored_row(0), 0, 0, chans)

    upsample_row(0, 0, edge[0])

    for r in range(rows):
        history_end(act_copies, r, has_next if r == order[0] else direct)
        history_end(blk_copies, 1 + r)

    @pl.when(relays)
    def _():
        for r in order[1:]:
            to_partner(r).wait_send()
            from_partner(r).wait_send()

    @pl.when(has_up)
    def _():
        history_end(blk_copies, 0)
        part_up.wait_send()

        @pl.when(later)
        def _():
            dbl_up.wait_send()

        @pl.when(starts)
        def _():
            blk_up.wait_send()

    @pl.when(has_down)
    def _():
        part_down.wait_send()
        blk_down.wait_send()

        @pl.when(t == 0)
        def _():
            blk_copies[0](rows + 1).wait_send()


def local(frames, tiles, latent, gain, conv_weight, conv_bias, time_weight, time_bias, up_weight, up_bias):
    _, rows, cols, chans = latent.shape
    outs_n = up_weight.shape[3]
    low = 128
    dma = pltpu.SemaphoreType.DMA
    row = (cols, chans)
    transposed = pl.pallas_call(
        functools.partial(kernel, frames, tiles),
        out_shape=jax.ShapeDtypeStruct((2, 2 * rows, outs_n, 2 * cols), BF16),
        in_specs=[pl.BlockSpec(memory_space=pltpu.HBM)] * 8,
        out_specs=pl.BlockSpec(memory_space=pltpu.VMEM),
        scratch_shapes=[
            pltpu.VMEM((rows,) + row, BF16),
            pltpu.VMEM((rows,) + row, BF16),
            pltpu.VMEM((2, rows) + row, BF16),
            pltpu.VMEM((rows,) + row, BF16),
            pltpu.VMEM((2,) + row, BF16),
            pltpu.VMEM((2,) + row, BF16),
            pltpu.VMEM((rows + 2,) + row, BF16),
            pltpu.VMEM((2, rows + 2) + row, BF16),
            pltpu.VMEM((rows + 2, 2) + row, BF16),
            pltpu.VMEM((chans,), F32),
            pltpu.VMEM((chans,), F32),
            pltpu.VMEM((2 * chans,), F32),
            pltpu.VMEM((outs_n,), F32),
            pltpu.VMEM((3, 3, chans, 3 * chans), BF16),
            pltpu.VMEM((3, chans, 2 * chans), BF16),
            pltpu.VMEM((3, 3, outs_n, chans), BF16),
            pltpu.VMEM((2, 4 * outs_n, 2 * chans), BF16),
            pltpu.VMEM((rows * cols, 3 * chans), F32),
            pltpu.VMEM((rows + 2, cols, 2 * chans), F32),
            pltpu.VMEM((2, 2 * cols, 4 * outs_n), F32),
            pltpu.VMEM((2 * cols, low), F32),
            pltpu.VMEM((2 * cols, low), F32),
            dma(()), dma((4,)), dma((3, 3)), dma(()), dma(()),
            dma((2, rows)), dma((2, rows)), dma((rows,)),
            dma((2, rows)), dma((rows,)),
            dma((2, rows + 2)), dma((2, rows + 2)), dma((rows + 2,)),
            dma((2,)), dma((2,)), dma((2,)), dma((2,)), dma((2,)),
        ],
        compiler_params=pltpu.CompilerParams(
            collective_id=0, has_side_effects=True, vmem_limit_bytes=48 * 1024 * 1024
        ),
    )(*(
        pltpu.with_memory_space_constraint(array, pltpu.HBM)
        for array in (
            latent, gain, conv_bias, time_bias, up_bias,
            conv_weight, time_weight, jnp.swapaxes(up_weight, 2, 3),
        )
    ))
    return jnp.swapaxes(transposed, 2, 3)


def solution(mesh):
    placed = (P("tm", "tile", None, None), P(), P(), P(), P(), P(), P(), P())
    return jax.shard_map(
        functools.partial(local, mesh.shape["tm"], mesh.shape["tile"]),
        mesh=mesh, in_specs=placed, out_specs=P("tm", "tile", None, None), check_vma=False,
    )
```

```python
import functools

import jax
import jax.numpy as jnp
from jax import lax
from jax.experimental import pallas as pl
from jax.experimental.pallas import tpu as pltpu
from jax.sharding import PartitionSpec as P

F32 = jnp.float32
BF16 = jnp.bfloat16
MESH = pl.DeviceIdType.MESH


def column_shift(flat, cols, step):
    total = flat.shape[0]
    rolled = pltpu.roll(flat, step % total, 0)
    place = lax.broadcasted_iota(jnp.int32, flat.shape, 0) % cols
    edge = 0 if step > 0 else cols - 1
    return jnp.where(place == edge, 0.0, rolled)


def kernel(
    frames, tiles,
    lat_hbm, gain_hbm, cb_hbm, tb_hbm, ub_hbm, cw_hbm, tw_hbm, uw_hbm,
    out_ref,
    lat, act, act_hist, act_relay, parts, part_in, blk, blk_hist, dbl,
    gain_ref, cb_ref, tb_ref, ub_ref, cw, tw, uw, umat, acc, mixed, edge, wide_lo, wide_hi,
    lat_sem, bias_sem, cw_sem, tw_sem, uw_sem,
    a_send, a_recv, a_fsend, r_send, r_recv, b_send, b_recv, b_fsend,
    p_down_sem, p_up_sem, b_down_sem, b_up_sem, d_up_sem,
):
    rows, cols, chans = lat.shape
    outs_n = uw.shape[2]
    low = 128
    high = outs_n - low
    cells = rows * cols
    t = lax.axis_index("tm")
    s = lax.axis_index("tile")
    odd = lax.rem(t, 2) == 1
    even = jnp.logical_not(odd)
    has_next = t + 2 < frames
    has_prev = t >= 2
    has_near = t >= 1
    starts = t < 2
    later = t >= 2
    has_up = s > 0
    has_down = s < tiles - 1

    lat_copy = pltpu.make_async_copy(lat_hbm.at[0], lat, lat_sem)
    lat_copy.start()
    half = frames // 2
    partner = s + 1 - 2 * lax.rem(s, 2)
    relays = t // 2 == half // 2 - 1
    relayed = t // 2 == half // 2
    direct = jnp.logical_and(has_next, jnp.logical_not(relays))

    sibling = t + 1 - 2 * lax.rem(t, 2)
    barrier = pltpu.get_barrier_semaphore()

    def greet(condition, where):
        @pl.when(condition)
        def _():
            pl.semaphore_signal(barrier, inc=1, device_id=where, device_id_type=MESH)

    pl.semaphore_signal(barrier, inc=1, device_id={"tm": sibling}, device_id_type=MESH)
    greet(has_next, {"tm": t + 2})
    greet(has_prev, {"tm": t - 2})
    greet(relays, {"tm": t + 2, "tile": partner})
    greet(relayed, {"tm": t - 2, "tile": partner})
    greet(has_up, {"tile": s - 1})
    greet(has_down, {"tile": s + 1})

    bias_copies = []
    for k, (src, dst) in enumerate(
        ((gain_hbm, gain_ref), (cb_hbm, cb_ref), (tb_hbm, tb_ref), (ub_hbm, ub_ref))
    ):
        copy = pltpu.make_async_copy(src, dst, bias_sem.at[k])
        copy.start()
        bias_copies.append(copy)

    cw_copies = {}
    for dt in (2, 0, 1):
        for dh in range(3):
            copy = pltpu.make_async_copy(
                cw_hbm.at[dt, dh],
                cw.at[dt, :, :, pl.ds(dh * chans, chans)],
                cw_sem.at[dt, dh],
            )
            copy.start()
            cw_copies[dt, dh] = copy
    tw_copy = pltpu.make_async_copy(tw_hbm, tw, tw_sem)
    tw_copy.start()
    uw_copy = pltpu.make_async_copy(uw_hbm, uw, uw_sem)
    uw_copy.start()

    def history_copies(own, hist, send, recv, fsend):
        def nearer(r):
            return pltpu.make_async_remote_copy(
                own.at[r], hist.at[1, r], send.at[0, r], recv.at[1, r],
                device_id={"tm": sibling}, device_id_type=MESH,
            )

        def farther(r):
            return pltpu.make_async_remote_copy(
                own.at[r], hist.at[0, r], send.at[1, r], recv.at[0, r],
                device_id={"tm": t + 2}, device_id_type=MESH,
            )

        def forward(r):
            return pltpu.make_async_remote_copy(
                hist.at[0, r], hist.at[1, r], fsend.at[r], recv.at[1, r],
                device_id={"tm": sibling}, device_id_type=MESH,
            )

        return nearer, farther, forward

    def history_start(copies, r, sends=has_next):
        nearer, farther, _ = copies

        @pl.when(sends)
        def _():
            farther(r).start()

        @pl.when(even)
        def _():
            nearer(r).start()

    def history_far(copies, r):
        _, farther, forward = copies
        farther(r).wait_recv()

        @pl.when(odd)
        def _():
            forward(r).start()

    def history_near(copies, r):
        copies[0](r).wait_recv()

    def history_end(copies, r, sends=has_next):
        nearer, farther, forward = copies

        @pl.when(sends)
        def _():
            farther(r).wait_send()

        @pl.when(even)
        def _():
            nearer(r).wait_send()

        @pl.when(jnp.logical_and(odd, has_prev))
        def _():
            forward(r).wait_send()

    def to_tile(src, dst, sems, where):
        return pltpu.make_async_remote_copy(
            src, dst, sems.at[0], sems.at[1], device_id={"tile": where}, device_id_type=MESH
        )

    first, last = 0, rows - 1
    act_copies = history_copies(act, act_hist, a_send, a_recv, a_fsend)
    blk_copies = history_copies(blk, blk_hist, b_send, b_recv, b_fsend)
    part_down = to_tile(parts.at[1], part_in.at[0], p_down_sem, s + 1)
    part_up = to_tile(parts.at[0], part_in.at[1], p_up_sem, s - 1)
    blk_down = to_tile(blk.at[rows], blk.at[0], b_down_sem, s + 1)
    blk_up = to_tile(blk.at[1], blk.at[rows + 1], b_up_sem, s - 1)
    dbl_up = to_tile(dbl.at[1], dbl.at[rows + 1], d_up_sem, s - 1)

    def activate(r):
        values = lat[r].astype(F32)
        meansq = jnp.mean(values * values, axis=-1, keepdims=True)
        scaled = values * lax.rsqrt(meansq + 1e-06) * gain_ref[...].reshape(1, chans)
        act[r] = (scaled * jax.nn.sigmoid(scaled)).astype(BF16)

    peers = 1
    for condition in (has_next, has_prev, relays, relayed, has_up, has_down):
        peers = peers + condition.astype(jnp.int32)

    def to_partner(r):
        return pltpu.make_async_remote_copy(
            act.at[r], act_relay.at[r], r_send.at[0, r], r_recv.at[r],
            device_id={"tile": partner}, device_id_type=MESH,
        )

    def from_partner(r):
        return pltpu.make_async_remote_copy(
            act_relay.at[r], act_hist.at[0, r], r_send.at[1, r], a_recv.at[0, r],
            device_id={"tm": t + 2, "tile": partner}, device_id_type=MESH,
        )

    order = tuple(range(rows))[::-1]
    lat_copy.wait()
    for copy in bias_copies:
        copy.wait()
    for r in order:
        activate(r)
        if r == order[0]:
            pl.semaphore_wait(barrier, peers)
        if r == order[0]:
            history_start(act_copies, r)
        else:
            @pl.when(relays)
            def _():
                to_partner(r).start()

            history_start(act_copies, r, direct)

    def widen(frame):
        flat = frame.reshape(-1, chans)
        wide = flat.astype(F32)
        before = column_shift(wide, cols, 1).astype(BF16)
        after = column_shift(wide, cols, -1).astype(BF16)
        return jnp.concatenate([before, flat, after], axis=1)

    def conv(stacked, dt, start, size):
        taps = cw.at[dt, :, :, pl.ds(start, size)][...].reshape(3 * chans, size)
        return jnp.dot(stacked, taps, preferred_element_type=F32)

    def weights_ready(dt):
        for dh in range(3):
            cw_copies[dt, dh].wait()

    weights_ready(2)
    acc[...] = conv(widen(act[...]), 2, 0, 3 * chans)
    @pl.when(relays)
    def _():
        for r in order[1:]:
            to_partner(r).wait_recv()
            from_partner(r).start()

    def sum_taps():
        uw_copy.wait()
        row_sets = {(0, 0): (0,), (0, 1): (1, 2), (1, 0): (0, 1), (1, 1): (2,)}
        for (a, i), picks in row_sets.items():
            taps = []
            for kw in range(3):
                tap = uw[picks[0], kw].astype(F32)
                for kh in picks[1:]:
                    tap = tap + uw[kh, kw].astype(F32)
                taps.append(tap)
            center = (taps[1] + taps[2], taps[0] + taps[1])
            sides = (taps[0], taps[2])
            lanes = pl.ds(i * chans, chans)
            for base, pair in ((0, center), (2 * outs_n, sides)):
                for b in range(2):
                    value = pair[b].astype(BF16)
                    umat[a, pl.ds(base + b * low, low), lanes] = value[:low]
                    umat[a, pl.ds(base + 2 * low + b * high, high), lanes] = value[low:]

    @pl.when(later)
    def _():
        sum_taps()
        weights_ready(0)
        weights_ready(1)

    for r in order:
        span = pl.ds(r * cols, cols)
        goes, stays = (0, chans) if r == last else (2 * chans, 0)
        out_part = 1 if r == last else 0

        @pl.when(has_prev)
        def _():
            history_far(act_copies, r)
            acc[span, :] += conv(widen(act_hist[0, r]), 0, 0, 3 * chans)

        @pl.when(has_near)
        def _():
            if r == order[0]:
                @pl.when(starts)
                def _():
                    weights_ready(1)

            history_near(act_copies, r)
            acc[span, pl.ds(goes, chans)] += conv(widen(act_hist[1, r]), 1, goes, chans)

        parts[out_part] = acc[span, pl.ds(goes, chans)].astype(BF16)
        if r == last:
            @pl.when(has_down)
            def _():
                part_down.start()
        else:
            @pl.when(has_up)
            def _():
                part_up.start()

        @pl.when(has_near)
        def _():
            acc[span, pl.ds(stays, 2 * chans)] += conv(widen(act_hist[1, r]), 1, stays, 2 * chans)

    def finish_row(r):
        total = acc[pl.ds(r * cols, cols), pl.ds(chans, chans)]
        if r > 0:
            total = total + acc[pl.ds((r - 1) * cols, cols), pl.ds(0, chans)]
        if r < rows - 1:
            total = total + acc[pl.ds((r + 1) * cols, cols), pl.ds(2 * chans, chans)]
        total = total + cb_ref[...].reshape(1, chans) + lat[r].astype(F32)
        if r == first:
            total = total + part_in[0].astype(F32)
        if r == last:
            total = total + part_in[1].astype(F32)
        blk[1 + r] = total.astype(BF16)

    tw_copy.wait()

    def mix(row, k):
        return jnp.dot(row, tw[k], preferred_element_type=F32)

    def newest(j):
        mixed[j] = mix(blk[j], 2) + tb_ref[...].reshape(1, 2 * chans)

    def mix_far(j):
        @pl.when(has_prev)
        def _():
            history_far(blk_copies, j)
            mixed[j] += mix(blk_hist[0, j], 0)

    def mix_near(j):
        @pl.when(has_near)
        def _():
            history_near(blk_copies, j)
            mixed[j] += mix(blk_hist[1, j], 1)

        for f in range(2):
            dbl[j, f] = mixed[j, :, pl.ds(f * chans, chans)].astype(BF16)

    def taps_dot(row, a, start, size):
        return lax.dot_general(
            row, umat[a, :, pl.ds(start, size)], (((1,), (1,)), ((), ())), preferred_element_type=F32
        )

    def stored_row(j):
        return dbl[j].reshape(2 * cols, chans)

    @pl.when(has_up)
    def _():
        part_down.wait_recv()

    @pl.when(jnp.logical_not(has_up))
    def _():
        part_in[0] = jnp.zeros((cols, chans), BF16)

    for r in range(rows - 1):
        finish_row(r)

        if r == first:
            @pl.when(has_up & starts)
            def _():
                blk_up.start()

        history_start(blk_copies, 1 + r)
        newest(1 + r)

    @pl.when(has_down)
    def _():
        part_up.wait_recv()

    @pl.when(jnp.logical_not(has_down))
    def _():
        part_in[1] = jnp.zeros((cols, chans), BF16)

    finish_row(last)

    @pl.when(has_down)
    def _():
        blk_down.start()

    history_start(blk_copies, rows)

    @pl.when(starts)
    def _():
        sum_taps()
        weights_ready(0)

        @pl.when(t == 0)
        def _():
            weights_ready(1)

    newest(rows)

    for r in range(rows):
        if r == last:
            @pl.when(has_up)
            def _():
                blk_down.wait_recv()
                history_start(blk_copies, 0)

        mix_far(1 + r)
        mix_near(1 + r)
        if r == first:
            @pl.when(has_up & later)
            def _():
                dbl_up.start()

            @pl.when(has_down & (t == 0))
            def _():
                blk_up.wait_recv()
                blk_copies[0](rows + 1).start()

            edge[0] = taps_dot(stored_row(1), 0, chans, chans)

    bias_row = ub_ref[...].reshape(1, outs_n)
    up_bias = jnp.concatenate(
        [bias_row[:, :low], bias_row[:, :low], bias_row[:, low:], bias_row[:, low:]], axis=1
    )

    def upsample_row(a, r, result):
        center = result[:, : 2 * outs_n] + up_bias
        sides = result[:, 2 * outs_n :]
        even = center[:, :low] + column_shift(sides[:, :low], cols, 1)
        uneven = center[:, low : 2 * low] + column_shift(sides[:, low : 2 * low], cols, -1)
        tail = sides[:, 2 * low :]
        lane = lax.broadcasted_iota(jnp.int32, tail.shape, 1)
        tail = center[:, 2 * low :] + jnp.where(
            lane < high, column_shift(tail, cols, 1), column_shift(tail, cols, -1)
        )
        swapped = pltpu.roll(tail, high, 1)
        for f in range(2):
            span = slice(f * cols, (f + 1) * cols)
            wide_lo[pl.ds(0, cols, stride=2), :] = even[span]
            wide_lo[pl.ds(1, cols, stride=2), :] = uneven[span]
            wide_hi[pl.ds(0, cols, stride=2), :] = tail[span]
            wide_hi[pl.ds(1, cols, stride=2), :] = swapped[span]
            out_ref[f, 2 * r + a, pl.ds(0, low), :] = wide_lo[...].T.astype(BF16)
            out_ref[f, 2 * r + a, pl.ds(low, high), :] = wide_hi[...].T[:high].astype(BF16)

    for r in range(rows):
        for a in range(2):
            if 0 < r + a < rows:
                both = jnp.concatenate([stored_row(r + a), stored_row(r + a + 1)], axis=1)
                upsample_row(a, r, taps_dot(both, a, 0, 2 * chans))

    @pl.when(has_up)
    def _():
        newest(0)
        mix_far(0)

    edge[1] = taps_dot(stored_row(rows), 1, 0, chans)

    @pl.when(has_down & starts)
    def _():
        @pl.when(t == 1)
        def _():
            blk_up.wait_recv()

        newest(rows + 1)

        @pl.when(t == 1)
        def _():
            history_near(blk_copies, rows + 1)
            mixed[rows + 1] += mix(blk_hist[1, rows + 1], 1)

        for f in range(2):
            dbl[rows + 1, f] = mixed[rows + 1, :, pl.ds(f * chans, chans)].astype(BF16)

    @pl.when(has_down & later)
    def _():
        dbl_up.wait_recv()

    @pl.when(has_down)
    def _():
        edge[1] += taps_dot(stored_row(rows + 1), 1, chans, chans)

    upsample_row(1, last, edge[1])

    @pl.when(has_up)
    def _():
        mix_near(0)
        edge[0] += taps_dot(stored_row(0), 0, 0, chans)

    upsample_row(0, 0, edge[0])

    for r in range(rows):
        history_end(act_copies, r, has_next if r == order[0] else direct)
        history_end(blk_copies, 1 + r)

    @pl.when(relays)
    def _():
        for r in order[1:]:
            to_partner(r).wait_send()
            from_partner(r).wait_send()

    @pl.when(has_up)
    def _():
        history_end(blk_copies, 0)
        part_up.wait_send()

        @pl.when(later)
        def _():
            dbl_up.wait_send()

        @pl.when(starts)
        def _():
            blk_up.wait_send()

    @pl.when(has_down)
    def _():
        part_down.wait_send()
        blk_down.wait_send()

        @pl.when(t == 0)
        def _():
            blk_copies[0](rows + 1).wait_send()


def local(frames, tiles, latent, gain, conv_weight, conv_bias, time_weight, time_bias, up_weight, up_bias):
    _, rows, cols, chans = latent.shape
    outs_n = up_weight.shape[3]
    low = 128
    dma = pltpu.SemaphoreType.DMA
    row = (cols, chans)
    transposed = pl.pallas_call(
        functools.partial(kernel, frames, tiles),
        out_shape=jax.ShapeDtypeStruct((2, 2 * rows, outs_n, 2 * cols), BF16),
        in_specs=[pl.BlockSpec(memory_space=pltpu.HBM)] * 8,
        out_specs=pl.BlockSpec(memory_space=pltpu.VMEM),
        scratch_shapes=[
            pltpu.VMEM((rows,) + row, BF16),
            pltpu.VMEM((rows,) + row, BF16),
            pltpu.VMEM((2, rows) + row, BF16),
            pltpu.VMEM((rows,) + row, BF16),
            pltpu.VMEM((2,) + row, BF16),
            pltpu.VMEM((2,) + row, BF16),
            pltpu.VMEM((rows + 2,) + row, BF16),
            pltpu.VMEM((2, rows + 2) + row, BF16),
            pltpu.VMEM((rows + 2, 2) + row, BF16),
            pltpu.VMEM((chans,), F32),
            pltpu.VMEM((chans,), F32),
            pltpu.VMEM((2 * chans,), F32),
            pltpu.VMEM((outs_n,), F32),
            pltpu.VMEM((3, 3, chans, 3 * chans), BF16),
            pltpu.VMEM((3, chans, 2 * chans), BF16),
            pltpu.VMEM((3, 3, outs_n, chans), BF16),
            pltpu.VMEM((2, 4 * outs_n, 2 * chans), BF16),
            pltpu.VMEM((rows * cols, 3 * chans), F32),
            pltpu.VMEM((rows + 2, cols, 2 * chans), F32),
            pltpu.VMEM((2, 2 * cols, 4 * outs_n), F32),
            pltpu.VMEM((2 * cols, low), F32),
            pltpu.VMEM((2 * cols, low), F32),
            dma(()), dma((4,)), dma((3, 3)), dma(()), dma(()),
            dma((2, rows)), dma((2, rows)), dma((rows,)),
            dma((2, rows)), dma((rows,)),
            dma((2, rows + 2)), dma((2, rows + 2)), dma((rows + 2,)),
            dma((2,)), dma((2,)), dma((2,)), dma((2,)), dma((2,)),
        ],
        compiler_params=pltpu.CompilerParams(
            collective_id=0, has_side_effects=True, vmem_limit_bytes=48 * 1024 * 1024
        ),
    )(*(
        pltpu.with_memory_space_constraint(array, pltpu.HBM)
        for array in (
            latent, gain, conv_bias, time_bias, up_bias,
            conv_weight, time_weight, jnp.swapaxes(up_weight, 2, 3),
        )
    ))
    return jnp.swapaxes(transposed, 2, 3)


def solution(mesh):
    placed = (P("tm", "tile", None, None), P(), P(), P(), P(), P(), P(), P())
    return jax.shard_map(
        functools.partial(local, mesh.shape["tm"], mesh.shape["tile"]),
        mesh=mesh, in_specs=placed, out_specs=P("tm", "tile", None, None), check_vma=False,
    )
```
